32 devices in a mesh: rep: 2 (over y), fsdp: 16 (over z, x, core).
Axes of the slice: x: 2, y: 2, z: 4, core: 2. Of those that a mesh axis runs over, the one named last changes fastest.
Arguments:
- tokens: bfloat16 [32, 128, 1536], P(('rep', 'fsdp')), may hold values from -6 to 6
- cotangent: bfloat16 [32, 128, 1536], P(('rep', 'fsdp')), may hold values from -6 to 6
- pic_start: int32 [32], P(('rep', 'fsdp')), may hold values from 0 to 96
- valid_mask: int32 [32, 128], P(('rep', 'fsdp')), may hold values from 0 to 1, as said below
- gain_attn: bfloat16 [1536], P('fsdp'), may hold values from 0.5 to 1.5
- attn_in: bfloat16 [1536, 6144], P('fsdp'), may hold values from -0.15625 to 0.15625
- forget_w: bfloat16 [1536, 24], P('fsdp'), may hold values from -0.15625 to 0.15625
- forget_bias: bfloat16 [24], replicated, may hold values from 0 to 7
- attn_out: bfloat16 [1536, 1536], P('fsdp'), may hold values from -0.625 to 0.625
- gain_ffn: bfloat16 [1536], P('fsdp'), may hold values from 0.5 to 1.5
- ffn_in: bfloat16 [2, 1536, 4096], P(None, None, 'fsdp'), may hold values from -0.15625 to 0.15625
- ffn_down: bfloat16 [4096, 1536], P('fsdp'), may hold values from -0.09375 to 0.09375
Outputs:
- activations: bfloat16 [32, 128, 1536], P(('rep', 'fsdp'))
- input_grad: float32 [32, 128, 1536], P(('rep', 'fsdp'))
- grad_gain_attn: float32 [1536], P('fsdp')
- grad_attn_in: float32 [1536, 6144], P('fsdp')
- grad_forget_w: float32 [1536, 24], P('fsdp')
- grad_forget_bias: float32 [24], replicated
- grad_attn_out: float32 [1536, 1536], P('fsdp')
- grad_gain_ffn: float32 [1536], P('fsdp')
- grad_ffn_in: float32 [2, 1536, 4096], P(None, None, 'fsdp')
- grad_ffn_down: float32 [4096, 1536], P('fsdp')
- stats: float32 [3], replicated
The draws below stay inside these ranges and needn't reach their ends.
Inputs may be any that keep to these rules, and one draw needn't show every extreme that they name: `valid_mask`: sequence b's valid tokens are a prefix of length 42 + 86 * b // 31 plus a jitter under 128 // 8, at most 128; the last sequence is full.
All inputs are finite; a program needn't handle non-finite values.
Results may differ from the reference program's by a relative error of at most 0.024.
Values may be sent and summed in bfloat16 or wider, within the bound.
A program may use at most 320 MiB of HBM per device.

```python
import jax
import jax.numpy as jnp
from jax import lax

D = 1536
H = 24
HD = 64
FF = 4096
SEQ = 128
SEQS = 32
PIC = 32


def draw_valid_mask(key, part):
    index = jnp.arange(SEQS, dtype=jnp.int32)
    ramped = SEQ // 3 + (SEQ - SEQ // 3) * index // max(SEQS - 1, 1)
    jitter = jax.random.randint(key, (SEQS,), 0, max(SEQ // 8, 1), dtype=jnp.int32)
    length = jnp.minimum(ramped + jitter, SEQ)
    positions = jnp.arange(SEQ, dtype=jnp.int32)
    return (positions[None, :] < length[:, None]).astype(jnp.int32)


def set_ends(array, stream_key, low, high):
    longest = array.shape.index(max(array.shape))
    spots = []
    for shift in (0, 1):
        where = [jax.random.randint(jax.random.fold_in(stream_key, axis), (), 0, length) for axis, length in enumerate(array.shape)]
        where[longest] = (where[longest] + shift) % array.shape[longest]
        spots.append(tuple(where))
    return array.at[spots[0]].set(low).at[spots[1]].set(high)


def block_levels(rng, extent, pieces, least, largest):
    def one(dim, parts):
        heights = jax.random.uniform(jax.random.fold_in(jax.random.fold_in(rng, 6), dim), (parts,), jnp.float32, least / len(pieces), largest / len(pieces))
        return jnp.repeat(jnp.exp(heights), extent[dim] // parts).reshape((-1,) + (1,) * (len(extent) - dim - 1))

    gain = one(*pieces[0])
    for cut in pieces[1:]:
        gain = gain * one(*cut)
    return gain


def centred(rng, dims, deviation, bound, shards=(), kind=jnp.bfloat16):
    values = deviation * jax.random.normal(rng, dims, jnp.float32)
    if shards:
        values = values * block_levels(rng, dims, shards, -0.22, 0.18)
    return jnp.clip(values, -bound, bound).astype(kind)


def setup_inputs(seed: int = 0) -> dict:
    key_list = jax.random.split(jax.random.key(seed), 13)
    return {
        "tokens": centred(key_list[0], (SEQS, SEQ, D), 1.0, 6.0, ((0, 32),)),
        "cotangent": centred(key_list[1], (SEQS, SEQ, D), 1.0, 6.0, ((0, 32),)),
        "pic_start": set_ends(jax.random.randint(key_list[2], (SEQS,), 0, SEQ - PIC + 1), jax.random.fold_in(key_list[2], 1), 0, SEQ - PIC).astype(jnp.int32),
        "valid_mask": draw_valid_mask(jax.random.fold_in(key_list[12], 71), 0),
        "gain_attn": jnp.clip(1.0 + 0.1 * jax.random.normal(key_list[4], (D,), jnp.float32), 0.5, 1.5).astype(jnp.bfloat16),
        "attn_in": centred(key_list[5], (D, 4 * D), D ** -0.5, 0.15625, ((0, 16),)),
        "forget_w": centred(key_list[6], (D, H), D ** -0.5, 0.15625, ((0, 16),)),
        "forget_bias": jnp.clip(jax.random.uniform(key_list[7], (H,), jnp.float32, 0.0, 7.0), 0.0, 7.0).astype(jnp.bfloat16),
        "attn_out": centred(key_list[8], (D, D), (D // 16) ** -0.5, 0.625, ((0, 16),)),
        "gain_ffn": jnp.clip(1.0 + 0.1 * jax.random.normal(key_list[9], (D,), jnp.float32), 0.5, 1.5).astype(jnp.bfloat16),
        "ffn_in": centred(key_list[10], (2, D, FF), D ** -0.5, 0.15625, ((2, 16),)),
        "ffn_down": centred(key_list[11], (FF, D), FF ** -0.5, 0.09375, ((0, 16),)),
    }


EPSILON = 1e-06
NEGATIVE = -1e+30
PRECISE = lax.Precision.HIGHEST

@jax.custom_vjp
def low(v):
    return lax.optimization_barrier(v.astype(jnp.bfloat16)).astype(jnp.float32)

@jax.custom_vjp
def low_back(v):
    return v

def low_keep(v):
    return (low(v), None)

def low_pass(kept, grad):
    return (grad,)

def back_keep(v):
    return (v, None)

def back_low(kept, grad):
    return (low(grad),)
low.defvjp(low_keep, low_pass)
low_back.defvjp(back_keep, back_low)

def norm_apply(values_in, gain_row):
    inverse = lax.rsqrt(lax.optimization_barrier(jnp.mean(values_in * values_in, axis=-1, keepdims=True)) + EPSILON)
    return values_in * inverse * gain_row

def layer(layer_in, params, starts_now, mask_now):
    gain_attn, attn_in, forget_w, forget_bias, attn_out, gain_ffn, ffn_in, ffn_down = params
    groups = layer_in.shape[0]
    rows_a = low(norm_apply(layer_in, gain_attn))
    projected = low_back(jnp.einsum('gsd,de->gse', rows_a, attn_in, precision=PRECISE))
    queries = low(projected[..., :D]).reshape(groups, SEQ, H, HD)
    keys_all = low(projected[..., D:2 * D]).reshape(groups, SEQ, H, HD)
    values_all = low(projected[..., 2 * D:3 * D]).reshape(groups, SEQ, H, HD)
    out_gate = jax.nn.sigmoid(projected[..., 3 * D:])
    forget_logit = low_back(jnp.einsum('gsd,dh->gsh', rows_a, forget_w, precision=PRECISE)) + forget_bias
    decay_sum = jnp.cumsum(jax.nn.log_sigmoid(forget_logit), axis=1)
    positions = jnp.arange(SEQ, dtype=jnp.int32)
    causal = positions[None, :] <= positions[:, None]
    inside = (positions[None, :] >= starts_now[:, None]) & (positions[None, :] < starts_now[:, None] + PIC)
    allowed = (causal[None] | inside[:, :, None] & inside[:, None, :]) & (mask_now[:, None, :] > 0)
    allowed = allowed[:, None]
    decay_heads = jnp.transpose(decay_sum, (0, 2, 1))
    spread = decay_heads[:, :, :, None] - decay_heads[:, :, None, :]
    decay_bias = jnp.where(causal[None, None], spread, -spread)
    dotted = low_back(jnp.einsum('gihe,gjhe->ghij', queries, keys_all, precision=PRECISE))
    scores = dotted * HD ** (-0.5) + decay_bias
    masked = jnp.where(allowed, scores, NEGATIVE)
    row_max = lax.optimization_barrier(jnp.max(masked, axis=-1, keepdims=True))
    weights = jnp.where(allowed, jnp.exp(masked - row_max), 0.0)
    probability = weights / lax.optimization_barrier(jnp.sum(weights, axis=-1, keepdims=True))
    attended = low_back(jnp.einsum('ghij,gjhe->gihe', low(probability), values_all, precision=PRECISE))
    attended = attended.reshape(groups, SEQ, D)
    gated_rows = low(attended * out_gate)
    branch_attn = low_back(jnp.einsum('gsi,io->gso', gated_rows, attn_out, precision=PRECISE))
    middle = layer_in + branch_attn
    rows_f = low(norm_apply(middle, gain_ffn))
    gate_up = low_back(jnp.einsum('gsd,kdf->kgsf', rows_f, ffn_in, precision=PRECISE))
    hidden = low(jax.nn.silu(gate_up[0]) * gate_up[1])
    branch_ffn = low_back(jnp.einsum('gsf,fd->gsd', hidden, ffn_down, precision=PRECISE))
    result = middle + branch_ffn
    valid_rows = mask_now.astype(jnp.float32)[:, :, None]
    square_sums = jnp.stack([jnp.sum(result * result * valid_rows), jnp.sum(branch_attn * branch_attn * valid_rows), jnp.sum(branch_ffn * branch_ffn * valid_rows)])
    return (result, square_sums)

def reference(tokens, cotangent, pic_start, valid_mask, gain_attn, attn_in, forget_w, forget_bias, attn_out, gain_ffn, ffn_in, ffn_down):
    params = tuple((weight.astype(jnp.float32) for weight in (gain_attn, attn_in, forget_w, forget_bias, attn_out, gain_ffn, ffn_in, ffn_down)))
    group_size = min(SEQS, max(1, 4096 // SEQ))
    step_count = SEQS // group_size

    def by_group(values_in):
        return values_in.reshape((step_count, group_size) + values_in.shape[1:])

    def one_group(totals, batch_rows):
        layer_in, cot_rows, starts_now, mask_now = batch_rows

        def forward(rows_in, params_in):
            return layer(rows_in, params_in, starts_now, mask_now)
        result, pull_back, square_sums = jax.vjp(forward, layer_in, params, has_aux=True)
        layer_grad, param_grads = pull_back(cot_rows)
        grad_totals, sum_totals = totals
        grad_totals = jax.tree.map(jnp.add, grad_totals, param_grads)
        return ((grad_totals, sum_totals + square_sums), (result.astype(jnp.bfloat16), layer_grad))
    initial = (jax.tree.map(jnp.zeros_like, params), jnp.zeros((3,), jnp.float32))
    batches = (by_group(tokens.astype(jnp.float32)), by_group(cotangent.astype(jnp.float32)), by_group(pic_start), by_group(valid_mask))
    (grad_totals, square_sums), (activations, input_grad) = lax.scan(one_group, initial, batches)
    count = jnp.sum(valid_mask.astype(jnp.float32))
    stats = jnp.sqrt(square_sums / (count * D) + EPSILON)
    return (activations.reshape(SEQS, SEQ, D), input_grad.reshape(SEQS, SEQ, D), grad_totals[0], grad_totals[1], grad_totals[2], grad_totals[3], grad_totals[4], grad_totals[5], grad_totals[6], grad_totals[7], stats)
```

```python
import functools

import jax
import jax.numpy as jnp
from jax import lax
from jax.experimental import pallas as pl
from jax.experimental.pallas import tpu as pltpu
from jax.sharding import PartitionSpec as P

H = 24
HD = 64
PIC = 32
TP = 8
DEPTH = 4
EPSILON = 1e-06
NEGATIVE = -1e30
MESH = pl.DeviceIdType.MESH
BF16 = jnp.bfloat16
F32 = jnp.float32
VMEM = pl.BlockSpec(memory_space=pltpu.VMEM)
ANY = pl.BlockSpec(memory_space=pl.ANY)


class Net:
    def __init__(self, reps, share, sems):
        self.reps, self.share, self.sems = reps, share, sems
        self.r = lax.axis_index("rep")
        self.f = lax.axis_index("fsdp")
        self.t = lax.div(self.f, share)
        self.u = lax.rem(self.f, share)
        self.z = lax.div(self.t, 2)
        self.x = lax.rem(self.t, 2)
        self.taken = 0
        self.sent = []

    def take(self, count=1):
        base = self.taken
        self.taken += count
        return base

    def place(self, t):
        return t * self.share + self.u

    def grid(self, z, x):
        return (z * 2 + x) * self.share + self.u

    def partners(self):
        for k in range(1, self.share):
            yield k, lax.rem(self.u + k, self.share)

    def greet(self, peers):
        barrier = pltpu.get_barrier_semaphore()
        total = 0
        for cond, r, f in peers:
            if cond is None:
                pl.semaphore_signal(barrier, 1, device_id=(r, f), device_id_type=MESH)
                total = total + 1
            else:

                @pl.when(cond)
                def _():
                    pl.semaphore_signal(barrier, 1, device_id=(r, f), device_id_type=MESH)

                total = total + cond.astype(jnp.int32)
        pl.semaphore_wait(barrier, total)

    def plane_peers(self):
        return [
            (self.z < DEPTH - 1, self.r, self.grid(self.z + 1, self.x)),
            (self.z > 0, self.r, self.grid(self.z - 1, self.x)),
            (None, self.r, self.grid(self.z, 1 - self.x)),
        ]

    def share_peers(self):
        return [(None, self.r, self.t * self.share + u) for _, u in self.partners()]

    def rep_peers(self):
        return [(None, lax.rem(self.r + k, self.reps), self.f) for k in range(1, self.reps)]

    def all_plane_peers(self):
        return [(None, self.r, self.place(lax.rem(self.t + k, TP))) for k in range(1, TP)]

    def send(self, src, dst, ssem, rsem, f, r=None, cond=None):
        copy = pltpu.make_async_remote_copy(
            src_ref=src,
            dst_ref=dst,
            send_sem=self.sems.at[ssem],
            recv_sem=self.sems.at[rsem],
            device_id=(self.r if r is None else r, f),
            device_id_type=MESH,
        )
        if cond is None:
            copy.start()
        else:
            pl.when(cond)(copy.start)
        self.sent.append((cond, copy))

    def arrive(self, dst, rsem, cond=None):
        copy = pltpu.make_async_remote_copy(
            src_ref=dst,
            dst_ref=dst,
            send_sem=self.sems.at[rsem],
            recv_sem=self.sems.at[rsem],
            device_id=(self.r, self.f),
            device_id_type=MESH,
        )
        if cond is None:
            copy.wait_recv()
        else:
            pl.when(cond)(copy.wait_recv)

    def drain(self):
        for cond, copy in self.sent:
            if cond is None:
                copy.wait_send()
            else:
                pl.when(cond)(copy.wait_send)
        self.sent = []


class Flood:
    def __init__(self, net, src, dst):
        self.net, self.src, self.dst = net, src, dst
        self.recv = net.take(TP)
        self.up, self.down = net.take(DEPTH), net.take(DEPTH)
        self.side = net.take(2 * DEPTH)

    def step(self, d):
        net = self.net
        z, x = net.z, net.x
        for k, way in enumerate((0,) if d == 0 else (-1, 1)):
            zo = jnp.clip(z + way * d, 0, DEPTH - 1)
            have = None if d == 0 else ((z - d >= 0) if way < 0 else (z + d <= DEPTH - 1))
            origin = zo * 2 + x
            dst = self.dst(origin)
            src = self.src if d == 0 else dst
            if d:
                net.arrive(dst, self.recv + origin, have)

            def also(cond):
                return cond if have is None else have & cond

            if way <= 0:
                net.send(
                    src, dst, self.up + d, self.recv + origin,
                    net.grid(jnp.minimum(z + 1, DEPTH - 1), x), cond=also(z < DEPTH - 1),
                )
            if way >= 0:
                net.send(
                    src, dst, self.down + d, self.recv + origin,
                    net.grid(jnp.maximum(z - 1, 0), x), cond=also(z > 0),
                )
            net.send(src, dst, self.side + 2 * d + k, self.recv + origin, net.grid(z, 1 - x), cond=have)

    def finish(self):
        for zo in range(DEPTH):
            origin = zo * 2 + 1 - self.net.x
            self.net.arrive(self.dst(origin), self.recv + origin)


def flood_all(floods):
    for d in range(DEPTH):
        for flood in floods:
            flood.step(d)
    for flood in floods:
        flood.finish()


class Collect:
    def __init__(self, net, part, side, up, down, stage, out):
        self.net, self.part, self.side, self.up, self.down = net, part, side, up, down
        self.stage, self.out = stage, out
        self.side_send, self.side_recv = net.take(DEPTH), net.take(DEPTH)
        self.up_send, self.up_recv = net.take(DEPTH), net.take(DEPTH)
        self.down_send, self.down_recv = net.take(DEPTH), net.take(DEPTH)

    def targets(self, d):
        z = self.net.z
        if d == 0:
            return [(0, z, None)]
        return [
            (1, jnp.minimum(z + d, DEPTH - 1), z + d <= DEPTH - 1),
            (-1, jnp.maximum(z - d, 0), z - d >= 0),
        ]

    def begin(self, d):
        net = self.net
        for way, zo, have in self.targets(d):
            net.send(
                self.part(zo * 2 + 1 - net.x), self.side(zo), self.side_send + zo, self.side_recv + zo,
                net.grid(net.z, 1 - net.x), cond=have,
            )

    def step(self, d):
        net = self.net
        z = net.z
        for way, zo, have in self.targets(d):

            def run(way=way, zo=zo):
                net.arrive(self.side(zo), self.side_recv + zo)
                if way == 0:
                    net.arrive(self.up(zo), self.up_recv + zo, z > 0)
                    net.arrive(self.down(zo), self.down_recv + zo, z < DEPTH - 1)
                    base = self.part(zo * 2 + net.x)[...].astype(F32) + self.side(zo)[...].astype(F32)
                    self.out[...] = base

                    @pl.when(z > 0)
                    def _():
                        self.out[...] += self.up(zo)[...].astype(F32)

                    @pl.when(z < DEPTH - 1)
                    def _():
                        self.out[...] += self.down(zo)[...].astype(F32)

                    return
                behind, sem = (self.up, self.up_recv) if way > 0 else (self.down, self.down_recv)
                more = z > 0 if way > 0 else z < DEPTH - 1
                net.arrive(behind(zo), sem + zo, more)
                base = self.part(zo * 2 + net.x)[...].astype(F32) + self.side(zo)[...].astype(F32)

                @pl.when(more)
                def _():
                    self.stage(zo)[...] = (base + behind(zo)[...].astype(F32)).astype(BF16)

                @pl.when(jnp.logical_not(more))
                def _():
                    self.stage(zo)[...] = base.astype(BF16)

            if have is None:
                run()
            else:
                pl.when(have)(run)
            if way > 0:
                net.send(
                    self.stage(zo), self.up(zo), self.up_send + zo, self.up_recv + zo,
                    net.grid(jnp.minimum(z + 1, DEPTH - 1), net.x), cond=have,
                )
            if way < 0:
                net.send(
                    self.stage(zo), self.down(zo), self.down_send + zo, self.down_recv + zo,
                    net.grid(jnp.maximum(z - 1, 0), net.x), cond=have,
                )


def collect_all(collects):
    for d in range(DEPTH - 1, -1, -1):
        for collect in collects:
            collect.begin(d)
    for d in range(DEPTH - 1, -1, -1):
        for collect in collects:
            collect.step(d)


def call(body, name, number, operands, in_specs, outs, scratch, sems, limit=60 << 20):
    return pl.pallas_call(
        body,
        name=name,
        out_shape=tuple(shape for shape, _ in outs),
        in_specs=in_specs,
        out_specs=tuple(spec for _, spec in outs),
        scratch_shapes=list(scratch) + [pltpu.SemaphoreType.DMA((sems,))],
        compiler_params=pltpu.CompilerParams(
            collective_id=number, has_side_effects=True, vmem_limit_bytes=limit
        ),
    )(*operands)


def chunk(rows, count, c):
    return pl.ds(c * (rows // count), rows // count)


def opening(reps, share, x, split, small, w_out, ffn_in, ffn_down):
    n = TP * share
    rows, cols = x.shape
    depth, width = split.shape[1:]

    def body(x_ref, w_ref, small_ref, wo_ref, wi_ref, wd_ref, xs, wc, smalls, wos, wis, wds, local, sems):
        net = Net(reps, share, sems)
        net.greet(
            [(None, net.r, lax.rem(net.f + k, n)) for k in range(1, n)]
        )
        own = [
            pltpu.make_async_copy(x_ref, xs.at[net.t], local.at[0]),
            pltpu.make_async_copy(w_ref.at[net.t], wc.at[net.f], local.at[1]),
            pltpu.make_async_copy(small_ref, smalls.at[net.f], local.at[2]),
            pltpu.make_async_copy(wo_ref, wos.at[net.u], local.at[3]),
        ]
        floods = [
            Flood(net, x_ref.at[chunk(rows, 2, c)], lambda t, c=c: xs.at[t, chunk(rows, 2, c)]) for c in range(2)
        ]
        small_send, small_recv = net.take(n), net.take(n)
        w_send, w_recv = net.take(TP), net.take(n)
        w_pass = net.take(share * TP)
        other = net.take(6 * share)
        for k in range(1, n):
            net.send(small_ref, smalls.at[net.f], small_send + k, small_recv + net.f, lax.rem(net.f + k, n))
        for k in range(1, TP):
            t = lax.rem(net.t + k, TP)
            net.send(w_ref.at[t], wc.at[net.f], w_send + k, w_recv + net.f, net.place(t))
        for flood in floods:
            flood.step(0)
        for k, u in net.partners():
            f = net.t * share + u
            slot = share - 1 - k
            net.send(w_ref.at[net.t], wc.at[net.f], w_send, w_recv + net.f, f) if share == 2 else net.send(
                w_ref.at[net.t], wc.at[net.f], other + 5 * share + k, w_recv + net.f, f
            )
            net.send(wo_ref, wos.at[net.u], other + k, other + share + net.u, f)
            net.send(wi_ref, wis.at[slot], other + 2 * share + k, other + 3 * share + slot, f)
            net.send(wd_ref, wds.at[slot], other + 4 * share + k, w_pass + slot, f)
        for copy in own:
            copy.start()
        for d in range(1, DEPTH):
            for flood in floods:
                flood.step(d)
        for k in range(1, TP):
            t = lax.rem(net.t + k, TP)
            source = net.place(t)
            net.arrive(wc.at[source], w_recv + source)
            for j, u in net.partners():
                net.send(
                    wc.at[source], wc.at[source], w_pass + share * k + j, w_recv + source, net.t * share + u
                )
        for k, u in net.partners():
            slot = k - 1
            net.arrive(wos.at[u], other + share + u)
            net.arrive(wis.at[slot], other + 3 * share + slot)
            net.arrive(wds.at[slot], w_pass + slot)
            for t in range(TP):
                net.arrive(wc.at[t * share + u], w_recv + t * share + u)
        for k in range(1, n):
            f = lax.rem(net.f + k, n)
            net.arrive(smalls.at[f], small_recv + f)
        for flood in floods:
            flood.finish()
        net.drain()
        for copy in own:
            copy.wait()

    shape = jax.ShapeDtypeStruct
    return call(
        body, "opening", 1, (x, split, small, w_out, ffn_in, ffn_down), [VMEM, VMEM, VMEM, VMEM, ANY, ANY],
        [
            (shape((TP, rows, cols), BF16), VMEM),
            (shape((n, depth, width), BF16), VMEM),
            (shape((n,) + small.shape, BF16), VMEM),
            (shape((share,) + w_out.shape, BF16), VMEM),
            (shape((share - 1,) + ffn_in.shape, BF16), ANY),
            (shape((share - 1,) + ffn_down.shape, BF16), ANY),
        ],
        [pltpu.SemaphoreType.DMA((4,))], 400,
    )


def gather_plane(reps, share, name, number, blocks, pieces=2):
    count = len(blocks)
    rows = blocks[0].shape[0]

    def body(*refs):
        srcs, dsts, local, sems = refs[:count], refs[count : 2 * count], refs[-2], refs[-1]
        net = Net(reps, share, sems)
        net.greet(net.plane_peers())
        floods = [
            Flood(net, src.at[chunk(rows, pieces, c)], lambda t, c=c, dst=dst: dst.at[t, chunk(rows, pieces, c)])
            for src, dst in zip(srcs, dsts)
            for c in range(pieces)
        ]
        own = [pltpu.make_async_copy(srcs[i], dsts[i].at[net.t], local.at[i]) for i in range(count)]
        for flood in floods:
            flood.step(0)
        for copy in own:
            copy.start()
        for d in range(1, DEPTH):
            for flood in floods:
                flood.step(d)
        for flood in floods:
            flood.finish()
        net.drain()
        for copy in own:
            copy.wait()

    return call(
        body, name, number, blocks, [VMEM] * count,
        [(jax.ShapeDtypeStruct((TP,) + block.shape, block.dtype), VMEM) for block in blocks],
        [pltpu.SemaphoreType.DMA((count,))], 24 * count * pieces,
    )


def scatter_plane(reps, share, name, number, parts, pieces=2):
    count = len(parts)
    _, rows, cols = parts[0].shape

    def body(*refs):
        srcs, outs = refs[:count], refs[count : 2 * count]
        side, up, down, stage, sems = refs[2 * count :]
        net = Net(reps, share, sems)
        net.greet(net.plane_peers())
        collects = []
        for i in range(count):
            for c in range(pieces):
                rc = chunk(rows, pieces, c)
                collects.append(
                    Collect(
                        net,
                        lambda t, i=i, rc=rc: srcs[i].at[t, rc],
                        *[lambda z, i=i, rc=rc, ref=ref: ref.at[i, z, rc] for ref in (side, up, down, stage)],
                        outs[i].at[rc],
                    )
                )
        collect_all(collects)
        net.drain()

    buffer = pltpu.VMEM((count, DEPTH, rows, cols), BF16)
    return call(
        body, name, number, parts, [VMEM] * count,
        [(jax.ShapeDtypeStruct((rows, cols), F32), VMEM)] * count,
        [buffer] * 4, 24 * count * pieces,
    )


def share_sum(reps, share, name, number, own_parts, given_parts):
    count = len(own_parts)

    def body(*refs):
        own, given = refs[:count], refs[count : 2 * count]
        outs = refs[2 * count : 3 * count]
        got = refs[3 * count : 4 * count]
        sems = refs[-1]
        net = Net(reps, share, sems)
        net.greet(net.share_peers() + net.rep_peers())
        first, arrived = net.take(count * share), net.take(count * share)
        away, back = net.take(count * reps), net.take(count * reps)
        for i in range(count):
            for k, u in net.partners():
                slot = share - 1 - k
                net.send(
                    given[i].at[k - 1], got[i].at[slot], first + i * share + k, arrived + i * share + slot,
                    net.t * share + u,
                )
        for i in range(count):
            for slot in range(share - 1):
                net.arrive(got[i].at[slot], arrived + i * share + slot)
            rows = own[i].shape[0]
            step = 256 if rows % 256 == 0 else rows

            @pl.loop(0, rows // step)
            def _(j):
                at = pl.ds(pl.multiple_of(j * step, step), step)
                total = own[i][at].astype(F32)
                for slot in range(share - 1):
                    total = total + got[i][slot, at].astype(F32)
                outs[i][net.r, at] = total.astype(BF16)

            for k in range(1, reps):
                net.send(
                    outs[i].at[net.r], outs[i].at[net.r], away + i * reps + k, back + i * reps + net.r,
                    net.f, r=lax.rem(net.r + k, reps),
                )
        for i in range(count):
            for k in range(1, reps):
                r = lax.rem(net.r + k, reps)
                net.arrive(outs[i].at[r], back + i * reps + r)
        net.drain()

    return call(
        body, name, number, tuple(own_parts) + tuple(given_parts), [VMEM] * (2 * count),
        [(jax.ShapeDtypeStruct((reps,) + part.shape, BF16), VMEM) for part in own_parts],
        [pltpu.VMEM(part.shape, BF16) for part in given_parts], 2 * count * (share + reps),
    )


def exchange_in(reps, share, number, part):
    _, _, depth, width = part.shape

    def body(part_ref, out, got, stage, sems):
        net = Net(reps, share, sems)
        net.greet(net.share_peers() + net.rep_peers() + net.all_plane_peers())
        first, arrived = net.take(TP * share), net.take(TP * share)
        over, landed = net.take(TP), net.take(TP)
        away, back = net.take(TP * reps), net.take(TP * reps)
        for j in range(TP):
            t = lax.rem(net.t + 1 + j, TP)
            for k, u in net.partners():
                slot = share - 1 - k
                net.send(
                    part_ref.at[t, u], got.at[slot, t], first + share * j + k, arrived + share * t + slot,
                    net.t * share + u,
                )
        for j in range(TP):
            t = lax.rem(net.t + 1 + j, TP)
            total = part_ref[t, net.u].astype(F32)
            for slot in range(share - 1):
                net.arrive(got.at[slot, t], arrived + share * t + slot)
                total = total + got[slot, t].astype(F32)
            if j < TP - 1:
                stage[j] = total.astype(BF16)
                net.send(stage.at[j], out.at[net.r, net.t], over + j, landed + net.t, net.place(t))
            else:
                out[net.r, net.t] = total.astype(BF16)
        for j in range(TP):
            t = lax.rem(net.t - j + TP, TP)
            if j:
                net.arrive(out.at[net.r, t], landed + t)
            for k in range(1, reps):
                net.send(
                    out.at[net.r, t], out.at[net.r, t], away + reps * j + k, back + TP * net.r + t,
                    net.f, r=lax.rem(net.r + k, reps),
                )
        for k in range(1, reps):
            r = lax.rem(net.r + k, reps)
            for t in range(TP):
                net.arrive(out.at[r, t], back + TP * r + t)
        net.drain()

    return call(
        body, "exchange_in", number, (part,), [VMEM],
        [(jax.ShapeDtypeStruct((reps, TP, depth, width), BF16), VMEM)],
        [pltpu.VMEM((share - 1, TP, depth, width), BF16), pltpu.VMEM((TP - 1, depth, width), BF16)],
        2 * TP * (share + reps + 1),
    )[0]


def exchange_small(reps, share, number, part):
    n = TP * share

    def body(part_ref, out, local, sems):
        net = Net(reps, share, sems)
        net.greet([(None, net.r, lax.rem(net.f + k, n)) for k in range(1, n)] + net.rep_peers())
        own = pltpu.make_async_copy(part_ref.at[net.f], out.at[net.r, net.f], local.at[0])
        own.start()
        over, landed = net.take(n), net.take(n)
        away, back = net.take(reps), net.take(reps)
        for k in range(1, n):
            f = lax.rem(net.f + k, n)
            net.send(part_ref.at[f], out.at[net.r, net.f], over + k, landed + net.f, f)
        own.wait()
        for k in range(1, n):
            f = lax.rem(net.f + k, n)
            net.arrive(out.at[net.r, f], landed + f)
        for k in range(1, reps):
            net.send(
                out.at[net.r], out.at[net.r], away + k, back + net.r, net.f, r=lax.rem(net.r + k, reps)
            )
        for k in range(1, reps):
            r = lax.rem(net.r + k, reps)
            net.arrive(out.at[r], back + r)
        net.drain()

    return call(
        body, "exchange_small", number, (part,), [VMEM],
        [(jax.ShapeDtypeStruct((reps,) + part.shape, F32), VMEM)],
        [pltpu.SemaphoreType.DMA((1,))], 2 * (n + reps),
    )[0]


def dot(spec, a, b):
    return jnp.einsum(spec, a, b, preferred_element_type=F32)


def per_device(
    reps,
    share,
    tokens,
    cotangent,
    pic_start,
    valid_mask,
    gain_attn,
    attn_in,
    forget_w,
    forget_bias,
    attn_out,
    gain_ffn,
    ffn_in,
    ffn_down,
):
    n = TP * share
    _, seq, model = tokens.shape
    held = attn_in.shape[0]
    heads = H // TP
    width = heads * HD
    f = lax.axis_index("fsdp")
    t = f // share
    u = f % share
    layer_in = tokens[0].astype(F32)

    split = jnp.transpose(attn_in.reshape(held, 4, TP, width), (2, 0, 1, 3)).reshape(TP, held, 4 * width)
    small = jnp.concatenate([forget_w.T, gain_attn[None], gain_ffn[None]])
    small = jnp.pad(small, ((0, 0), (0, 128 - held)))
    marks = jnp.concatenate(
        [valid_mask.astype(BF16), jnp.broadcast_to(pic_start.astype(BF16)[:, None], (1, seq))]
    )
    small = jnp.concatenate([small, marks, jnp.zeros((32 - H - 4, 128), BF16)])
    xs, w_cols, smalls, w_rows, other_in, other_down = opening(
        reps, share, tokens[0], split, small, attn_out, ffn_in, ffn_down
    )
    w_cols = w_cols.reshape(model, 4 * width)
    w_rows = w_rows.reshape(width, model)
    gain_a = smalls[:, H, :held].reshape(model).astype(F32)
    gain_f = smalls[:, H + 1, :held].reshape(model).astype(F32)
    w_forget = lax.dynamic_slice_in_dim(smalls, heads * t, heads, axis=1)[:, :, :held]
    w_forget = jnp.transpose(w_forget, (1, 0, 2)).reshape(heads, model)
    bias = lax.dynamic_slice_in_dim(forget_bias, heads * t, heads).astype(F32)
    plane = smalls.reshape(TP, share, 32, 128)
    plane = lax.dynamic_index_in_dim(plane, u, axis=1, keepdims=False)
    key_valid = plane[:, H + 2] > 0
    starts = plane[:, H + 3, 0].astype(jnp.int32)

    xs = xs.astype(F32)
    inverse = lax.rsqrt(jnp.mean(xs * xs, axis=-1, keepdims=True) + EPSILON)
    rows_a = (xs * inverse * gain_a).astype(BF16).reshape(TP * seq, model)
    projected = dot("sd,de->se", rows_a, w_cols)

    def by_head(k):
        return projected[:, k * width : (k + 1) * width].astype(BF16).reshape(TP, seq, heads, HD)

    queries, keys_all, values_all = by_head(0), by_head(1), by_head(2)
    out_gate = jax.nn.sigmoid(projected[:, 3 * width :])
    forget_logit = (dot("sd,hd->sh", rows_a, w_forget) + bias).reshape(TP, seq, heads)
    decay_sum = jnp.cumsum(jax.nn.log_sigmoid(forget_logit), axis=1)
    positions = jnp.arange(seq, dtype=jnp.int32)
    inside = (positions[None] >= starts[:, None]) & (positions[None] < starts[:, None] + PIC)
    causal = positions[None, :] <= positions[:, None]
    allowed = ((causal[None] | inside[:, :, None] & inside[:, None, :]) & key_valid[:, None, :])[:, None]
    decay_heads = jnp.transpose(decay_sum, (0, 2, 1))
    spread = decay_heads[:, :, :, None] - decay_heads[:, :, None, :]
    decay_bias = jnp.where(causal, spread, -spread)
    scores = dot("gihe,gjhe->ghij", queries, keys_all) * HD ** (-0.5) + decay_bias
    masked = jnp.where(allowed, scores, NEGATIVE)
    row_max = jnp.max(masked, axis=-1, keepdims=True)
    weights = jnp.where(allowed, jnp.exp(masked - row_max), 0.0)
    probability = weights / jnp.sum(weights, axis=-1, keepdims=True)
    prob_low = probability.astype(BF16)
    attended = dot("ghij,gjhe->gihe", prob_low, values_all).reshape(TP * seq, width)
    gated_rows = (attended * out_gate).astype(BF16)
    attn_part = dot("si,io->so", gated_rows, w_rows).astype(BF16).reshape(TP, seq, model)
    (branch_attn,) = scatter_plane(reps, share, "sum_attn", 2, (attn_part,))
    middle = layer_in + branch_attn
    scale_f = lax.rsqrt(jnp.mean(middle * middle, axis=-1, keepdims=True) + EPSILON)
    rows_f_own = (middle * scale_f * gain_f).astype(BF16)

    rows_f, ffn_grad = gather_plane(reps, share, "gather_rows", 3, (rows_f_own, cotangent[0]))
    rows_f = rows_f.reshape(TP * seq, model)
    ffn_grad = ffn_grad.reshape(TP * seq, model)
    ffn_part, rows_part, in_grads, down_grads = 0.0, 0.0, [], []
    for k in range(share):
        w_in = ffn_in if k == 0 else other_in[k - 1]
        w_down = ffn_down if k == 0 else other_down[k - 1]
        gate_part = dot("sd,df->sf", rows_f, w_in[0])
        up_part = dot("sd,df->sf", rows_f, w_in[1])
        gate_sig = jax.nn.sigmoid(gate_part)
        hidden = (gate_part * gate_sig * up_part).astype(BF16)
        ffn_part = ffn_part + dot("sf,fd->sd", hidden, w_down)
        hidden_grad = dot("sd,fd->sf", ffn_grad, w_down)
        down_grads.append(dot("sf,sd->fd", hidden, ffn_grad).astype(BF16))
        gate_grad = (hidden_grad * up_part * gate_sig * (1.0 + gate_part * (1.0 - gate_sig))).astype(BF16)
        up_grad = (hidden_grad * gate_part * gate_sig).astype(BF16)
        in_grads.append(
            jnp.concatenate(
                [dot("sd,sf->df", rows_f, gate_grad).astype(BF16), dot("sd,sf->df", rows_f, up_grad).astype(BF16)]
            )
        )
        rows_part = rows_part + dot("sf,df->sd", gate_grad, w_in[0]) + dot("sf,df->sd", up_grad, w_in[1])
    rows_f_grad, branch_ffn = scatter_plane(
        reps, share, "sum_ffn", 4,
        (rows_part.astype(BF16).reshape(TP, seq, model), ffn_part.astype(BF16).reshape(TP, seq, model)),
    )
    result = middle + branch_ffn
    out_grad = cotangent[0].astype(F32)
    lifted = rows_f_grad * gain_f
    dotted_f = jnp.mean(middle * lifted, axis=-1, keepdims=True)
    middle_grad = out_grad + scale_f * lifted - middle * (scale_f * scale_f * scale_f) * dotted_f
    gain_f_grad = jnp.sum(rows_f_grad * middle * scale_f, axis=0)

    (branch_grad,) = gather_plane(reps, share, "gather_grad", 5, (middle_grad.astype(BF16),))
    ffn_in_sum, ffn_down_sum = share_sum(
        reps, share, "ffn_grads", 6, (in_grads[0], down_grads[0]),
        (jnp.stack(in_grads[1:]), jnp.stack(down_grads[1:])),
    )
    branch_grad = branch_grad.reshape(TP * seq, model)
    gated_grad = dot("so,io->si", branch_grad, w_rows)
    out_part = dot("si,so->io", gated_rows, branch_grad).astype(BF16).reshape(share, width // share, model)
    attended_grad = (gated_grad * out_gate).astype(BF16).reshape(TP, seq, heads, HD)
    outgate_grad = gated_grad * attended * (out_gate * (1.0 - out_gate))
    prob_grad = dot("gihe,gjhe->ghij", attended_grad, values_all)
    score_grad = probability * (prob_grad - jnp.sum(probability * prob_grad, axis=-1, keepdims=True))
    dotted_grad = (score_grad * HD ** (-0.5)).astype(BF16)
    query_grad = dot("ghij,gjhe->gihe", dotted_grad, keys_all)
    key_grad = dot("ghij,gihe->gjhe", dotted_grad, queries)
    value_grad = dot("ghij,gihe->gjhe", prob_low, attended_grad)
    signed = jnp.where(causal, score_grad, -score_grad)
    decay_grad = jnp.sum(signed, axis=-1) - jnp.sum(signed, axis=-2)
    later_sums = jnp.cumsum(decay_grad[..., ::-1], axis=-1)[..., ::-1]
    logit_grad = jnp.transpose(later_sums, (0, 2, 1)) * jax.nn.sigmoid(-forget_logit)
    bias_grad = jnp.sum(logit_grad, axis=(0, 1))
    logit_low = logit_grad.astype(BF16).reshape(TP * seq, heads)
    proj_grad = jnp.concatenate(
        [g.reshape(TP * seq, width) for g in (query_grad, key_grad, value_grad)] + [outgate_grad], axis=1
    ).astype(BF16)
    w_cols_grad = dot("sd,se->de", rows_a, proj_grad).astype(BF16).reshape(TP, share, held, 4 * width)
    forget_part = dot("sh,sd->hd", logit_low, rows_a)
    rows_a_part = dot("se,de->sd", proj_grad, w_cols) + dot("sh,hd->sd", logit_low, w_forget)
    (rows_a_grad,) = scatter_plane(
        reps, share, "sum_rows", 7, (rows_a_part.astype(BF16).reshape(TP, seq, model),)
    )
    own_out = lax.dynamic_index_in_dim(out_part, u, axis=0, keepdims=False)
    given_out = jnp.stack(
        [lax.dynamic_index_in_dim(out_part, (u + k) % share, axis=0, keepdims=False) for k in range(1, share)]
    )
    (out_sum,) = share_sum(reps, share, "out_grads", 8, (own_out,), (given_out,))
    in_sum = exchange_in(reps, share, 9, w_cols_grad)
    scale_a = lax.rsqrt(jnp.mean(layer_in * layer_in, axis=-1, keepdims=True) + EPSILON)
    lifted = rows_a_grad * gain_a
    dotted_a = jnp.mean(layer_in * lifted, axis=-1, keepdims=True)
    input_grad = middle_grad + scale_a * lifted - layer_in * (scale_a * scale_a * scale_a) * dotted_a
    gain_a_grad = jnp.sum(rows_a_grad * layer_in * scale_a, axis=0)

    valid_rows = valid_mask[0].astype(F32)
    valid_col = valid_rows[:, None]
    scalars = jnp.stack(
        [
            jnp.sum(result * result * valid_col),
            jnp.sum(branch_attn * branch_attn * valid_col),
            jnp.sum(branch_ffn * branch_ffn * valid_col),
            jnp.sum(valid_rows),
        ]
    )
    scalars = jnp.concatenate([scalars, bias_grad, jnp.zeros((held - 4 - heads,), F32)])
    tiles = jnp.concatenate(
        [
            gain_a_grad.reshape(1, n, held),
            gain_f_grad.reshape(1, n, held),
            forget_part.reshape(heads, n, held),
            jnp.broadcast_to(scalars, (1, n, held)),
            jnp.zeros((8 - heads - 3, n, held), F32),
        ]
    )
    tiles = jnp.pad(jnp.transpose(tiles, (1, 0, 2)), ((0, 0), (0, 0), (0, 128 - held)))
    gathered = exchange_small(reps, share, 10, tiles)
    grad_gain_a = jnp.sum(gathered[:, :, 0, :held], axis=(0, 1))
    grad_gain_f = jnp.sum(gathered[:, :, 1, :held], axis=(0, 1))
    by_chip = gathered.reshape(reps, TP, share, 8, 128)
    grad_forget = jnp.sum(by_chip[:, :, :, 2 : 2 + heads, :held], axis=(0, 2)).reshape(H, held).T
    square_sums = jnp.sum(gathered[:, :, 2 + heads, :4], axis=(0, 1))
    bias_total = jnp.sum(by_chip[:, :, :, 2 + heads, 4 : 4 + heads], axis=(0, 2)).reshape(H)
    stats = jnp.sqrt(square_sums[:3] / (square_sums[3] * model) + EPSILON)

    def over_reps(values_in):
        return jnp.sum(values_in.astype(F32), axis=0)

    grad_in = over_reps(in_sum).reshape(TP, held, 4, width)
    grad_in = jnp.transpose(grad_in, (1, 2, 0, 3)).reshape(held, 4 * model)
    return (
        result.astype(BF16)[None],
        input_grad[None],
        grad_gain_a,
        grad_in,
        grad_forget,
        bias_total,
        over_reps(out_sum),
        grad_gain_f,
        over_reps(ffn_in_sum).reshape(ffn_in.shape),
        over_reps(ffn_down_sum),
        stats,
    )


def solution(mesh):
    placed = (
        P(("rep", "fsdp"), None, None),
        P(("rep", "fsdp"), None, None),
        P(("rep", "fsdp")),
        P(("rep", "fsdp"), None),
        P("fsdp"),
        P("fsdp", None),
        P("fsdp", None),
        P(),
        P("fsdp", None),
        P("fsdp"),
        P(None, None, "fsdp"),
        P("fsdp", None),
    )
    return jax.shard_map(
        functools.partial(per_device, mesh.shape["rep"], mesh.shape["fsdp"] // TP),
        mesh=mesh,
        in_specs=placed,
        out_specs=(
            P(("rep", "fsdp"), None, None),
            P(("rep", "fsdp"), None, None),
            P("fsdp"),
            P("fsdp", None),
            P("fsdp", None),
            P(),
            P("fsdp", None),
            P("fsdp"),
            P(None, None, "fsdp"),
            P("fsdp", None),
            P(),
        ),
        check_vma=False,
    )
```

```python
import functools

import jax
import jax.numpy as jnp
from jax import lax
from jax.experimental import pallas as pl
from jax.experimental.pallas import tpu as pltpu
from jax.sharding import PartitionSpec as P

H = 24
HD = 64
PIC = 32
TP = 8
DEPTH = 4
EPSILON = 1e-06
NEGATIVE = -1e30
MESH = pl.DeviceIdType.MESH
BF16 = jnp.bfloat16
F32 = jnp.float32
VMEM = pl.BlockSpec(memory_space=pltpu.VMEM)
ANY = pl.BlockSpec(memory_space=pl.ANY)


class Net:
    def __init__(self, reps, share, sems):
        self.reps, self.share, self.sems = reps, share, sems
        self.r = lax.axis_index("rep")
        self.f = lax.axis_index("fsdp")
        self.t = lax.div(self.f, share)
        self.u = lax.rem(self.f, share)
        self.z = lax.div(self.t, 2)
        self.x = lax.rem(self.t, 2)
        self.none = self.f * 0
        self.taken = 0
        self.sent = []

    def take(self, count=1):
        base = self.taken
        self.taken += count
        return base

    def place(self, t):
        return t * self.share + self.u

    def grid(self, z, x):
        return (z * 2 + x) * self.share + self.u

    def partners(self):
        for k in range(1, self.share):
            yield k, lax.rem(self.u + k, self.share)

    def greet(self, peers):
        barrier = pltpu.get_barrier_semaphore()
        total = 0
        for cond, r, f in peers:
            if cond is None:
                pl.semaphore_signal(barrier, 1, device_id=(r, f), device_id_type=MESH)
                total = total + 1
            else:

                @pl.when(cond)
                def _():
                    pl.semaphore_signal(barrier, 1, device_id=(r, f), device_id_type=MESH)

                total = total + cond.astype(jnp.int32)
        pl.semaphore_wait(barrier, total)

    def plane_peers(self):
        return [
            (self.z < DEPTH - 1, self.r, self.grid(self.z + 1, self.x)),
            (self.z > 0, self.r, self.grid(self.z - 1, self.x)),
            (None, self.r, self.grid(self.z, 1 - self.x)),
        ]

    def share_peers(self):
        return [(None, self.r, self.t * self.share + u) for _, u in self.partners()]

    def rep_peers(self):
        return [(None, lax.rem(self.r + k, self.reps), self.f) for k in range(1, self.reps)]

    def all_plane_peers(self):
        return [(None, self.r, self.place(lax.rem(self.t + k, TP))) for k in range(1, TP)]

    def copy(self, src, dst, ssem, rsem, f, r=None):
        return pltpu.make_async_remote_copy(
            src_ref=src,
            dst_ref=dst,
            send_sem=self.sems.at[ssem],
            recv_sem=self.sems.at[rsem],
            device_id=(self.r if r is None else r, f),
            device_id_type=MESH,
        )

    def send(self, src, dst, ssem, rsem, f, r=None, cond=None):
        copy = self.copy(src, dst, ssem, rsem, f, r)
        if cond is None:
            copy.start()
        else:
            pl.when(cond)(copy.start)
        self.sent.append((cond, copy))

    def arrive(self, dst, rsem, cond=None):
        copy = pltpu.make_async_remote_copy(
            src_ref=dst,
            dst_ref=dst,
            send_sem=self.sems.at[rsem],
            recv_sem=self.sems.at[rsem],
            device_id=(self.r, self.f),
            device_id_type=MESH,
        )
        if cond is None:
            copy.wait_recv()
        else:
            pl.when(cond)(copy.wait_recv)

    def drain(self):
        for cond, copy in self.sent:
            if cond is None:
                copy.wait_send()
            else:
                pl.when(cond)(copy.wait_send)
        self.sent = []


def nearest(z, k):
    swapped = (1, 0, 2, 3)[k] if isinstance(k, int) else None
    far = lax.div(z, 2)
    edge = z + far * (3 - 2 * z)
    if swapped is None:
        inner = jnp.where(k == 0, 1, jnp.where(k == 1, 0, k))
        place = jnp.where(edge == 0, k, inner)
    else:
        place = k + edge * (swapped - k)
    return far * 3 + (1 - 2 * far) * place


class Wave:
    def __init__(self, net, block):
        self.net, self.block = net, block
        self.recv = net.take(TP)
        self.up, self.down, self.side = net.take(DEPTH), net.take(DEPTH), net.take(DEPTH)

    def copies(self, k):
        net = self.net
        z, x = net.z, net.x
        zo = nearest(z, k)
        t = zo * 2 + x
        block, sem = self.block(t), self.recv + t
        return [
            (
                (zo <= z) & (z < DEPTH - 1),
                net.copy(block, block, self.up + k, sem, net.grid(jnp.minimum(z + 1, DEPTH - 1), x)),
            ),
            (
                (zo >= z) & (z > 0),
                net.copy(block, block, self.down + k, sem, net.grid(jnp.maximum(z - 1, 0), x)),
            ),
            (None, net.copy(block, block, self.side + k, sem, net.grid(z, 1 - x))),
        ]

    def hand_on(self, k, own=False):
        net = self.net
        t = nearest(net.z, k) * 2 + net.x
        if not own:
            net.arrive(self.block(t), self.recv + t, None if isinstance(k, int) else k > 0)
        for cond, copy in self.copies(k):
            if cond is None:
                copy.start()
            else:
                pl.when(cond)(copy.start)

    def across(self, k):
        t = nearest(self.net.z, k) * 2 + 1 - self.net.x
        self.net.arrive(self.block(t), self.recv + t)

    def drain(self):
        @pl.loop(0, DEPTH)
        def _(k):
            for cond, copy in self.copies(k):
                if cond is None:
                    copy.wait_send()
                else:
                    pl.when(cond)(copy.wait_send)


class Gather:
    def __init__(self, net, part, side, up, down, total):
        self.net, self.part, self.side, self.up, self.down, self.total = net, part, side, up, down, total
        self.sems = [net.take(DEPTH) for _ in range(6)]

    def across(self, k):
        net = self.net
        zo = nearest(net.z, k)
        return net.copy(
            self.part(zo * 2 + 1 - net.x), self.side(zo), self.sems[0] + zo, self.sems[1] + zo,
            net.grid(net.z, 1 - net.x),
        )

    def along(self, k):
        net = self.net
        z = net.z
        zo = nearest(z, k)
        part = self.part(zo * 2 + net.x)
        return [
            (
                zo > z,
                net.copy(
                    part, self.up(zo), self.sems[2] + zo, self.sems[3] + zo,
                    net.grid(jnp.minimum(z + 1, DEPTH - 1), net.x),
                ),
            ),
            (
                zo < z,
                net.copy(
                    part, self.down(zo), self.sems[4] + zo, self.sems[5] + zo,
                    net.grid(jnp.maximum(z - 1, 0), net.x),
                ),
            ),
        ]

    def begin(self, k):
        self.across(k).start()

    def step(self, k):
        net = self.net
        z = net.z
        zo = nearest(z, k)
        part = self.part(zo * 2 + net.x)
        net.arrive(self.side(zo), self.sems[1] + zo)
        self.total[...] = part[...].astype(F32) + self.side(zo)[...].astype(F32)
        for cond, ref, sem in (
            ((zo >= z) & (z > 0), self.up(zo), self.sems[3]),
            ((zo <= z) & (z < DEPTH - 1), self.down(zo), self.sems[5]),
        ):

            @pl.when(cond)
            def _():
                net.arrive(ref, sem + zo)
                self.total[...] += ref[...].astype(F32)

        @pl.when(zo != z)
        def _():
            part[...] = self.total[...].astype(BF16)

        for cond, copy in self.along(k):
            pl.when(cond)(copy.start)

    def drain(self):
        @pl.loop(0, DEPTH)
        def _(k):
            self.across(k).wait_send()
            for cond, copy in self.along(k):
                pl.when(cond)(copy.wait_send)


def call(body, name, number, operands, in_specs, outs, scratch, sems, limit=60 << 20):
    return pl.pallas_call(
        body,
        name=name,
        out_shape=tuple(shape for shape, _ in outs),
        in_specs=in_specs,
        out_specs=tuple(spec for _, spec in outs),
        scratch_shapes=list(scratch) + [pltpu.SemaphoreType.DMA((sems,))],
        compiler_params=pltpu.CompilerParams(
            collective_id=number, has_side_effects=True, vmem_limit_bytes=limit
        ),
    )(*operands)


def chunk(rows, count, c):
    return pl.ds(c * (rows // count), rows // count)


def matmul_nt(a, b):
    return lax.dot_general(a, b, (((1,), (1,)), ((), ())), preferred_element_type=F32)


def matmul_tn(a, b):
    return lax.dot_general(a, b, (((0,), (0,)), ((), ())), preferred_element_type=F32)


def matmul(a, b):
    return jnp.dot(a, b, preferred_element_type=F32)


def tile(j, size):
    return pl.ds(pl.multiple_of(j * size, size), size)


PIECES = 2


def feed_forward(reps, share, x, branch, gain, valid, cot, w_in, w_down):
    seq, model = x.shape
    hs = w_in.shape[2]
    hidden_all = share * hs
    rows_all = TP * seq
    pair = 2 * seq
    half = seq // PIECES

    def body(
        x_ref, branch_ref, gain_ref, valid_ref, cot_ref, in_ref, down_ref,
        act_ref, grad_ref, sums_ref, in_out, down_out,
        middle, rows, cot_all, w_all, wd, hid, grads, part, side, up, down, rows_sum, ffn_sum,
        in_part, down_part, in_got, down_got, local, sems,
    ):
        net = Net(reps, share, sems)
        own = [
            pltpu.make_async_copy(in_ref.at[0], w_all.at[:, pl.ds(0, hs)], local.at[0]),
            pltpu.make_async_copy(in_ref.at[1], w_all.at[:, pl.ds(hs, hs)], local.at[1]),
            pltpu.make_async_copy(down_ref, wd.at[pl.ds(0, hs)], local.at[2]),
            pltpu.make_async_copy(cot_ref, cot_all, local.at[3]),
        ]
        for copy in own:
            copy.start()

        def block(ref, t):
            return ref.at[tile(t, seq)]

        middle[...] = x_ref[...].astype(F32) + branch_ref[...]
        scale = lax.rsqrt(jnp.mean(middle[...] * middle[...], axis=-1, keepdims=True) + EPSILON)
        block(rows, net.t)[...] = (middle[...] * scale * gain_ref[1:2]).astype(BF16)
        net.greet(net.plane_peers() + net.share_peers() + net.rep_peers())

        waves = [
            Wave(net, lambda t, c=c: rows.at[pl.ds(pl.multiple_of(t * seq + c * half, half), half)])
            for c in range(PIECES)
        ]
        weights = net.take(3 * share), net.take(3 * share)
        for wave in waves:
            wave.hand_on(0, own=True)
        arriving = []
        for k, u in net.partners():
            f, p = net.t * share + u, share - k
            for j, (src, dst) in enumerate(
                [
                    (in_ref.at[0], w_all.at[:, pl.ds(2 * hs * p, hs)]),
                    (in_ref.at[1], w_all.at[:, pl.ds(2 * hs * p + hs, hs)]),
                    (down_ref, wd.at[pl.ds(hs * p, hs)]),
                ]
            ):
                net.send(src, dst, weights[0] + 3 * k + j, weights[1] + 3 * p + j, f)
                arriving.append((dst, weights[1] + 3 * p + j))

        def unit(k):
            at = tile(nearest(net.z, k), pair)
            projected = matmul(rows[at], w_all[...])
            hidden_grad = matmul_nt(cot_all[at], wd[...])
            for p in range(share):
                gate = projected[:, 2 * hs * p : 2 * hs * p + hs]
                lift = projected[:, 2 * hs * p + hs : 2 * hs * (p + 1)]
                back = hidden_grad[:, hs * p : hs * (p + 1)]
                sig = jax.nn.sigmoid(gate)
                silu = gate * sig
                hid[at, hs * p : hs * (p + 1)] = (silu * lift).astype(BF16)
                grads[at, 2 * hs * p : 2 * hs * p + hs] = (
                    back * lift * sig * (1.0 + gate * (1.0 - sig))
                ).astype(BF16)
                grads[at, 2 * hs * p + hs : 2 * hs * (p + 1)] = (back * silu).astype(BF16)

            @pl.loop(0, 3)
            def _(j):
                to = tile(j, model // 3)
                part[0, at, to] = matmul_nt(grads[at], w_all[to]).astype(BF16)
                part[1, at, to] = matmul(hid[at], wd[:, to]).astype(BF16)

        @pl.loop(1, DEPTH + 1)
        def _(k):
            @pl.when(k < DEPTH)
            def _():
                for wave in waves:
                    wave.hand_on(k)

            @pl.when(k == 1)
            def _():
                for copy in own:
                    copy.wait()
                for dst, sem in arriving:
                    net.arrive(dst, sem)

            for wave in waves:
                wave.across(k - 1)
            unit(k - 1)

        def piece(ref, i, c, count):
            return lambda j: ref.at[i, pl.ds(pl.multiple_of(j * seq + c * half, half), half)]

        gathers = [
            [
                Gather(
                    net, piece(part, i, c, TP), piece(side, i, c, DEPTH), piece(up, i, c, DEPTH),
                    piece(down, i, c, DEPTH), total.at[pl.ds(c * half, half)],
                )
                for c in range(PIECES)
            ]
            for i, total in enumerate((rows_sum, ffn_sum))
        ]
        for both in gathers:

            @pl.loop(0, DEPTH)
            def _(j):
                for gather in both:
                    gather.begin(DEPTH - 1 - j)

        @pl.loop(0, model // 256)
        def _(j):
            at = tile(j, 256)
            in_part[at] = matmul_tn(rows[:, at], grads[...]).astype(BF16)

        @pl.loop(0, 3)
        def _(j):
            at = tile(j, model // 3)
            down_part[:, at] = matmul_tn(hid[...], cot_all[:, at]).astype(BF16)

        first, arrived = net.take(2 * share), net.take(2 * share)
        away, back = net.take(2 * reps), net.take(2 * reps)
        for k, u in net.partners():
            f, slot = net.t * share + u, share - 1 - k
            net.send(
                in_part.at[:, pl.ds(2 * hs * k, 2 * hs)], in_got.at[slot], first + 2 * k, arrived + 2 * slot, f
            )
            net.send(
                down_part.at[pl.ds(hs * k, hs)], down_got.at[slot], first + 2 * k + 1, arrived + 2 * slot + 1, f
            )

        def own_grads():
            for slot in range(share - 1):
                net.arrive(in_got.at[slot], arrived + 2 * slot)
                net.arrive(down_got.at[slot], arrived + 2 * slot + 1)

            @pl.loop(0, model // 256)
            def _(j):
                at = tile(j, 256)
                total = in_part[at, : 2 * hs].astype(F32)
                for slot in range(share - 1):
                    total = total + in_got[slot, at].astype(F32)
                in_out[net.r, at] = total.astype(BF16)

            total = down_part[:hs].astype(F32)
            for slot in range(share - 1):
                total = total + down_got[slot].astype(F32)
            down_out[net.r] = total.astype(BF16)
            for k in range(1, reps):
                r = lax.rem(net.r + k, reps)
                net.send(in_out.at[net.r], in_out.at[net.r], away + 2 * k, back + 2 * net.r, net.f, r=r)
                net.send(down_out.at[net.r], down_out.at[net.r], away + 2 * k + 1, back + 2 * net.r + 1, net.f, r=r)

        def steps(both, start, stop):
            @pl.loop(start, stop)
            def _(j):
                for gather in both:
                    gather.step(DEPTH - 1 - j)

        steps(gathers[0], 0, 2)
        own_grads()
        steps(gathers[0], 2, DEPTH)
        steps(gathers[1], 0, DEPTH)

        result = middle[...] + ffn_sum[...]
        act_ref[...] = result.astype(BF16)
        valid_col = valid_ref[...]
        scale = lax.rsqrt(jnp.mean(middle[...] * middle[...], axis=-1, keepdims=True) + EPSILON)
        lifted = rows_sum[...] * gain_ref[1:2]
        mean = jnp.mean(middle[...] * lifted, axis=-1, keepdims=True)
        grad_ref[...] = (
            block(cot_all, net.t)[...].astype(F32) + scale * lifted - middle[...] * (scale * scale * scale) * mean
        )
        sums_ref[...] = jnp.zeros_like(sums_ref)
        sums_ref[0:1] = jnp.sum(rows_sum[...] * middle[...] * scale, axis=0, keepdims=True)
        sums_ref[1:2] = jnp.sum(result * result * valid_col, axis=0, keepdims=True)
        sums_ref[2:3] = jnp.sum(branch_ref[...] * branch_ref[...] * valid_col, axis=0, keepdims=True)
        sums_ref[3:4] = jnp.sum(ffn_sum[...] * ffn_sum[...] * valid_col, axis=0, keepdims=True)
        for k in range(1, reps):
            r = lax.rem(net.r + k, reps)
            net.arrive(in_out.at[r], back + 2 * r)
            net.arrive(down_out.at[r], back + 2 * r + 1)
        net.drain()
        for wave in waves:
            wave.drain()
        for gather in gathers[0] + gathers[1]:
            gather.drain()

    shape = jax.ShapeDtypeStruct
    line = pltpu.VMEM((2, DEPTH * seq, model), BF16)
    return call(
        body, "feed_forward", 3, (x, branch, gain, valid, cot, w_in, w_down), [VMEM] * 4 + [ANY] * 3,
        [
            (shape((seq, model), BF16), VMEM),
            (shape((seq, model), F32), VMEM),
            (shape((8, model), F32), VMEM),
            (shape((reps, model, 2 * hs), BF16), VMEM),
            (shape((reps, hs, model), BF16), VMEM),
        ],
        [
            pltpu.VMEM((seq, model), F32),
            pltpu.VMEM((rows_all, model), BF16),
            pltpu.VMEM((rows_all, model), BF16),
            pltpu.VMEM((model, 2 * hidden_all), BF16),
            pltpu.VMEM((hidden_all, model), BF16),
            pltpu.VMEM((rows_all, hidden_all), BF16),
            pltpu.VMEM((rows_all, 2 * hidden_all), BF16),
            pltpu.VMEM((2, rows_all, model), BF16),
            line, line, line,
            pltpu.VMEM((seq, model), F32),
            pltpu.VMEM((seq, model), F32),
            pltpu.VMEM((model, 2 * hidden_all), BF16),
            pltpu.VMEM((hidden_all, model), BF16),
            pltpu.VMEM((share - 1, model, 2 * hs), BF16),
            pltpu.VMEM((share - 1, hs, model), BF16),
            pltpu.SemaphoreType.DMA((4,)),
        ],
        40 * PIECES + 24 * 2 * PIECES + 20 * share + 10 * reps,
    )


HEADS = H // TP
ROWS = 16


def lane_mask(shape, low, high):
    lane = lax.broadcasted_iota(jnp.int32, shape, 1)
    return (lane >= low) & (lane < high)


def head_pieces(t, block):
    base = block * H * HD + t * HEADS * HD
    return [(base, 2 * HD, block * 2 * HD), (base + 2 * HD, HD, 8 * HD + block * HD)]


def attention(reps, share, x, cot, w_in, small, w_out, bias_row, bias_col):
    n = TP * share
    seq, model = x.shape
    held = w_in.shape[0]
    width = 4 * HEADS * HD
    rows_all = TP * seq
    pair = 2 * seq
    half = seq // PIECES
    last = HEADS - 1

    def body(
        x_ref, cot_ref, in_ref, small_ref, out_ref, bias_row_ref, bias_col_ref,
        branch_ref, cot_out, rows_out, proj_out, sig_out, att_out, prob_out, logit_ref, wc_out, wo_out, wf_ref, gains_ref,
        xs, cots, rows, proj, sig, att, prob, wc, wo, split, smalls, lines, part, side, up, down, gated, local, sems,
    ):
        net = Net(reps, share, sems)

        def seq_block(ref, t):
            return ref.at[tile(t, seq)]

        def held_rows(f):
            return wc.at[tile(f, held)]

        own = [
            pltpu.make_async_copy(x_ref, seq_block(xs, net.t), local.at[0]),
            pltpu.make_async_copy(cot_ref, seq_block(cots, net.t), local.at[1]),
            pltpu.make_async_copy(small_ref, smalls.at[net.f], local.at[2]),
            pltpu.make_async_copy(out_ref, wo.at[tile(net.u, held)], local.at[3]),
        ]
        for copy in own:
            copy.start()
        for t in range(TP):
            for block in range(4):
                for column, wide, to in head_pieces(t, block):
                    split[t, :, to : to + wide] = in_ref[:, column : column + wide]
        wo[share * held :] = jnp.zeros((wo.shape[0] - share * held, model), BF16)
        others = [lax.rem(net.f + k, n) for k in range(n)]
        chips = [lax.rem(net.t + k, TP) for k in range(TP)]
        partners = list(net.partners())
        net.greet([(None, net.r, f) for f in others[1:]])

        small_send, small_recv = net.take(n), net.take(n)
        w_send, w_recv = net.take(TP), net.take(n)
        w_pass = net.take(share * TP)
        wo_send, wo_recv = net.take(share), net.take(share)
        for k in range(1, n):
            net.send(small_ref, smalls.at[net.f], small_send + k, small_recv + net.f, others[k])
        for k in range(1, TP):
            net.send(split.at[chips[k]], held_rows(net.f), w_send + k, w_recv + net.f, net.place(chips[k]))
        own_cols = pltpu.make_async_copy(split.at[net.t], held_rows(net.f), local.at[4])
        own_cols.start()
        for k, u in partners:
            f = net.t * share + u
            net.send(split.at[net.t], held_rows(net.f), w_pass + k, w_recv + net.f, f)
            net.send(out_ref, wo.at[tile(net.u, held)], wo_send + k, wo_recv + net.u, f)

        def pieces(ref):
            return [
                Wave(net, lambda t, c=c: ref.at[pl.ds(pl.multiple_of(t * seq + c * half, half), half)])
                for c in range(PIECES)
            ]

        waves, cot_waves = pieces(xs), pieces(cots)
        for copy in own:
            copy.wait()
        for wave in waves:
            wave.hand_on(0, own=True)
        for wave in cot_waves:
            wave.copies(0)[2][1].start()

        def weights():
            for k in range(1, TP):
                source = net.place(chips[k])
                net.arrive(held_rows(source), w_recv + source)
                for j, u in partners:
                    net.send(
                        held_rows(source), held_rows(source), w_pass + share * k + j, w_recv + source,
                        net.t * share + u,
                    )
            for k in range(1, n):
                net.arrive(smalls.at[others[k]], small_recv + others[k])
            for j in range(model // 128):
                line = jnp.zeros((32, 128), F32)
                for f in range(j * 128 // held, ((j + 1) * 128 - 1) // held + 1):
                    start = f * held - j * 128
                    piece = pltpu.roll(smalls[f].astype(F32), net.none + start % 128, 1)
                    line = jnp.where(lane_mask((32, 128), start, start + held), piece, line)
                lines[:, j * 128 : (j + 1) * 128] = line
            pick = lax.broadcasted_iota(jnp.int32, (ROWS, 32), 0) + HEADS * net.t
            pick = pick == lax.broadcasted_iota(jnp.int32, (ROWS, 32), 1)
            pick &= lax.broadcasted_iota(jnp.int32, (ROWS, 32), 0) < HEADS
            wf_ref[...] = matmul(pick.astype(BF16), lines[...].astype(BF16)).astype(BF16)
            gains_ref[...] = lines[H : H + 8]
            for k, u in partners:
                net.arrive(wo.at[tile(u, held)], wo_recv + u)
                for t in range(TP):
                    net.arrive(held_rows(t * share + u), w_recv + t * share + u)
            own_cols.wait()

        square = (seq, seq)
        at_row = lax.broadcasted_iota(jnp.int32, square, 0)
        at_col = lax.broadcasted_iota(jnp.int32, square, 1)

        def unit(k):
            place = nearest(net.z, k)
            at = tile(place, pair)
            values_in = xs[at].astype(F32)
            inverse = lax.rsqrt(jnp.mean(values_in * values_in, axis=-1, keepdims=True) + EPSILON)
            rows[at] = (values_in * inverse * gains_ref[0:1]).astype(BF16)
            projected = matmul(rows[at], wc[...])
            proj[at] = projected.astype(BF16)
            sig[at, : 2 * HD] = jax.nn.sigmoid(projected[:, 6 * HD : 8 * HD])
            tail = pltpu.roll(jax.nn.sigmoid(projected[:, 10 * HD : 12 * HD]), net.none + HD, 1)
            sig[at, 2 * HD :] = jnp.where(lane_mask(tail.shape, 0, HD), tail, 0.0)

            @pl.loop(0, 2)
            def _(j):
                t = place * 2 + j
                here = tile(t, seq)
                marks = smalls[net.place(t)].astype(F32)
                valid = marks[H + 2 : H + 3]
                start = marks[H + 3 : H + 4].astype(jnp.int32)
                causal = at_col <= at_row
                inside = (at_row >= start) & (at_row < start + PIC) & (at_col >= start) & (at_col < start + PIC)
                allowed = (causal | inside) & (valid > 0.0)
                sign = jnp.where(causal, 1.0, -1.0)
                below = sign * 0.5 + 0.5
                logit_col = matmul_nt(rows[here], wf_ref[...]) + bias_row_ref[...]
                logit_row = matmul_nt(wf_ref[...], rows[here]) + bias_col_ref[...]
                logit_ref[t] = logit_row
                decay_col = jnp.dot(
                    below, log_sigmoid(logit_col), precision=lax.Precision.HIGHEST, preferred_element_type=F32
                )
                decay_row = lax.dot_general(
                    log_sigmoid(logit_row), below, (((1,), (1,)), ((), ())),
                    precision=lax.Precision.HIGHEST, preferred_element_type=F32,
                )
                outs = []
                for h in range(HEADS):
                    if h < last:
                        query = jnp.where(lane_mask((seq, 2 * HD), h * HD, h * HD + HD), proj[here, : 2 * HD], 0)
                        key, value = proj[here, 2 * HD : 4 * HD], proj[here, 4 * HD : 6 * HD]
                    else:
                        query = jnp.where(lane_mask((seq, 2 * HD), 0, HD), proj[here, 8 * HD : 10 * HD], 0)
                        key = pltpu.roll(proj[here, 8 * HD : 10 * HD].astype(F32), net.none + HD, 1).astype(BF16)
                        value = proj[here, 10 * HD :]
                    scores = matmul_nt(query, key) * HD ** (-0.5)
                    scores = scores + sign * (decay_col[:, h : h + 1] - decay_row[h : h + 1])
                    masked = jnp.where(allowed, scores, NEGATIVE)
                    weights_now = jnp.exp(masked - jnp.max(masked, axis=-1, keepdims=True))
                    probability = weights_now / jnp.sum(weights_now, axis=-1, keepdims=True)
                    prob[t * HEADS + h] = probability
                    outs.append(matmul(probability.astype(BF16), value))
                low = lane_mask((seq, 2 * HD), 0, HD)
                att[here, : 2 * HD] = jnp.where(low, outs[0], outs[1])
                att[here, 2 * HD :] = jnp.where(low, outs[2], 0.0)

            gated[...] = (att[at] * sig[at]).astype(BF16)

            @pl.loop(0, 3)
            def _(j):
                to = tile(j, model // 3)
                part[at, to] = matmul(gated[...], wo[:, to]).astype(BF16)

        for wave in waves:
            wave.hand_on(1)
        weights()

        @pl.loop(1, DEPTH + 1)
        def _(k):
            @pl.when((k > 1) & (k < DEPTH))
            def _():
                for wave in waves:
                    wave.hand_on(k)

            @pl.when(k == DEPTH - 1)
            def _():
                for wave in cot_waves:
                    for cond, copy in wave.copies(0)[:2]:
                        pl.when(cond)(copy.start)

            for wave in waves:
                wave.across(k - 1)
            unit(k - 1)

        keep = [
            pltpu.make_async_copy(src, dst, local.at[5 + i])
            for i, (src, dst) in enumerate(
                [
                    (rows, rows_out), (proj, proj_out), (sig, sig_out), (att, att_out), (prob, prob_out),
                    (wc, wc_out), (wo, wo_out),
                ]
            )
        ]
        gathers = [
            Gather(
                net,
                *[
                    lambda j, ref=ref, c=c: ref.at[pl.ds(pl.multiple_of(j * seq + c * half, half), half)]
                    for ref in (part, side, up, down)
                ],
                branch_ref.at[pl.ds(c * half, half)],
            )
            for c in range(PIECES)
        ]

        @pl.loop(0, DEPTH)
        def _(j):
            for gather in gathers:
                gather.begin(DEPTH - 1 - j)

        for copy in keep:
            copy.start()

        @pl.loop(0, DEPTH)
        def _(j):
            for gather in gathers:
                gather.step(DEPTH - 1 - j)

            @pl.when(j < DEPTH - 1)
            def _():
                for wave in cot_waves:
                    wave.hand_on(j + 1)

        for k in range(DEPTH):
            for wave in cot_waves:
                wave.across(k)
        save = pltpu.make_async_copy(cots, cot_out, local.at[1])
        save.start()
        net.drain()
        for wave in waves + cot_waves:
            wave.drain()
        for gather in gathers:
            gather.drain()
        for copy in keep:
            copy.wait()
        save.wait()

    shape = jax.ShapeDtypeStruct
    line = pltpu.VMEM((DEPTH * seq, model), BF16)
    kept = [
        ((rows_all, model), BF16),
        ((rows_all, model), BF16),
        ((rows_all, width), BF16),
        ((rows_all, 4 * HD), F32),
        ((rows_all, 4 * HD), F32),
        ((TP * HEADS, seq, seq), F32),
    ]
    return call(
        body, "attention", 1, (x, cot, w_in, small, w_out, bias_row, bias_col),
        [ANY, ANY, VMEM, VMEM, ANY, VMEM, VMEM],
        [(shape((seq, model), F32), VMEM)]
        + [(shape(*what), ANY) for what in kept]
        + [
            (shape((TP, ROWS, seq), F32), VMEM),
            (shape((model, width), BF16), ANY),
            (shape((4 * HD, model), BF16), ANY),
            (shape((ROWS, model), BF16), VMEM),
            (shape((8, model), F32), VMEM),
        ],
        [pltpu.VMEM((rows_all, model), BF16)]
        + [pltpu.VMEM(*what) for what in kept]
        + [
            pltpu.VMEM((model, width), BF16),
            pltpu.VMEM((4 * HD, model), BF16),
            pltpu.VMEM((TP, held, width), BF16),
            pltpu.VMEM((n, 32, 128), BF16),
            pltpu.VMEM((32, model), F32),
            pltpu.VMEM((rows_all, model), BF16),
            line, line, line,
            pltpu.VMEM((pair, 4 * HD), BF16),
            pltpu.SemaphoreType.DMA((12,)),
        ],
        2 * 20 * PIECES + 24 * PIECES + 3 * n + TP + share * TP + 2 * share,
    )


def attention_back(
    reps, share, x, middle_grad, sums, valid, rows_a, proj, sig, att, prob, logit, wc, wo, wf, gains
):
    n = TP * share
    seq, model = x.shape
    width = 4 * HEADS * HD
    held = model // n
    rows_all = TP * seq
    pair = 2 * seq
    half = seq // PIECES
    last = HEADS - 1
    window = 256

    def body(
        x_ref, grad_ref, sums_ref, valid_ref, rows_in, proj_in, sig_in, att_in, prob_in, logit_ref, wc_in, wo_in, wf_ref,
        gains_ref, input_ref, in_ref, out_ref, small_ref,
        rows, proj, sig, att, prob, wcs, wos, bgs, pg, gated, part, side, up, down, rows_sum, ag, og, low_logit, bias_sum,
        forget_sum, lines, in_part, in_got, in_all, out_part, out_got, out_all, small_got, small_mid, local, sems,
    ):
        net = Net(reps, share, sems)
        others = [lax.rem(net.f + k, n) for k in range(n)]
        chips = [lax.rem(net.t + k, TP) for k in range(TP)]
        partners = list(net.partners())
        own = [
            pltpu.make_async_copy(src, dst, local.at[i])
            for i, (src, dst) in enumerate(
                [
                    (wo_in, wos), (sig_in, sig), (att_in, att), (proj_in, proj), (prob_in, prob), (rows_in, rows),
                    (wc_in, wcs),
                ]
            )
        ]
        for copy in own:
            copy.start()
        bgs[tile(net.t, seq)] = grad_ref[...].astype(BF16)
        net.greet([(None, net.r, f) for f in others[1:]] + net.rep_peers())
        waves = [
            Wave(net, lambda t, c=c: bgs.at[pl.ds(pl.multiple_of(t * seq + c * half, half), half)])
            for c in range(PIECES)
        ]
        for wave in waves:
            wave.hand_on(0, own=True)
        bias_sum[...] = jnp.zeros_like(bias_sum)
        forget_sum[...] = jnp.zeros_like(forget_sum)
        for copy in own:
            copy.wait()

        square = (seq, seq)
        causal = lax.broadcasted_iota(jnp.int32, square, 1) <= lax.broadcasted_iota(jnp.int32, square, 0)
        below = jnp.where(causal, 1.0, 0.0)
        low = lane_mask((seq, 2 * HD), 0, HD)
        head_row = lax.broadcasted_iota(jnp.int32, (ROWS, seq), 0)

        def unit(k):
            place = nearest(net.z, k)
            at = tile(place, pair)
            gated_grad = matmul_nt(bgs[at], wos[...])
            gate, attended = sig[at], att[at]
            ag[...] = (gated_grad * gate).astype(BF16)
            gated[at] = (attended * gate).astype(BF16)
            gate_grad = gated_grad * attended * (gate * (1.0 - gate))
            pg[at, 6 * HD : 8 * HD] = gate_grad[:, : 2 * HD].astype(BF16)
            og[...] = pltpu.roll(gate_grad[:, 2 * HD :], net.none + HD, 1)

            @pl.loop(0, 2)
            def _(j):
                t = place * 2 + j
                here = tile(t, seq)
                inner = tile(j, seq)
                swapped = pltpu.roll(proj[here, 8 * HD : 10 * HD].astype(F32), net.none + HD, 1).astype(BF16)
                decay_grad = jnp.zeros((ROWS, seq), F32)
                found = []
                for h in range(HEADS):
                    probability = prob[t * HEADS + h]
                    if h < last:
                        back_all = ag[inner, : 2 * HD]
                        back = jnp.where(lane_mask((seq, 2 * HD), h * HD, h * HD + HD), back_all, 0)
                        query, key, value = (proj[here, 2 * HD * i : 2 * HD * (i + 1)] for i in range(3))
                    else:
                        back = back_all = ag[inner, 2 * HD :]
                        query, key, value = swapped, swapped, proj[here, 10 * HD :]
                    prob_grad = matmul_nt(back, value)
                    score_grad = probability * (
                        prob_grad - jnp.sum(probability * prob_grad, axis=-1, keepdims=True)
                    )
                    dotted_grad = (score_grad * HD ** (-0.5)).astype(BF16)
                    found.append(
                        (
                            matmul(dotted_grad, key),
                            matmul_tn(dotted_grad, query),
                            matmul_tn(probability.astype(BF16), back_all),
                        )
                    )
                    signed = jnp.where(causal, score_grad, -score_grad)
                    line = jnp.sum(signed.T - signed, axis=0, keepdims=True)
                    decay_grad = jnp.where(head_row == h, line, decay_grad)
                for i in range(3):
                    pg[here, 2 * HD * i : 2 * HD * (i + 1)] = jnp.where(low, found[0][i], found[1][i]).astype(BF16)
                pg[here, 8 * HD : 10 * HD] = jnp.where(low, found[2][0], found[2][1]).astype(BF16)
                pg[here, 10 * HD :] = jnp.where(low, found[2][2], og[inner]).astype(BF16)
                later = jnp.dot(decay_grad, below, precision=lax.Precision.HIGHEST, preferred_element_type=F32)
                logit_grad = later * jax.nn.sigmoid(-logit_ref[t])
                bias_sum[...] += logit_grad
                low_logit[j] = logit_grad.astype(BF16)
                forget_sum[...] += matmul(logit_grad.astype(BF16), rows[here])

            @pl.loop(0, 3)
            def _(i):
                to = tile(i, model // 3)
                main = matmul_nt(pg[at], wcs[to])
                for j in range(2):
                    extra = matmul_tn(low_logit[j], wf_ref[:, to])
                    part[tile(place * 2 + j, seq), to] = (main[j * seq : (j + 1) * seq] + extra).astype(BF16)

        @pl.loop(1, DEPTH + 1)
        def _(k):
            @pl.when(k < DEPTH)
            def _():
                for wave in waves:
                    wave.hand_on(k)

            for wave in waves:
                wave.across(k - 1)
            unit(k - 1)

        gathers = [
            Gather(
                net,
                *[
                    lambda j, ref=ref, c=c: ref.at[pl.ds(pl.multiple_of(j * seq + c * half, half), half)]
                    for ref in (part, side, up, down)
                ],
                rows_sum.at[pl.ds(c * half, half)],
            )
            for c in range(PIECES)
        ]

        @pl.loop(0, DEPTH)
        def _(j):
            for gather in gathers:
                gather.begin(DEPTH - 1 - j)

        @pl.loop(0, model // 256)
        def _(j):
            at = tile(j, 256)
            in_part[at] = matmul_tn(rows[:, at], pg[...]).astype(BF16)

        @pl.loop(0, 3)
        def _(j):
            at = tile(j, model // 3)
            out_part[:, at] = matmul_tn(gated[...], bgs[:, at]).astype(BF16)

        def owned(t, u):
            return tile(t * share + u, held)

        in_send, in_recv = net.take(share * TP), net.take(share * TP)
        out_send, out_recv = net.take(share), net.take(share)
        over, landed = net.take(TP), net.take(TP)
        away, back_in = net.take(TP * reps), net.take(TP * reps)
        out_away, out_back = net.take(reps), net.take(reps)
        small_send, small_recv = net.take(n), net.take(n)
        mid_send, mid_recv = net.take(reps), net.take(reps)
        for k, u in partners:
            slot, f = share - 1 - k, net.t * share + u
            for j in range(TP):
                t = chips[(j + 1) % TP]
                net.send(
                    in_part.at[owned(t, u)], in_got.at[slot, t], in_send + share * j + k, in_recv + share * t + slot, f
                )
            net.send(out_part.at[tile(u, held)], out_got.at[slot], out_send + k, out_recv + slot, f)

        def steps(start, stop):
            @pl.loop(start, stop)
            def _(j):
                for gather in gathers:
                    gather.step(DEPTH - 1 - j)

        steps(0, 1)
        for j in range(TP):
            t = chips[(j + 1) % TP]
            total = in_part[owned(t, net.u)].astype(F32)
            for slot in range(share - 1):
                net.arrive(in_got.at[slot, t], in_recv + share * t + slot)
                total = total + in_got[slot, t].astype(F32)
            if j < TP - 1:
                in_part[owned(t, net.u)] = total.astype(BF16)
            else:
                in_all[net.r, t] = total.astype(BF16)
        total = out_part[tile(net.u, held)].astype(F32)
        for slot in range(share - 1):
            net.arrive(out_got.at[slot], out_recv + slot)
            total = total + out_got[slot].astype(F32)
        out_all[net.r] = total.astype(BF16)
        for j in range(TP - 1):
            t = chips[j + 1]
            net.send(in_part.at[owned(t, net.u)], in_all.at[net.r, net.t], over + j, landed + net.t, net.place(t))
        replicas = [lax.rem(net.r + k, reps) for k in range(reps)]
        for k in range(1, reps):
            net.send(
                out_all.at[net.r], out_all.at[net.r], out_away + k, out_back + net.r, net.f, r=replicas[k]
            )
            net.send(
                in_all.at[net.r, net.t], in_all.at[net.r, net.t], away + k, back_in + TP * net.r + net.t, net.f,
                r=replicas[k],
            )
        steps(1, DEPTH)

        layer_in = x_ref[...].astype(F32)
        scale = lax.rsqrt(jnp.mean(layer_in * layer_in, axis=-1, keepdims=True) + EPSILON)
        lifted = rows_sum[...] * gains_ref[0:1]
        mean = jnp.mean(layer_in * lifted, axis=-1, keepdims=True)
        input_ref[...] = grad_ref[...] + scale * lifted - layer_in * (scale * scale * scale) * mean
        lines[...] = jnp.zeros_like(lines)
        lines[0:1, :model] = jnp.sum(rows_sum[...] * layer_in * scale, axis=0, keepdims=True)
        lines[1:2, :model] = sums_ref[0:1]
        lines[2 : 2 + HEADS, :model] = forget_sum[:HEADS]
        for i in range(3):
            lines[5 + i : 6 + i] = jnp.broadcast_to(
                jnp.sum(sums_ref[1 + i : 2 + i], axis=1, keepdims=True), (1, model + window)
            )
        lines[8:9] = jnp.broadcast_to(jnp.sum(valid_ref[...], axis=0, keepdims=True), (1, model + window))
        lines[9 : 9 + HEADS] = jnp.broadcast_to(
            jnp.sum(bias_sum[:HEADS], axis=1, keepdims=True), (HEADS, model + window)
        )

        def seen(f):
            return pl.ds(pl.multiple_of(lax.div(f * held, 128) * 128, 128), window)

        small_got[net.f] = lines[:, seen(net.f)]
        for k in range(1, n):
            net.send(
                lines.at[:, seen(others[k])], small_got.at[net.f], small_send + k, small_recv + net.f, others[k]
            )
        for j in range(1, TP):
            t = chips[TP - j]
            net.arrive(in_all.at[net.r, t], landed + t)
            for k in range(1, reps):
                net.send(
                    in_all.at[net.r, t], in_all.at[net.r, t], away + reps * j + k, back_in + TP * net.r + t, net.f,
                    r=replicas[k],
                )
        for k in range(1, n):
            net.arrive(small_got.at[others[k]], small_recv + others[k])
        for t in range(TP):
            total = small_got[t * share]
            for u in range(1, share):
                total = total + small_got[t * share + u]
            small_mid[net.r, t] = total
        for k in range(1, reps):
            net.send(
                small_mid.at[net.r], small_mid.at[net.r], mid_send + k, mid_recv + net.r, net.f, r=replicas[k]
            )
        for k in range(1, reps):
            r = replicas[k]
            net.arrive(out_all.at[r], out_back + r)
            for t in range(TP):
                net.arrive(in_all.at[r, t], back_in + TP * r + t)
            net.arrive(small_mid.at[r], mid_recv + r)
        for t in range(TP):
            for block in range(4):
                for column, wide, to in head_pieces(t, block):
                    total = in_all[0, t, :, to : to + wide].astype(F32)
                    for r in range(1, reps):
                        total = total + in_all[r, t, :, to : to + wide].astype(F32)
                    in_ref[:, column : column + wide] = total
        total, small = out_all[0].astype(F32), small_mid[0]
        for r in range(1, reps):
            total = total + out_all[r].astype(F32)
            small = small + small_mid[r]
        out_ref[...] = total
        small_ref[...] = small
        net.drain()
        for wave in waves:
            wave.drain()
        for gather in gathers:
            gather.drain()

    shape = jax.ShapeDtypeStruct
    line = pltpu.VMEM((DEPTH * seq, model), BF16)
    return call(
        body, "attention_back", 5,
        (x, middle_grad, sums, valid, rows_a, proj, sig, att, prob, logit, wc, wo, wf, gains),
        [VMEM] * 4 + [ANY] * 5 + [VMEM, ANY, ANY, VMEM, VMEM],
        [
            (shape((seq, model), F32), VMEM),
            (shape((held, 4 * model), F32), VMEM),
            (shape((held, model), F32), VMEM),
            (shape((TP, ROWS, window), F32), VMEM),
        ],
        [
            pltpu.VMEM((rows_all, model), BF16),
            pltpu.VMEM((rows_all, width), BF16),
            pltpu.VMEM((rows_all, 4 * HD), F32),
            pltpu.VMEM((rows_all, 4 * HD), F32),
            pltpu.VMEM((TP * HEADS, seq, seq), F32),
            pltpu.VMEM((model, width), BF16),
            pltpu.VMEM((4 * HD, model), BF16),
            pltpu.VMEM((rows_all, model), BF16),
            pltpu.VMEM((rows_all, width), BF16),
            pltpu.VMEM((rows_all, 4 * HD), BF16),
            pltpu.VMEM((rows_all, model), BF16),
            line, line, line,
            pltpu.VMEM((seq, model), F32),
            pltpu.VMEM((pair, 4 * HD), BF16),
            pltpu.VMEM((pair, 2 * HD), F32),
            pltpu.VMEM((2, ROWS, seq), BF16),
            pltpu.VMEM((ROWS, seq), F32),
            pltpu.VMEM((ROWS, model), F32),
            pltpu.VMEM((ROWS, model + window), F32),
            pltpu.VMEM((model, width), BF16),
            pltpu.VMEM((share - 1, TP, held, width), BF16),
            pltpu.VMEM((reps, TP, held, width), BF16),
            pltpu.VMEM((4 * HD, model), BF16),
            pltpu.VMEM((share - 1, held, model), BF16),
            pltpu.VMEM((reps, held, model), BF16),
            pltpu.VMEM((n, ROWS, window), F32),
            pltpu.VMEM((reps, TP, ROWS, window), F32),
            pltpu.SemaphoreType.DMA((8,)),
        ],
        20 * PIECES + 24 * PIECES + 2 * share * (TP + 1) + 2 * TP + 2 * reps * (TP + 2) + 2 * n,
    )


def log_sigmoid(values_in):
    return jnp.minimum(values_in, 0.0) - jnp.log1p(jnp.exp(-jnp.abs(values_in)))


def per_device(
    reps,
    share,
    tokens,
    cotangent,
    pic_start,
    valid_mask,
    gain_attn,
    attn_in,
    forget_w,
    forget_bias,
    attn_out,
    gain_ffn,
    ffn_in,
    ffn_down,
):
    n = TP * share
    _, seq, model = tokens.shape
    held = attn_in.shape[0]
    heads = H // TP
    f = lax.axis_index("fsdp")
    t = f // share

    small = jnp.concatenate([forget_w.T, gain_attn[None], gain_ffn[None]])
    small = jnp.pad(small, ((0, 0), (0, 128 - held)))
    marks = jnp.concatenate(
        [valid_mask.astype(BF16), jnp.broadcast_to(pic_start.astype(BF16)[:, None], (1, seq))]
    )
    small = jnp.concatenate([small, marks, jnp.zeros((32 - H - 4, 128), BF16)])
    bias = lax.dynamic_slice_in_dim(forget_bias, heads * t, heads).astype(F32)
    bias = jnp.pad(bias, (0, ROWS - heads))
    branch_attn, cot, rows_a, proj, sig, att, probability, logit, w_cols, w_rows, w_forget, gains = attention(
        reps, share, tokens[0], cotangent[0], attn_in, small, attn_out, bias[None], bias[:, None]
    )
    valid_col = valid_mask[0].astype(F32)[:, None]
    activations, middle_grad, sums, ffn_in_sum, ffn_down_sum = feed_forward(
        reps, share, tokens[0], branch_attn, gains, valid_col, cot, ffn_in, ffn_down
    )
    input_grad, grad_in, grad_out, gathered = attention_back(
        reps, share, tokens[0], middle_grad, sums, valid_col, rows_a, proj, sig, att, probability, logit, w_cols, w_rows,
        w_forget, gains,
    )

    mine = lax.dynamic_slice_in_dim(gathered, f * held % 128, held, axis=2)
    together = jnp.sum(mine, axis=0)
    grad_forget = mine[:, 2 : 2 + heads].reshape(H, held).T
    bias_total = mine[:, 9 : 9 + heads, 0].reshape(H)
    stats = jnp.sqrt(together[5:8, 0] / (together[8, 0] * model) + EPSILON)

    def over_reps(values_in):
        return jnp.sum(values_in.astype(F32), axis=0)

    hs = ffn_in.shape[2]
    grad_ffn_in = over_reps(ffn_in_sum)
    grad_ffn_in = jnp.stack([grad_ffn_in[:, :hs], grad_ffn_in[:, hs:]])
    return (
        activations[None],
        input_grad[None],
        together[0],
        grad_in,
        grad_forget,
        bias_total,
        grad_out,
        together[1],
        grad_ffn_in,
        over_reps(ffn_down_sum),
        stats,
    )


def solution(mesh):
    placed = (
        P(("rep", "fsdp"), None, None),
        P(("rep", "fsdp"), None, None),
        P(("rep", "fsdp")),
        P(("rep", "fsdp"), None),
        P("fsdp"),
        P("fsdp", None),
        P("fsdp", None),
        P(),
        P("fsdp", None),
        P("fsdp"),
        P(None, None, "fsdp"),
        P("fsdp", None),
    )
    return jax.shard_map(
        functools.partial(per_device, mesh.shape["rep"], mesh.shape["fsdp"] // TP),
        mesh=mesh,
        in_specs=placed,
        out_specs=(
            P(("rep", "fsdp"), None, None),
            P(("rep", "fsdp"), None, None),
            P("fsdp"),
            P("fsdp", None),
            P("fsdp", None),
            P(),
            P("fsdp", None),
            P("fsdp"),
            P(None, None, "fsdp"),
            P("fsdp", None),
            P(),
        ),
        check_vma=False,
    )
```

```python
import functools

import jax
import jax.numpy as jnp
from jax import lax
from jax.experimental import pallas as pl
from jax.experimental.pallas import tpu as pltpu
from jax.sharding import PartitionSpec as P

H = 24
HD = 64
PIC = 32
TP = 8
DEPTH = 4
EPSILON = 1e-06
NEGATIVE = -1e30
MESH = pl.DeviceIdType.MESH
BF16 = jnp.bfloat16
F32 = jnp.float32
VMEM = pl.BlockSpec(memory_space=pltpu.VMEM)
ANY = pl.BlockSpec(memory_space=pl.ANY)


class Net:
    def __init__(self, reps, share, sems):
        self.reps, self.share, self.sems = reps, share, sems
        self.r = lax.axis_index("rep")
        self.f = lax.axis_index("fsdp")
        self.t = lax.div(self.f, share)
        self.u = lax.rem(self.f, share)
        self.z = lax.div(self.t, 2)
        self.x = lax.rem(self.t, 2)
        self.none = self.f * 0
        self.taken = 0
        self.sent = []

    def take(self, count=1):
        base = self.taken
        self.taken += count
        return base

    def place(self, t):
        return t * self.share + self.u

    def grid(self, z, x):
        return (z * 2 + x) * self.share + self.u

    def partners(self):
        for k in range(1, self.share):
            yield k, lax.rem(self.u + k, self.share)

    def greet(self, peers):
        barrier = pltpu.get_barrier_semaphore()
        total = 0
        for cond, r, f in peers:
            if cond is None:
                pl.semaphore_signal(barrier, 1, device_id=(r, f), device_id_type=MESH)
                total = total + 1
            else:

                @pl.when(cond)
                def _():
                    pl.semaphore_signal(barrier, 1, device_id=(r, f), device_id_type=MESH)

                total = total + cond.astype(jnp.int32)
        pl.semaphore_wait(barrier, total)

    def plane_peers(self):
        return [
            (self.z < DEPTH - 1, self.r, self.grid(self.z + 1, self.x)),
            (self.z > 0, self.r, self.grid(self.z - 1, self.x)),
            (None, self.r, self.grid(self.z, 1 - self.x)),
        ]

    def share_peers(self):
        return [(None, self.r, self.t * self.share + u) for _, u in self.partners()]

    def rep_peers(self):
        return [(None, lax.rem(self.r + k, self.reps), self.f) for k in range(1, self.reps)]

    def all_plane_peers(self):
        return [(None, self.r, self.place(lax.rem(self.t + k, TP))) for k in range(1, TP)]

    def copy(self, src, dst, ssem, rsem, f, r=None):
        return pltpu.make_async_remote_copy(
            src_ref=src,
            dst_ref=dst,
            send_sem=self.sems.at[ssem],
            recv_sem=self.sems.at[rsem],
            device_id=(self.r if r is None else r, f),
            device_id_type=MESH,
        )

    def send(self, src, dst, ssem, rsem, f, r=None, cond=None):
        copy = self.copy(src, dst, ssem, rsem, f, r)
        if cond is None:
            copy.start()
        else:
            pl.when(cond)(copy.start)
        self.sent.append((cond, copy))

    def arrive(self, dst, rsem, cond=None):
        copy = pltpu.make_async_remote_copy(
            src_ref=dst,
            dst_ref=dst,
            send_sem=self.sems.at[rsem],
            recv_sem=self.sems.at[rsem],
            device_id=(self.r, self.f),
            device_id_type=MESH,
        )
        if cond is None:
            copy.wait_recv()
        else:
            pl.when(cond)(copy.wait_recv)

    def drain(self):
        for cond, copy in self.sent:
            if cond is None:
                copy.wait_send()
            else:
                pl.when(cond)(copy.wait_send)
        self.sent = []


def nearest(z, k):
    swapped = (1, 0, 2, 3)[k] if isinstance(k, int) else None
    far = lax.div(z, 2)
    edge = z + far * (3 - 2 * z)
    if swapped is None:
        inner = jnp.where(k == 0, 1, jnp.where(k == 1, 0, k))
        place = jnp.where(edge == 0, k, inner)
    else:
        place = k + edge * (swapped - k)
    return far * 3 + (1 - 2 * far) * place


class Wave:
    def __init__(self, net, block):
        self.net, self.block = net, block
        self.recv = net.take(TP)
        self.up, self.down, self.side = net.take(DEPTH), net.take(DEPTH), net.take(DEPTH)

    def copies(self, k):
        net = self.net
        z, x = net.z, net.x
        zo = nearest(z, k)
        t = zo * 2 + x
        block, sem = self.block(t), self.recv + t
        return [
            (
                (zo <= z) & (z < DEPTH - 1),
                net.copy(block, block, self.up + k, sem, net.grid(jnp.minimum(z + 1, DEPTH - 1), x)),
            ),
            (
                (zo >= z) & (z > 0),
                net.copy(block, block, self.down + k, sem, net.grid(jnp.maximum(z - 1, 0), x)),
            ),
            (None, net.copy(block, block, self.side + k, sem, net.grid(z, 1 - x))),
        ]

    def hand_on(self, k, own=False):
        net = self.net
        t = nearest(net.z, k) * 2 + net.x
        if not own:
            net.arrive(self.block(t), self.recv + t, None if isinstance(k, int) else k > 0)
        for cond, copy in self.copies(k):
            if cond is None:
                copy.start()
            else:
                pl.when(cond)(copy.start)

    def across(self, k):
        t = nearest(self.net.z, k) * 2 + 1 - self.net.x
        self.net.arrive(self.block(t), self.recv + t)

    def drain(self):
        @pl.loop(0, DEPTH)
        def _(k):
            for cond, copy in self.copies(k):
                if cond is None:
                    copy.wait_send()
                else:
                    pl.when(cond)(copy.wait_send)


class Gather:
    def __init__(self, net, part, side, up, down, total):
        self.net, self.part, self.side, self.up, self.down, self.total = net, part, side, up, down, total
        self.sems = [net.take(DEPTH) for _ in range(6)]

    def across(self, k):
        net = self.net
        zo = nearest(net.z, k)
        return net.copy(
            self.part(zo * 2 + 1 - net.x), self.side(zo), self.sems[0] + zo, self.sems[1] + zo,
            net.grid(net.z, 1 - net.x),
        )

    def along(self, k):
        net = self.net
        z = net.z
        zo = nearest(z, k)
        part = self.part(zo * 2 + net.x)
        return [
            (
                zo > z,
                net.copy(
                    part, self.up(zo), self.sems[2] + zo, self.sems[3] + zo,
                    net.grid(jnp.minimum(z + 1, DEPTH - 1), net.x),
                ),
            ),
            (
                zo < z,
                net.copy(
                    part, self.down(zo), self.sems[4] + zo, self.sems[5] + zo,
                    net.grid(jnp.maximum(z - 1, 0), net.x),
                ),
            ),
        ]

    def begin(self, k):
        self.across(k).start()

    def step(self, k):
        net = self.net
        z = net.z
        zo = nearest(z, k)
        part = self.part(zo * 2 + net.x)
        net.arrive(self.side(zo), self.sems[1] + zo)
        self.total[...] = part[...].astype(F32) + self.side(zo)[...].astype(F32)
        for cond, ref, sem in (
            ((zo >= z) & (z > 0), self.up(zo), self.sems[3]),
            ((zo <= z) & (z < DEPTH - 1), self.down(zo), self.sems[5]),
        ):

            @pl.when(cond)
            def _():
                net.arrive(ref, sem + zo)
                self.total[...] += ref[...].astype(F32)

        @pl.when(zo != z)
        def _():
            part[...] = self.total[...].astype(BF16)

        for cond, copy in self.along(k):
            pl.when(cond)(copy.start)

    def drain(self):
        @pl.loop(0, DEPTH)
        def _(k):
            self.across(k).wait_send()
            for cond, copy in self.along(k):
                pl.when(cond)(copy.wait_send)


def call(body, name, number, operands, in_specs, outs, scratch, sems, limit=60 << 20):
    return pl.pallas_call(
        body,
        name=name,
        out_shape=tuple(shape for shape, _ in outs),
        in_specs=in_specs,
        out_specs=tuple(spec for _, spec in outs),
        scratch_shapes=list(scratch) + [pltpu.SemaphoreType.DMA((sems,))],
        compiler_params=pltpu.CompilerParams(
            collective_id=number, has_side_effects=True, vmem_limit_bytes=limit
        ),
    )(*operands)


def chunk(rows, count, c):
    return pl.ds(c * (rows // count), rows // count)


def matmul_nt(a, b):
    return lax.dot_general(a, b, (((1,), (1,)), ((), ())), preferred_element_type=F32)


def matmul_tn(a, b):
    return lax.dot_general(a, b, (((0,), (0,)), ((), ())), preferred_element_type=F32)


def matmul(a, b):
    return jnp.dot(a, b, preferred_element_type=F32)


def tile(j, size):
    return pl.ds(pl.multiple_of(j * size, size), size)


PIECES = 2


def feed_forward(reps, share, x, branch, gain, valid, cot, w_in, w_down):
    seq, model = x.shape
    hs = w_in.shape[2]
    hidden_all = share * hs
    rows_all = TP * seq
    pair = 2 * seq
    half = seq // PIECES

    def body(
        x_ref, branch_ref, gain_ref, valid_ref, cot_ref, in_ref, down_ref,
        act_ref, grad_ref, sums_ref, in_out, down_out,
        middle, rows, cot_all, w_all, wd, hid, grads, part, side, up, down, rows_sum, ffn_sum,
        in_part, down_part, in_got, down_got, local, sems,
    ):
        net = Net(reps, share, sems)
        own = [
            pltpu.make_async_copy(in_ref.at[0], w_all.at[:, pl.ds(0, hs)], local.at[0]),
            pltpu.make_async_copy(in_ref.at[1], w_all.at[:, pl.ds(hs, hs)], local.at[1]),
            pltpu.make_async_copy(down_ref, wd.at[pl.ds(0, hs)], local.at[2]),
            pltpu.make_async_copy(cot_ref, cot_all, local.at[3]),
        ]
        for copy in own:
            copy.start()

        def block(ref, t):
            return ref.at[tile(t, seq)]

        middle[...] = x_ref[...].astype(F32) + branch_ref[...]
        scale = lax.rsqrt(jnp.mean(middle[...] * middle[...], axis=-1, keepdims=True) + EPSILON)
        block(rows, net.t)[...] = (middle[...] * scale * gain_ref[1:2]).astype(BF16)
        net.greet(net.plane_peers() + net.share_peers() + net.rep_peers())

        waves = [
            Wave(net, lambda t, c=c: rows.at[pl.ds(pl.multiple_of(t * seq + c * half, half), half)])
            for c in range(PIECES)
        ]
        weights = net.take(3 * share), net.take(3 * share)
        for wave in waves:
            wave.hand_on(0, own=True)
        arriving = []
        for k, u in net.partners():
            f, p = net.t * share + u, share - k
            for j, (src, dst) in enumerate(
                [
                    (in_ref.at[0], w_all.at[:, pl.ds(2 * hs * p, hs)]),
                    (in_ref.at[1], w_all.at[:, pl.ds(2 * hs * p + hs, hs)]),
                    (down_ref, wd.at[pl.ds(hs * p, hs)]),
                ]
            ):
                net.send(src, dst, weights[0] + 3 * k + j, weights[1] + 3 * p + j, f)
                arriving.append((dst, weights[1] + 3 * p + j))

        def unit(k):
            at = tile(nearest(net.z, k), pair)
            projected = matmul(rows[at], w_all[...])
            hidden_grad = matmul_nt(cot_all[at], wd[...])
            for p in range(share):
                gate = projected[:, 2 * hs * p : 2 * hs * p + hs]
                lift = projected[:, 2 * hs * p + hs : 2 * hs * (p + 1)]
                back = hidden_grad[:, hs * p : hs * (p + 1)]
                sig = jax.nn.sigmoid(gate)
                silu = gate * sig
                hid[at, hs * p : hs * (p + 1)] = (silu * lift).astype(BF16)
                grads[at, 2 * hs * p : 2 * hs * p + hs] = (
                    back * lift * sig * (1.0 + gate * (1.0 - sig))
                ).astype(BF16)
                grads[at, 2 * hs * p + hs : 2 * hs * (p + 1)] = (back * silu).astype(BF16)

            @pl.loop(0, 3)
            def _(j):
                to = tile(j, model // 3)
                part[0, at, to] = matmul_nt(grads[at], w_all[to]).astype(BF16)
                part[1, at, to] = matmul(hid[at], wd[:, to]).astype(BF16)

        def piece(ref, i, c, count):
            return lambda j: ref.at[i, pl.ds(pl.multiple_of(j * seq + c * half, half), half)]

        gathers = [
            [
                Gather(
                    net, piece(part, i, c, TP), piece(side, i, c, DEPTH), piece(up, i, c, DEPTH),
                    piece(down, i, c, DEPTH), total.at[pl.ds(c * half, half)],
                )
                for c in range(PIECES)
            ]
            for i, total in enumerate((rows_sum, ffn_sum))
        ]
        @pl.loop(1, DEPTH + 1)
        def _(k):
            @pl.when(k < DEPTH)
            def _():
                for wave in waves:
                    wave.hand_on(k)

            @pl.when(k == 1)
            def _():
                for copy in own:
                    copy.wait()
                for dst, sem in arriving:
                    net.arrive(dst, sem)

            for wave in waves:
                wave.across(k - 1)

            @pl.when(k == DEPTH)
            def _():
                for gather in gathers[0]:
                    gather.begin(DEPTH - 2)

            unit(k - 1)

        for k in (DEPTH - 1, *range(DEPTH - 3, -1, -1)):
            for gather in gathers[0]:
                gather.begin(k)
        for k in range(DEPTH - 1, -1, -1):
            for gather in gathers[1]:
                gather.begin(k)

        @pl.loop(0, model // 256)
        def _(j):
            at = tile(j, 256)
            in_part[at] = matmul_tn(rows[:, at], grads[...]).astype(BF16)

        @pl.loop(0, 3)
        def _(j):
            at = tile(j, model // 3)
            down_part[:, at] = matmul_tn(hid[...], cot_all[:, at]).astype(BF16)

        first, arrived = net.take(2 * share), net.take(2 * share)
        away, back = net.take(2 * reps), net.take(2 * reps)
        for k, u in net.partners():
            f, slot = net.t * share + u, share - 1 - k
            net.send(
                in_part.at[:, pl.ds(2 * hs * k, 2 * hs)], in_got.at[slot], first + 2 * k, arrived + 2 * slot, f
            )
            net.send(
                down_part.at[pl.ds(hs * k, hs)], down_got.at[slot], first + 2 * k + 1, arrived + 2 * slot + 1, f
            )

        def own_grads():
            for slot in range(share - 1):
                net.arrive(in_got.at[slot], arrived + 2 * slot)
                net.arrive(down_got.at[slot], arrived + 2 * slot + 1)

            @pl.loop(0, model // 256)
            def _(j):
                at = tile(j, 256)
                total = in_part[at, : 2 * hs].astype(F32)
                for slot in range(share - 1):
                    total = total + in_got[slot, at].astype(F32)
                in_out[net.r, at] = total.astype(BF16)

            total = down_part[:hs].astype(F32)
            for slot in range(share - 1):
                total = total + down_got[slot].astype(F32)
            down_out[net.r] = total.astype(BF16)
            for k in range(1, reps):
                r = lax.rem(net.r + k, reps)
                net.send(in_out.at[net.r], in_out.at[net.r], away + 2 * k, back + 2 * net.r, net.f, r=r)
                net.send(down_out.at[net.r], down_out.at[net.r], away + 2 * k + 1, back + 2 * net.r + 1, net.f, r=r)

        def steps(both, start, stop):
            @pl.loop(start, stop)
            def _(j):
                for gather in both:
                    gather.step(DEPTH - 1 - j)

        steps(gathers[0], 0, 2)
        own_grads()
        steps(gathers[0], 2, DEPTH)
        steps(gathers[1], 0, DEPTH)

        result = middle[...] + ffn_sum[...]
        act_ref[...] = result.astype(BF16)
        valid_col = valid_ref[...]
        scale = lax.rsqrt(jnp.mean(middle[...] * middle[...], axis=-1, keepdims=True) + EPSILON)
        lifted = rows_sum[...] * gain_ref[1:2]
        mean = jnp.mean(middle[...] * lifted, axis=-1, keepdims=True)
        grad_ref[...] = (
            block(cot_all, net.t)[...].astype(F32) + scale * lifted - middle[...] * (scale * scale * scale) * mean
        )
        sums_ref[...] = jnp.zeros_like(sums_ref)
        sums_ref[0:1] = jnp.sum(rows_sum[...] * middle[...] * scale, axis=0, keepdims=True)
        sums_ref[1:2] = jnp.sum(result * result * valid_col, axis=0, keepdims=True)
        sums_ref[2:3] = jnp.sum(branch_ref[...] * branch_ref[...] * valid_col, axis=0, keepdims=True)
        sums_ref[3:4] = jnp.sum(ffn_sum[...] * ffn_sum[...] * valid_col, axis=0, keepdims=True)
        for k in range(1, reps):
            r = lax.rem(net.r + k, reps)
            net.arrive(in_out.at[r], back + 2 * r)
            net.arrive(down_out.at[r], back + 2 * r + 1)
        net.drain()
        for wave in waves:
            wave.drain()
        for gather in gathers[0] + gathers[1]:
            gather.drain()

    shape = jax.ShapeDtypeStruct
    line = pltpu.VMEM((2, DEPTH * seq, model), BF16)
    return call(
        body, "feed_forward", 3, (x, branch, gain, valid, cot, w_in, w_down), [VMEM] * 4 + [ANY] * 3,
        [
            (shape((seq, model), BF16), VMEM),
            (shape((seq, model), F32), VMEM),
            (shape((8, model), F32), VMEM),
            (shape((reps, model, 2 * hs), BF16), VMEM),
            (shape((reps, hs, model), BF16), VMEM),
        ],
        [
            pltpu.VMEM((seq, model), F32),
            pltpu.VMEM((rows_all, model), BF16),
            pltpu.VMEM((rows_all, model), BF16),
            pltpu.VMEM((model, 2 * hidden_all), BF16),
            pltpu.VMEM((hidden_all, model), BF16),
            pltpu.VMEM((rows_all, hidden_all), BF16),
            pltpu.VMEM((rows_all, 2 * hidden_all), BF16),
            pltpu.VMEM((2, rows_all, model), BF16),
            line, line, line,
            pltpu.VMEM((seq, model), F32),
            pltpu.VMEM((seq, model), F32),
            pltpu.VMEM((model, 2 * hidden_all), BF16),
            pltpu.VMEM((hidden_all, model), BF16),
            pltpu.VMEM((share - 1, model, 2 * hs), BF16),
            pltpu.VMEM((share - 1, hs, model), BF16),
            pltpu.SemaphoreType.DMA((4,)),
        ],
        40 * PIECES + 24 * 2 * PIECES + 20 * share + 10 * reps,
    )


HEADS = H // TP
ROWS = 16


def cuts(reps, held):
    return reps if held % (16 * reps) == 0 else 1


def lane_mask(shape, low, high):
    lane = lax.broadcasted_iota(jnp.int32, shape, 1)
    return (lane >= low) & (lane < high)


def head_pieces(t, block):
    base = block * H * HD + t * HEADS * HD
    return [(base, 2 * HD, block * 2 * HD), (base + 2 * HD, HD, 8 * HD + block * HD)]


def attention(reps, share, x, cot, w_in, small, w_out, bias_row, bias_col):
    n = TP * share
    seq, model = x.shape
    held = w_in.shape[0]
    width = 4 * HEADS * HD
    rows_all = TP * seq
    pair = 2 * seq
    half = seq // PIECES
    last = HEADS - 1
    cut = cuts(reps, held)

    def body(
        x_ref, cot_ref, in_ref, small_ref, out_ref, bias_row_ref, bias_col_ref,
        branch_ref, cot_out, rows_out, proj_out, sig_out, att_out, prob_out, logit_ref, wc_out, wo_out, wf_ref, gains_ref,
        xs, cots, rows, proj, sig, att, prob, wc, wo, split, smalls, lines, part, side, up, down, gated, local, sems,
    ):
        net = Net(reps, share, sems)

        def seq_block(ref, t):
            return ref.at[tile(t, seq)]

        def held_rows(f):
            return wc.at[tile(f, held)]

        def spot(r):
            return r if cut > 1 else 0

        def piece_of(r):
            return tile(spot(r), held // cut)

        def held_piece(f, r):
            return wc.at[pl.ds(pl.multiple_of(f * held + spot(r) * (held // cut), held // cut), held // cut)]

        own = [
            pltpu.make_async_copy(x_ref, seq_block(xs, net.t), local.at[0]),
            pltpu.make_async_copy(cot_ref, seq_block(cots, net.t), local.at[1]),
            pltpu.make_async_copy(small_ref, smalls.at[net.f], local.at[2]),
            pltpu.make_async_copy(out_ref, wo.at[tile(net.u, held)], local.at[3]),
        ]
        for copy in own:
            copy.start()
        for t in range(TP):
            for block in range(4):
                for column, wide, to in head_pieces(t, block):
                    split[t, :, to : to + wide] = in_ref[:, column : column + wide]
        wo[share * held :] = jnp.zeros((wo.shape[0] - share * held, model), BF16)
        others = [lax.rem(net.f + k, n) for k in range(n)]
        chips = [lax.rem(net.t + k, TP) for k in range(TP)]
        partners = list(net.partners())
        replicas = [lax.rem(net.r + k, reps) for k in range(reps)]
        net.greet([(None, net.r, f) for f in others[1:]] + [(None, r, net.f) for r in replicas[1:cut]])

        small_send, small_recv = net.take(n), net.take(n)
        w_send, w_recv = net.take(TP), net.take(n * cut)
        w_pass = net.take(share * TP * (cut + 1))
        w_away = net.take(TP * cut)
        wo_send, wo_recv = net.take(share), net.take(share)
        for k in range(1, n):
            net.send(small_ref, smalls.at[net.f], small_send + k, small_recv + net.f, others[k])
        for k in range(1, TP):
            net.send(
                split.at[chips[k], piece_of(net.r)], held_piece(net.f, net.r), w_send + k, w_recv + cut * net.f + spot(net.r),
                net.place(chips[k]),
            )
        own_cols = pltpu.make_async_copy(split.at[net.t], held_rows(net.f), local.at[4])
        own_cols.start()
        for k, u in partners:
            f = net.t * share + u
            net.send(split.at[net.t], held_rows(net.f), w_pass + k, w_recv + cut * net.f, f)
            net.send(out_ref, wo.at[tile(net.u, held)], wo_send + k, wo_recv + net.u, f)

        def pieces(ref):
            return [
                Wave(net, lambda t, c=c: ref.at[pl.ds(pl.multiple_of(t * seq + c * half, half), half)])
                for c in range(PIECES)
            ]

        waves, cot_waves = pieces(xs), pieces(cots)
        for copy in own:
            copy.wait()
        for wave in waves:
            wave.hand_on(0, own=True)
        for wave in cot_waves:
            wave.copies(0)[2][1].start()

        def weights():
            for q in range(cut):
                r = replicas[q]
                for k in range(1, TP):
                    source = net.place(chips[k])
                    got, sem = held_piece(source, r), w_recv + cut * source + spot(r)
                    net.arrive(got, sem)
                    for j, u in partners:
                        net.send(got, got, w_pass + share * (TP * (q + 1) + k) + j, sem, net.t * share + u)
                    for p in range(1, cut if q == 0 else 1):
                        net.send(got, got, w_away + TP * p + k, sem, net.f, r=replicas[p])
            for k in range(1, n):
                net.arrive(smalls.at[others[k]], small_recv + others[k])
            for j in range(model // 128):
                line = jnp.zeros((32, 128), F32)
                for f in range(j * 128 // held, ((j + 1) * 128 - 1) // held + 1):
                    start = f * held - j * 128
                    piece = pltpu.roll(smalls[f].astype(F32), net.none + start % 128, 1)
                    line = jnp.where(lane_mask((32, 128), start, start + held), piece, line)
                lines[:, j * 128 : (j + 1) * 128] = line
            pick = lax.broadcasted_iota(jnp.int32, (ROWS, 32), 0) + HEADS * net.t
            pick = pick == lax.broadcasted_iota(jnp.int32, (ROWS, 32), 1)
            pick &= lax.broadcasted_iota(jnp.int32, (ROWS, 32), 0) < HEADS
            wf_ref[...] = matmul(pick.astype(BF16), lines[...].astype(BF16)).astype(BF16)
            gains_ref[...] = lines[H : H + 8]
            for k, u in partners:
                net.arrive(wo.at[tile(u, held)], wo_recv + u)
                net.arrive(held_rows(net.t * share + u), w_recv + cut * (net.t * share + u))
                for k in range(1, TP):
                    f = chips[k] * share + u
                    for r in replicas[:cut]:
                        net.arrive(held_piece(f, r), w_recv + cut * f + spot(r))
            own_cols.wait()

        square = (seq, seq)
        at_row = lax.broadcasted_iota(jnp.int32, square, 0)
        at_col = lax.broadcasted_iota(jnp.int32, square, 1)

        def unit(k):
            place = nearest(net.z, k)
            at = tile(place, pair)
            values_in = xs[at].astype(F32)
            inverse = lax.rsqrt(jnp.mean(values_in * values_in, axis=-1, keepdims=True) + EPSILON)
            rows[at] = (values_in * inverse * gains_ref[0:1]).astype(BF16)
            projected = matmul(rows[at], wc[...])
            proj[at] = projected.astype(BF16)
            sig[at, : 2 * HD] = jax.nn.sigmoid(projected[:, 6 * HD : 8 * HD])
            tail = pltpu.roll(jax.nn.sigmoid(projected[:, 10 * HD : 12 * HD]), net.none + HD, 1)
            sig[at, 2 * HD :] = jnp.where(lane_mask(tail.shape, 0, HD), tail, 0.0)

            @pl.loop(0, 2, unroll=True)
            def _(j):
                t = place * 2 + j
                here = tile(t, seq)
                marks = smalls[net.place(t)].astype(F32)
                valid = marks[H + 2 : H + 3]
                start = marks[H + 3 : H + 4].astype(jnp.int32)
                causal = at_col <= at_row
                inside = (at_row >= start) & (at_row < start + PIC) & (at_col >= start) & (at_col < start + PIC)
                allowed = (causal | inside) & (valid > 0.0)
                sign = jnp.where(causal, 1.0, -1.0)
                below = sign * 0.5 + 0.5
                logit_col = matmul_nt(rows[here], wf_ref[...]) + bias_row_ref[...]
                logit_row = matmul_nt(wf_ref[...], rows[here]) + bias_col_ref[...]
                logit_ref[t] = logit_row
                decay_col = jnp.dot(
                    below, log_sigmoid(logit_col), precision=lax.Precision.HIGHEST, preferred_element_type=F32
                )
                decay_row = lax.dot_general(
                    log_sigmoid(logit_row), below, (((1,), (1,)), ((), ())),
                    precision=lax.Precision.HIGHEST, preferred_element_type=F32,
                )
                outs = []
                for h in range(HEADS):
                    if h < last:
                        query = jnp.where(lane_mask((seq, 2 * HD), h * HD, h * HD + HD), proj[here, : 2 * HD], 0)
                        key, value = proj[here, 2 * HD : 4 * HD], proj[here, 4 * HD : 6 * HD]
                    else:
                        query = jnp.where(lane_mask((seq, 2 * HD), 0, HD), proj[here, 8 * HD : 10 * HD], 0)
                        key = pltpu.roll(proj[here, 8 * HD : 10 * HD].astype(F32), net.none + HD, 1).astype(BF16)
                        value = proj[here, 10 * HD :]
                    scores = matmul_nt(query, key) * HD ** (-0.5)
                    scores = scores + sign * (decay_col[:, h : h + 1] - decay_row[h : h + 1])
                    masked = jnp.where(allowed, scores, NEGATIVE)
                    weights_now = jnp.exp(masked - jnp.max(masked, axis=-1, keepdims=True))
                    probability = weights_now / jnp.sum(weights_now, axis=-1, keepdims=True)
                    prob[t * HEADS + h] = probability
                    outs.append(matmul(probability.astype(BF16), value))
                low = lane_mask((seq, 2 * HD), 0, HD)
                att[here, : 2 * HD] = jnp.where(low, outs[0], outs[1])
                att[here, 2 * HD :] = jnp.where(low, outs[2], 0.0)

            gated[...] = (att[at] * sig[at]).astype(BF16)

            @pl.loop(0, 3)
            def _(j):
                to = tile(j, model // 3)
                part[at, to] = matmul(gated[...], wo[:, to]).astype(BF16)

        gathers = [
            Gather(
                net,
                *[
                    lambda j, ref=ref, c=c: ref.at[pl.ds(pl.multiple_of(j * seq + c * half, half), half)]
                    for ref in (part, side, up, down)
                ],
                branch_ref.at[pl.ds(c * half, half)],
            )
            for c in range(PIECES)
        ]

        for wave in waves:
            wave.hand_on(1)
        weights()

        @pl.loop(1, DEPTH + 1)
        def _(k):
            @pl.when((k > 1) & (k < DEPTH))
            def _():
                for wave in waves:
                    wave.hand_on(k)

            @pl.when(k == DEPTH - 1)
            def _():
                for wave in cot_waves:
                    for cond, copy in wave.copies(0)[:2]:
                        pl.when(cond)(copy.start)

            for wave in waves:
                wave.across(k - 1)

            @pl.when(k == DEPTH)
            def _():
                for gather in gathers:
                    gather.begin(DEPTH - 2)

            unit(k - 1)

        keep = [
            pltpu.make_async_copy(src, dst, local.at[5 + i])
            for i, (src, dst) in enumerate(
                [
                    (rows, rows_out), (proj, proj_out), (sig, sig_out), (att, att_out), (prob, prob_out),
                    (wc, wc_out), (wo, wo_out),
                ]
            )
        ]
        for k in (DEPTH - 1, *range(DEPTH - 3, -1, -1)):
            for gather in gathers:
                gather.begin(k)

        for copy in keep:
            copy.start()

        @pl.loop(0, DEPTH)
        def _(j):
            for gather in gathers:
                gather.step(DEPTH - 1 - j)

            @pl.when(j < DEPTH - 1)
            def _():
                for wave in cot_waves:
                    wave.hand_on(j + 1)

        for k in range(DEPTH):
            for wave in cot_waves:
                wave.across(k)
        save = pltpu.make_async_copy(cots, cot_out, local.at[1])
        save.start()
        net.drain()
        for wave in waves + cot_waves:
            wave.drain()
        for gather in gathers:
            gather.drain()
        for copy in keep:
            copy.wait()
        save.wait()

    shape = jax.ShapeDtypeStruct
    line = pltpu.VMEM((DEPTH * seq, model), BF16)
    kept = [
        ((rows_all, model), BF16),
        ((rows_all, model), BF16),
        ((rows_all, width), BF16),
        ((rows_all, 4 * HD), F32),
        ((rows_all, 4 * HD), F32),
        ((TP * HEADS, seq, seq), F32),
    ]
    return call(
        body, "attention", 1, (x, cot, w_in, small, w_out, bias_row, bias_col),
        [ANY, ANY, VMEM, VMEM, ANY, VMEM, VMEM],
        [(shape((seq, model), F32), VMEM)]
        + [(shape(*what), ANY) for what in kept]
        + [
            (shape((TP, ROWS, seq), F32), VMEM),
            (shape((model, width), BF16), ANY),
            (shape((4 * HD, model), BF16), ANY),
            (shape((ROWS, model), BF16), VMEM),
            (shape((8, model), F32), VMEM),
        ],
        [pltpu.VMEM((rows_all, model), BF16)]
        + [pltpu.VMEM(*what) for what in kept]
        + [
            pltpu.VMEM((model, width), BF16),
            pltpu.VMEM((4 * HD, model), BF16),
            pltpu.VMEM((TP, held, width), BF16),
            pltpu.VMEM((n, 32, 128), BF16),
            pltpu.VMEM((32, model), F32),
            pltpu.VMEM((rows_all, model), BF16),
            line, line, line,
            pltpu.VMEM((pair, 4 * HD), BF16),
            pltpu.SemaphoreType.DMA((12,)),
        ],
        2 * 20 * PIECES + 24 * PIECES + (2 + cut) * n + (1 + cut) * (TP + share * TP) + 2 * share,
    )


def attention_back(
    reps, share, x, middle_grad, sums, valid, rows_a, proj, sig, att, prob, logit, wc, wo, wf, gains
):
    n = TP * share
    seq, model = x.shape
    width = 4 * HEADS * HD
    held = model // n
    rows_all = TP * seq
    pair = 2 * seq
    half = seq // PIECES
    last = HEADS - 1
    window = 256
    cut = cuts(reps, held)
    bit = held // cut
    sheets = 1 if cut > 1 else reps

    def body(
        x_ref, grad_ref, sums_ref, valid_ref, rows_in, proj_in, sig_in, att_in, prob_in, logit_ref, wc_in, wo_in, wf_ref,
        gains_ref, input_ref, in_ref, out_ref, gains_out, forget_ref, bias_ref, stats_ref,
        rows, proj, sig, att, prob, wcs, wos, bgs, pg, gated, part, side, up, down, rows_sum, ag, og, low_logit, bias_sum,
        forget_sum, lines, late, in_part, in_got, swapped_in, in_all, out_part, out_got, out_all, small_got, first_got,
        small_mid, local, sems,
    ):
        net = Net(reps, share, sems)
        others = [lax.rem(net.f + k, n) for k in range(n)]
        chips = [lax.rem(net.t + k, TP) for k in range(TP)]
        partners = list(net.partners())
        own = [
            pltpu.make_async_copy(src, dst, local.at[i])
            for i, (src, dst) in enumerate(
                [
                    (wo_in, wos), (sig_in, sig), (att_in, att), (proj_in, proj), (prob_in, prob), (rows_in, rows),
                    (wc_in, wcs),
                ]
            )
        ]
        for copy in own:
            copy.start()
        bgs[tile(net.t, seq)] = grad_ref[...].astype(BF16)
        net.greet([(None, net.r, f) for f in others[1:]] + net.rep_peers())
        waves = [
            Wave(net, lambda t, c=c: bgs.at[pl.ds(pl.multiple_of(t * seq + c * half, half), half)])
            for c in range(PIECES)
        ]
        for wave in waves:
            wave.hand_on(0, own=True)
        bias_sum[...] = jnp.zeros_like(bias_sum)
        forget_sum[...] = jnp.zeros_like(forget_sum)
        for copy in own:
            copy.wait()

        square = (seq, seq)
        causal = lax.broadcasted_iota(jnp.int32, square, 1) <= lax.broadcasted_iota(jnp.int32, square, 0)
        below = jnp.where(causal, 1.0, 0.0)
        low = lane_mask((seq, 2 * HD), 0, HD)
        head_row = lax.broadcasted_iota(jnp.int32, (ROWS, seq), 0)

        def unit(k):
            place = nearest(net.z, k)
            at = tile(place, pair)
            gated_grad = matmul_nt(bgs[at], wos[...])
            gate, attended = sig[at], att[at]
            ag[...] = (gated_grad * gate).astype(BF16)
            gated[at] = (attended * gate).astype(BF16)
            gate_grad = gated_grad * attended * (gate * (1.0 - gate))
            pg[at, 6 * HD : 8 * HD] = gate_grad[:, : 2 * HD].astype(BF16)
            og[...] = pltpu.roll(gate_grad[:, 2 * HD :], net.none + HD, 1)

            @pl.loop(0, 2, unroll=True)
            def _(j):
                t = place * 2 + j
                here = tile(t, seq)
                inner = tile(j, seq)
                swapped = pltpu.roll(proj[here, 8 * HD : 10 * HD].astype(F32), net.none + HD, 1).astype(BF16)
                decay_grad = jnp.zeros((ROWS, seq), F32)
                found = []
                for h in range(HEADS):
                    probability = prob[t * HEADS + h]
                    if h < last:
                        back_all = ag[inner, : 2 * HD]
                        back = jnp.where(lane_mask((seq, 2 * HD), h * HD, h * HD + HD), back_all, 0)
                        query, key, value = (proj[here, 2 * HD * i : 2 * HD * (i + 1)] for i in range(3))
                    else:
                        back = back_all = ag[inner, 2 * HD :]
                        query, key, value = swapped, swapped, proj[here, 10 * HD :]
                    prob_grad = matmul_nt(back, value)
                    score_grad = probability * (
                        prob_grad - jnp.sum(probability * prob_grad, axis=-1, keepdims=True)
                    )
                    dotted_grad = (score_grad * HD ** (-0.5)).astype(BF16)
                    found.append(
                        (
                            matmul(dotted_grad, key),
                            matmul_tn(dotted_grad, query),
                            matmul_tn(probability.astype(BF16), back_all),
                        )
                    )
                    signed = jnp.where(causal, score_grad, -score_grad)
                    line = jnp.sum(signed.T - signed, axis=0, keepdims=True)
                    decay_grad = jnp.where(head_row == h, line, decay_grad)
                for i in range(3):
                    pg[here, 2 * HD * i : 2 * HD * (i + 1)] = jnp.where(low, found[0][i], found[1][i]).astype(BF16)
                pg[here, 8 * HD : 10 * HD] = jnp.where(low, found[2][0], found[2][1]).astype(BF16)
                pg[here, 10 * HD :] = jnp.where(low, found[2][2], og[inner]).astype(BF16)
                later = jnp.dot(decay_grad, below, precision=lax.Precision.HIGHEST, preferred_element_type=F32)
                logit_grad = later * jax.nn.sigmoid(-logit_ref[t])
                bias_sum[...] += logit_grad
                low_logit[j] = logit_grad.astype(BF16)
                forget_sum[...] += matmul(logit_grad.astype(BF16), rows[here])

            @pl.loop(0, 3)
            def _(i):
                to = tile(i, model // 3)
                main = matmul_nt(pg[at], wcs[to])
                for j in range(2):
                    extra = matmul_tn(low_logit[j], wf_ref[:, to])
                    part[tile(place * 2 + j, seq), to] = (main[j * seq : (j + 1) * seq] + extra).astype(BF16)

        gathers = [
            Gather(
                net,
                *[
                    lambda j, ref=ref, c=c: ref.at[pl.ds(pl.multiple_of(j * seq + c * half, half), half)]
                    for ref in (part, side, up, down)
                ],
                rows_sum.at[pl.ds(c * half, half)],
            )
            for c in range(PIECES)
        ]

        @pl.loop(1, DEPTH + 1)
        def _(k):
            @pl.when(k < DEPTH)
            def _():
                for wave in waves:
                    wave.hand_on(k)

            for wave in waves:
                wave.across(k - 1)

            @pl.when(k == DEPTH)
            def _():
                for gather in gathers:
                    gather.begin(DEPTH - 2)

            unit(k - 1)

        for k in (DEPTH - 1, *range(DEPTH - 3, -1, -1)):
            for gather in gathers:
                gather.begin(k)

        @pl.loop(0, model // 256)
        def _(j):
            at = tile(j, 256)
            in_part[at] = matmul_tn(rows[:, at], pg[...]).astype(BF16)

        @pl.loop(0, 3)
        def _(j):
            at = tile(j, model // 3)
            out_part[:, at] = matmul_tn(gated[...], bgs[:, at]).astype(BF16)

        def owned(t, u):
            return tile(t * share + u, held)

        def seen(f):
            start = jnp.minimum(lax.div(f * held, 128) * 128, model - window)
            return pl.ds(pl.multiple_of(start, 128), window)

        small_send, small_recv = net.take(n), net.take(n)
        lines[...] = jnp.zeros_like(lines)
        lines[0:1] = sums_ref[0:1]
        lines[1 : 1 + HEADS] = forget_sum[:HEADS]
        for i in range(3):
            lines[4 + i : 5 + i] = jnp.broadcast_to(jnp.sum(sums_ref[1 + i : 2 + i], axis=1, keepdims=True), (1, model))
        lines[7:8] = jnp.broadcast_to(jnp.sum(valid_ref[...], axis=0, keepdims=True), (1, model))
        lines[8 : 8 + HEADS] = jnp.broadcast_to(jnp.sum(bias_sum[:HEADS], axis=1, keepdims=True), (HEADS, model))
        small_got[net.f] = lines[:, seen(net.f)]
        for k in range(1, n):
            net.send(
                lines.at[:, seen(others[k])], small_got.at[net.f], small_send + k, small_recv + net.f, others[k]
            )

        in_send, in_recv = net.take(share * TP), net.take(share * TP)
        out_send, out_recv = net.take(share), net.take(share)
        over, landed = net.take(TP), net.take(TP)
        away, back_in = net.take(TP * reps), net.take(TP * reps)
        out_away, out_back = net.take(reps), net.take(reps)
        first_send, first_recv = net.take(n), net.take(n)
        mid_send, mid_recv = net.take(reps), net.take(reps)
        swap_send, swap_recv = net.take(TP * reps), net.take(TP * reps)
        for k, u in partners:
            slot, f = share - 1 - k, net.t * share + u
            for j in range(TP):
                t = chips[(j + 1) % TP]
                net.send(
                    in_part.at[owned(t, u)], in_got.at[slot, t], in_send + share * j + k, in_recv + share * t + slot, f
                )
            net.send(out_part.at[tile(u, held)], out_got.at[slot], out_send + k, out_recv + slot, f)

        replicas = [lax.rem(net.r + k, reps) for k in range(reps)]

        def owned_bit(t, r):
            start = (t * share + net.u) * held + (r * bit if cut > 1 else 0)
            return pl.ds(pl.multiple_of(start, bit), bit)

        def piece(r, t):
            return in_all.at[0, t, tile(r, bit)] if cut > 1 else in_all.at[r, t]

        def steps(start, stop):
            @pl.loop(start, stop)
            def _(j):
                for gather in gathers:
                    gather.step(DEPTH - 1 - j)

        steps(0, 1)
        for j in range(TP):
            t = chips[(j + 1) % TP]
            total = in_part[owned(t, net.u)].astype(F32)
            for slot in range(share - 1):
                net.arrive(in_got.at[slot, t], in_recv + share * t + slot)
                total = total + in_got[slot, t].astype(F32)
            in_part[owned(t, net.u)] = total.astype(BF16)
            if cut > 1:
                for k in range(1, reps):
                    net.send(
                        in_part.at[owned_bit(t, replicas[k])], swapped_in.at[net.r, t], swap_send + TP * k + j,
                        swap_recv + TP * net.r + t, net.f, r=replicas[k],
                    )
        total = out_part[tile(net.u, held)].astype(F32)
        for slot in range(share - 1):
            net.arrive(out_got.at[slot], out_recv + slot)
            total = total + out_got[slot].astype(F32)
        out_all[net.r] = total.astype(BF16)
        steps(1, 2)
        for j in range(TP):
            t = chips[(j + 1) % TP]
            here = owned_bit(t, net.r)
            if cut > 1:
                total = in_part[here].astype(F32)
                for k in range(1, reps):
                    net.arrive(swapped_in.at[replicas[k], t], swap_recv + TP * replicas[k] + t)
                    total = total + swapped_in[replicas[k], t].astype(F32)
                in_part[here] = total.astype(BF16)
            if j < TP - 1:
                net.send(in_part.at[here], piece(net.r, net.t), over + j, landed + net.t, net.place(t))
            else:
                piece(net.r, net.t)[...] = in_part[here]
        for k in range(1, reps):
            net.send(
                out_all.at[net.r], out_all.at[net.r], out_away + k, out_back + net.r, net.f, r=replicas[k]
            )
            net.send(
                piece(net.r, net.t), piece(net.r, net.t), away + k, back_in + TP * net.r + net.t, net.f, r=replicas[k]
            )
        steps(2, DEPTH)

        layer_in = x_ref[...].astype(F32)
        scale = lax.rsqrt(jnp.mean(layer_in * layer_in, axis=-1, keepdims=True) + EPSILON)
        lifted = rows_sum[...] * gains_ref[0:1]
        mean = jnp.mean(layer_in * lifted, axis=-1, keepdims=True)
        input_ref[...] = grad_ref[...] + scale * lifted - layer_in * (scale * scale * scale) * mean
        late[...] = jnp.broadcast_to(
            jnp.sum(rows_sum[...] * layer_in * scale, axis=0, keepdims=True), (8, model)
        )
        first_got[net.f] = late[:, seen(net.f)]
        for k in range(1, n):
            net.send(
                late.at[:, seen(others[k])], first_got.at[net.f], first_send + k, first_recv + net.f, others[k]
            )
        for j in range(1, TP):
            t = chips[TP - j]
            net.arrive(piece(net.r, t), landed + t)
            for k in range(1, reps):
                net.send(
                    piece(net.r, t), piece(net.r, t), away + reps * j + k, back_in + TP * net.r + t, net.f, r=replicas[k]
                )
        for k in range(1, n):
            net.arrive(small_got.at[others[k]], small_recv + others[k])
        for t in range(TP):
            total = small_got[t * share]
            for u in range(1, share):
                total = total + small_got[t * share + u]
            small_mid[net.r, t, :ROWS] = total
        for k in range(1, n):
            net.arrive(first_got.at[others[k]], first_recv + others[k])
        for t in range(TP):
            total = first_got[t * share]
            for u in range(1, share):
                total = total + first_got[t * share + u]
            small_mid[net.r, t, ROWS:] = total
        for k in range(1, reps):
            net.send(
                small_mid.at[net.r], small_mid.at[net.r], mid_send + k, mid_recv + net.r, net.f, r=replicas[k]
            )
        for k in range(1, reps):
            r = replicas[k]
            net.arrive(out_all.at[r], out_back + r)
            for t in range(TP):
                net.arrive(piece(r, t), back_in + TP * r + t)
        for t in range(TP):
            for block in range(4):
                for column, wide, to in head_pieces(t, block):
                    total = in_all[0, t, :, to : to + wide].astype(F32)
                    for r in range(1, sheets):
                        total = total + in_all[r, t, :, to : to + wide].astype(F32)
                    in_ref[:, column : column + wide] = total
        for r in replicas[1:]:
            net.arrive(small_mid.at[r], mid_recv + r)
        total, small = out_all[0].astype(F32), small_mid[0]
        for r in range(1, reps):
            total = total + out_all[r].astype(F32)
            small = small + small_mid[r]
        out_ref[...] = total
        together = jnp.sum(small, axis=0)
        turn = lax.rem(2 * window - (net.f * held - jnp.minimum(lax.div(net.f * held, 128) * 128, model - window)), window)
        gain_rows = pltpu.roll(together, turn, 1)
        gains_out[0:1] = gain_rows[ROWS : ROWS + 1, :held]
        gains_out[1:2] = gain_rows[0:1, :held]
        mean_squares = together[4:7, :128] / (together[7:8, :128] * model)
        stats_ref[...] = jnp.sqrt(mean_squares + EPSILON)
        forget = jnp.zeros((128, 128), F32)
        biases = jnp.zeros((1, 128), F32)
        lane = lax.broadcasted_iota(jnp.int32, (1, 128), 1)
        for t in range(TP):
            turned = pltpu.roll(small[t], turn, 1)[:, :128]
            for h in range(HEADS):
                row = HEADS * t + h
                forget = jnp.where(
                    lax.broadcasted_iota(jnp.int32, (128, 128), 0) == row, turned[1 + h : 2 + h], forget
                )
                biases = jnp.where(lane == row, small[t, 8 + h : 9 + h, :128], biases)
        forget_ref[...] = forget.T[:held, :H]
        bias_ref[...] = biases[:, :H]
        net.drain()
        for wave in waves:
            wave.drain()
        for gather in gathers:
            gather.drain()

    shape = jax.ShapeDtypeStruct
    line = pltpu.VMEM((DEPTH * seq, model), BF16)
    return call(
        body, "attention_back", 5,
        (x, middle_grad, sums, valid, rows_a, proj, sig, att, prob, logit, wc, wo, wf, gains),
        [VMEM] * 4 + [ANY] * 5 + [VMEM, ANY, ANY, VMEM, VMEM],
        [
            (shape((seq, model), F32), VMEM),
            (shape((held, 4 * model), F32), VMEM),
            (shape((held, model), F32), VMEM),
            (shape((2, held), F32), VMEM),
            (shape((held, H), F32), VMEM),
            (shape((1, H), F32), VMEM),
            (shape((3, 128), F32), VMEM),
        ],
        [
            pltpu.VMEM((rows_all, model), BF16),
            pltpu.VMEM((rows_all, width), BF16),
            pltpu.VMEM((rows_all, 4 * HD), F32),
            pltpu.VMEM((rows_all, 4 * HD), F32),
            pltpu.VMEM((TP * HEADS, seq, seq), F32),
            pltpu.VMEM((model, width), BF16),
            pltpu.VMEM((4 * HD, model), BF16),
            pltpu.VMEM((rows_all, model), BF16),
            pltpu.VMEM((rows_all, width), BF16),
            pltpu.VMEM((rows_all, 4 * HD), BF16),
            pltpu.VMEM((rows_all, model), BF16),
            line, line, line,
            pltpu.VMEM((seq, model), F32),
            pltpu.VMEM((pair, 4 * HD), BF16),
            pltpu.VMEM((pair, 2 * HD), F32),
            pltpu.VMEM((2, ROWS, seq), BF16),
            pltpu.VMEM((ROWS, seq), F32),
            pltpu.VMEM((ROWS, model), F32),
            pltpu.VMEM((ROWS, model), F32),
            pltpu.VMEM((8, model), F32),
            pltpu.VMEM((model, width), BF16),
            pltpu.VMEM((share - 1, TP, held, width), BF16),
            pltpu.VMEM((reps, TP, bit, width) if cut > 1 else (1, 1, 16, 128), BF16),
            pltpu.VMEM((sheets, TP, held, width), BF16),
            pltpu.VMEM((4 * HD, model), BF16),
            pltpu.VMEM((share - 1, held, model), BF16),
            pltpu.VMEM((reps, held, model), BF16),
            pltpu.VMEM((n, ROWS, window), F32),
            pltpu.VMEM((n, 8, window), F32),
            pltpu.VMEM((reps, TP, ROWS + 8, window), F32),
            pltpu.SemaphoreType.DMA((8,)),
        ],
        20 * PIECES + 24 * PIECES + 2 * share * (TP + 1) + 2 * TP + 2 * reps * (2 * TP + 2) + 4 * n,
    )


def log_sigmoid(values_in):
    return jnp.minimum(values_in, 0.0) - jnp.log1p(jnp.exp(-jnp.abs(values_in)))


def per_device(
    reps,
    share,
    tokens,
    cotangent,
    pic_start,
    valid_mask,
    gain_attn,
    attn_in,
    forget_w,
    forget_bias,
    attn_out,
    gain_ffn,
    ffn_in,
    ffn_down,
):
    n = TP * share
    _, seq, model = tokens.shape
    held = attn_in.shape[0]
    heads = H // TP
    f = lax.axis_index("fsdp")
    t = f // share

    small = jnp.concatenate([forget_w.T, gain_attn[None], gain_ffn[None]])
    small = jnp.pad(small, ((0, 0), (0, 128 - held)))
    marks = jnp.concatenate(
        [valid_mask.astype(BF16), jnp.broadcast_to(pic_start.astype(BF16)[:, None], (1, seq))]
    )
    small = jnp.concatenate([small, marks, jnp.zeros((32 - H - 4, 128), BF16)])
    bias = lax.dynamic_slice_in_dim(forget_bias, heads * t, heads).astype(F32)
    bias = jnp.pad(bias, (0, ROWS - heads))
    branch_attn, cot, rows_a, proj, sig, att, probability, logit, w_cols, w_rows, w_forget, gains = attention(
        reps, share, tokens[0], cotangent[0], attn_in, small, attn_out, bias[None], bias[:, None]
    )
    valid_col = valid_mask[0].astype(F32)[:, None]
    activations, middle_grad, sums, ffn_in_sum, ffn_down_sum = feed_forward(
        reps, share, tokens[0], branch_attn, gains, valid_col, cot, ffn_in, ffn_down
    )
    input_grad, grad_in, grad_out, grad_gains, grad_forget, bias_total, stats = attention_back(
        reps, share, tokens[0], middle_grad, sums, valid_col, rows_a, proj, sig, att, probability, logit, w_cols, w_rows,
        w_forget, gains,
    )

    def over_reps(values_in):
        return jnp.sum(values_in.astype(F32), axis=0)

    hs = ffn_in.shape[2]
    grad_ffn_in = over_reps(ffn_in_sum)
    grad_ffn_in = jnp.stack([grad_ffn_in[:, :hs], grad_ffn_in[:, hs:]])
    return (
        activations[None],
        input_grad[None],
        grad_gains[0],
        grad_in,
        grad_forget,
        bias_total[0],
        grad_out,
        grad_gains[1],
        grad_ffn_in,
        over_reps(ffn_down_sum),
        stats[:, 0],
    )


def solution(mesh):
    placed = (
        P(("rep", "fsdp"), None, None),
        P(("rep", "fsdp"), None, None),
        P(("rep", "fsdp")),
        P(("rep", "fsdp"), None),
        P("fsdp"),
        P("fsdp", None),
        P("fsdp", None),
        P(),
        P("fsdp", None),
        P("fsdp"),
        P(None, None, "fsdp"),
        P("fsdp", None),
    )
    return jax.shard_map(
        functools.partial(per_device, mesh.shape["rep"], mesh.shape["fsdp"] // TP),
        mesh=mesh,
        in_specs=placed,
        out_specs=(
            P(("rep", "fsdp"), None, None),
            P(("rep", "fsdp"), None, None),
            P("fsdp"),
            P("fsdp", None),
            P("fsdp", None),
            P(),
            P("fsdp", None),
            P("fsdp"),
            P(None, None, "fsdp"),
            P("fsdp", None),
            P(),
        ),
        check_vma=False,
    )
```

```python
import functools

import jax
import jax.numpy as jnp
from jax import lax
from jax.experimental import pallas as pl
from jax.experimental.pallas import tpu as pltpu
from jax.sharding import PartitionSpec as P

H = 24
HD = 64
PIC = 32
TP = 8
DEPTH = 4
EPSILON = 1e-06
NEGATIVE = -1e30
MESH = pl.DeviceIdType.MESH
BF16 = jnp.bfloat16
F32 = jnp.float32
VMEM = pl.BlockSpec(memory_space=pltpu.VMEM)
ANY = pl.BlockSpec(memory_space=pl.ANY)


class Net:
    def __init__(self, reps, share, sems):
        self.reps, self.share, self.sems = reps, share, sems
        self.r = lax.axis_index("rep")
        self.f = lax.axis_index("fsdp")
        self.t = lax.div(self.f, share)
        self.u = lax.rem(self.f, share)
        self.z = lax.div(self.t, 2)
        self.x = lax.rem(self.t, 2)
        self.none = self.f * 0
        self.taken = 0
        self.sent = []

    def take(self, count=1):
        base = self.taken
        self.taken += count
        return base

    def place(self, t):
        return t * self.share + self.u

    def grid(self, z, x):
        return (z * 2 + x) * self.share + self.u

    def pair(self):
        return self.z + 1 - 2 * lax.rem(self.z, 2)

    def partners(self):
        for k in range(1, self.share):
            yield k, lax.rem(self.u + k, self.share)

    def greet(self, peers):
        barrier = pltpu.get_barrier_semaphore()
        total = 0
        for cond, r, f in peers:
            if cond is None:
                pl.semaphore_signal(barrier, 1, device_id=(r, f), device_id_type=MESH)
                total = total + 1
            else:

                @pl.when(cond)
                def _():
                    pl.semaphore_signal(barrier, 1, device_id=(r, f), device_id_type=MESH)

                total = total + cond.astype(jnp.int32)
        pl.semaphore_wait(barrier, total)

    def plane_peers(self):
        return [
            (self.z < DEPTH - 1, self.r, self.grid(self.z + 1, self.x)),
            (self.z > 0, self.r, self.grid(self.z - 1, self.x)),
            (None, self.r, self.grid(self.z, 1 - self.x)),
        ]

    def share_peers(self):
        return [(None, self.r, self.t * self.share + u) for _, u in self.partners()]

    def rep_peers(self):
        return [(None, lax.rem(self.r + k, self.reps), self.f) for k in range(1, self.reps)]

    def all_plane_peers(self):
        return [(None, self.r, self.place(lax.rem(self.t + k, TP))) for k in range(1, TP)]

    def copy(self, src, dst, ssem, rsem, f, r=None):
        return pltpu.make_async_remote_copy(
            src_ref=src,
            dst_ref=dst,
            send_sem=self.sems.at[ssem],
            recv_sem=self.sems.at[rsem],
            device_id=(self.r if r is None else r, f),
            device_id_type=MESH,
        )

    def send(self, src, dst, ssem, rsem, f, r=None, cond=None):
        copy = self.copy(src, dst, ssem, rsem, f, r)
        if cond is None:
            copy.start()
        else:
            pl.when(cond)(copy.start)
        self.sent.append((cond, copy))

    def arrive(self, dst, rsem, cond=None):
        copy = pltpu.make_async_remote_copy(
            src_ref=dst,
            dst_ref=dst,
            send_sem=self.sems.at[rsem],
            recv_sem=self.sems.at[rsem],
            device_id=(self.r, self.f),
            device_id_type=MESH,
        )
        if cond is None:
            copy.wait_recv()
        else:
            pl.when(cond)(copy.wait_recv)

    def drain(self):
        for cond, copy in self.sent:
            if cond is None:
                copy.wait_send()
            else:
                pl.when(cond)(copy.wait_send)
        self.sent = []


def nearest(z, k):
    swapped = (1, 0, 2, 3)[k] if isinstance(k, int) else None
    far = lax.div(z, 2)
    edge = z + far * (3 - 2 * z)
    if swapped is None:
        inner = jnp.where(k == 0, 1, jnp.where(k == 1, 0, k))
        place = jnp.where(edge == 0, k, inner)
    else:
        place = k + edge * (swapped - k)
    return far * 3 + (1 - 2 * far) * place


class Wave:
    def __init__(self, net, block, bent=False):
        self.net, self.block, self.bent = net, block, bent
        self.recv = net.take(TP)
        self.up, self.down, self.side = net.take(DEPTH), net.take(DEPTH), net.take(DEPTH)

    def copies(self, k):
        net = self.net
        z, x = net.z, net.x
        zo = nearest(z, k)
        t = zo * 2 + x
        block, sem = self.block(t), self.recv + t
        return [
            (
                (zo <= z) & (z < DEPTH - 1),
                net.copy(block, block, self.up + k, sem, net.grid(jnp.minimum(z + 1, DEPTH - 1), x)),
            ),
            (
                (zo >= z) & (z > 0),
                net.copy(block, block, self.down + k, sem, net.grid(jnp.maximum(z - 1, 0), x)),
            ),
            (None, net.copy(block, block, self.side + k, sem, net.grid(z, 1 - x))),
        ]

    def turn(self):
        if self.bent:
            net = self.net
            t = net.z * 2 + 1 - net.x
            block, sem = self.block(t), self.recv + t
            net.arrive(block, sem)
            net.copy(block, block, self.side + 1, sem, net.grid(net.pair(), net.x)).start()

    def hand_on(self, k, own=False):
        net = self.net
        t = nearest(net.z, k) * 2 + net.x
        if not own:
            net.arrive(self.block(t), self.recv + t, None if isinstance(k, int) else k > 0)
        up, down, side = self.copies(k)
        for cond, copy in (up, down):
            pl.when(cond)(copy.start)
        if self.bent:
            pl.when(net.none + k != 1)(side[1].start)
        else:
            side[1].start()

    def across(self, k):
        t = nearest(self.net.z, k) * 2 + 1 - self.net.x
        self.net.arrive(self.block(t), self.recv + t, self.net.none + k > 0 if self.bent else None)

    def drain(self):
        @pl.loop(0, DEPTH)
        def _(k):
            for cond, copy in self.copies(k):
                if cond is None:
                    copy.wait_send()
                else:
                    pl.when(cond)(copy.wait_send)


class Gather:
    def __init__(self, net, part, side, up, down, total, bent=False):
        self.net, self.part, self.side, self.up, self.down, self.total = net, part, side, up, down, total
        self.bent = bent
        self.sems = [net.take(DEPTH) for _ in range(6)]

    def across(self, k):
        net = self.net
        zo = nearest(net.z, k)
        return net.copy(
            self.part(zo * 2 + 1 - net.x), self.side(zo), self.sems[0] + zo, self.sems[1] + zo,
            net.grid(net.z, 1 - net.x),
        )

    def along(self, k):
        net = self.net
        z = net.z
        zo = nearest(z, k)
        part = self.part(zo * 2 + net.x)
        return [
            (
                zo > z,
                net.copy(
                    part, self.up(zo), self.sems[2] + zo, self.sems[3] + zo,
                    net.grid(jnp.minimum(z + 1, DEPTH - 1), net.x),
                ),
            ),
            (
                zo < z,
                net.copy(
                    part, self.down(zo), self.sems[4] + zo, self.sems[5] + zo,
                    net.grid(jnp.maximum(z - 1, 0), net.x),
                ),
            ),
        ]

    def begin(self, k):
        net = self.net
        z, pair = net.z, net.pair()
        if self.bent and k == 1:
            net.copy(
                self.part(pair * 2 + 1 - net.x), self.side(z), self.sems[0] + pair, self.sems[1] + z,
                net.grid(pair, net.x),
            ).start()
            return
        if self.bent and k == 0:
            net.arrive(self.side(pair), self.sems[1] + pair)
            part = self.part(z * 2 + 1 - net.x)
            part[...] = (part[...].astype(F32) + self.side(pair)[...].astype(F32)).astype(BF16)
        self.across(k).start()

    def step(self, k):
        net = self.net
        z = net.z
        zo = nearest(z, k)
        part = self.part(zo * 2 + net.x)
        if self.bent:
            self.total[...] = part[...].astype(F32)

            @pl.when(k != 1)
            def _():
                net.arrive(self.side(zo), self.sems[1] + zo)
                self.total[...] += self.side(zo)[...].astype(F32)
        else:
            net.arrive(self.side(zo), self.sems[1] + zo)
            self.total[...] = part[...].astype(F32) + self.side(zo)[...].astype(F32)
        for cond, ref, sem in (
            ((zo >= z) & (z > 0), self.up(zo), self.sems[3]),
            ((zo <= z) & (z < DEPTH - 1), self.down(zo), self.sems[5]),
        ):

            @pl.when(cond)
            def _():
                net.arrive(ref, sem + zo)
                self.total[...] += ref[...].astype(F32)

        @pl.when(zo != z)
        def _():
            part[...] = self.total[...].astype(BF16)

        for cond, copy in self.along(k):
            pl.when(cond)(copy.start)

    def drain(self):
        @pl.loop(0, DEPTH)
        def _(k):
            self.across(k).wait_send()
            for cond, copy in self.along(k):
                pl.when(cond)(copy.wait_send)


def column(row):
    size = row.shape[1]
    square = (size, size)
    same = lax.broadcasted_iota(jnp.int32, square, 0) == lax.broadcasted_iota(jnp.int32, square, 1)
    return jnp.sum(jnp.where(same, row, 0.0), axis=1, keepdims=True)


def begin_last(gathers, bent):
    for gather in gathers:
        if gather.bent == bent:
            gather.begin(0)


def call(body, name, number, operands, in_specs, outs, scratch, sems, limit=60 << 20):
    return pl.pallas_call(
        body,
        name=name,
        out_shape=tuple(shape for shape, _ in outs),
        in_specs=in_specs,
        out_specs=tuple(spec for _, spec in outs),
        scratch_shapes=list(scratch) + [pltpu.SemaphoreType.DMA((sems,))],
        compiler_params=pltpu.CompilerParams(
            collective_id=number, has_side_effects=True, vmem_limit_bytes=limit
        ),
    )(*operands)


def chunk(rows, count, c):
    return pl.ds(c * (rows // count), rows // count)


def matmul_nt(a, b):
    return lax.dot_general(a, b, (((1,), (1,)), ((), ())), preferred_element_type=F32)


def matmul_tn(a, b):
    return lax.dot_general(a, b, (((0,), (0,)), ((), ())), preferred_element_type=F32)


def matmul(a, b):
    return jnp.dot(a, b, preferred_element_type=F32)


def tile(j, size):
    return pl.ds(pl.multiple_of(j * size, size), size)


PIECES = 2


def feed_forward(reps, share, x, branch, gain, valid, cot, w_in, w_down):
    seq, model = x.shape
    hs = w_in.shape[2]
    hidden_all = share * hs
    rows_all = TP * seq
    pair = 2 * seq
    half = seq // PIECES

    def body(
        x_ref, branch_ref, gain_ref, valid_ref, cot_ref, in_ref, down_ref,
        act_ref, grad_ref, sums_ref, in_out, down_out,
        middle, rows, cot_all, w_all, wd, hid, grads, part, side, up, down, rows_sum, ffn_sum,
        in_part, down_part, in_got, down_got, local, sems,
    ):
        net = Net(reps, share, sems)
        own = [
            pltpu.make_async_copy(in_ref.at[0], w_all.at[:, pl.ds(0, hs)], local.at[0]),
            pltpu.make_async_copy(in_ref.at[1], w_all.at[:, pl.ds(hs, hs)], local.at[1]),
            pltpu.make_async_copy(down_ref, wd.at[pl.ds(0, hs)], local.at[2]),
            pltpu.make_async_copy(cot_ref, cot_all, local.at[3]),
        ]
        for copy in own:
            copy.start()

        def block(ref, t):
            return ref.at[tile(t, seq)]

        middle[...] = x_ref[...].astype(F32) + branch_ref[...]
        scale = lax.rsqrt(jnp.mean(middle[...] * middle[...], axis=-1, keepdims=True) + EPSILON)
        block(rows, net.t)[...] = (middle[...] * scale * gain_ref[1:2]).astype(BF16)
        net.greet(net.plane_peers() + net.share_peers() + net.rep_peers())

        waves = [
            Wave(net, lambda t, c=c: rows.at[pl.ds(pl.multiple_of(t * seq + c * half, half), half)])
            for c in range(PIECES)
        ]
        weights = net.take(3 * share), net.take(3 * share)
        for wave in waves:
            wave.hand_on(0, own=True)
        arriving = []
        for k, u in net.partners():
            f, p = net.t * share + u, share - k
            for j, (src, dst) in enumerate(
                [
                    (in_ref.at[0], w_all.at[:, pl.ds(2 * hs * p, hs)]),
                    (in_ref.at[1], w_all.at[:, pl.ds(2 * hs * p + hs, hs)]),
                    (down_ref, wd.at[pl.ds(hs * p, hs)]),
                ]
            ):
                net.send(src, dst, weights[0] + 3 * k + j, weights[1] + 3 * p + j, f)
                arriving.append((dst, weights[1] + 3 * p + j))

        def unit(k):
            at = tile(nearest(net.z, k), pair)
            projected = matmul(rows[at], w_all[...])
            hidden_grad = matmul_nt(cot_all[at], wd[...])
            for p in range(share):
                gate = projected[:, 2 * hs * p : 2 * hs * p + hs]
                lift = projected[:, 2 * hs * p + hs : 2 * hs * (p + 1)]
                back = hidden_grad[:, hs * p : hs * (p + 1)]
                sig = jax.nn.sigmoid(gate)
                silu = gate * sig
                hid[at, hs * p : hs * (p + 1)] = (silu * lift).astype(BF16)
                grads[at, 2 * hs * p : 2 * hs * p + hs] = (
                    back * lift * sig * (1.0 + gate * (1.0 - sig))
                ).astype(BF16)
                grads[at, 2 * hs * p + hs : 2 * hs * (p + 1)] = (back * silu).astype(BF16)

            @pl.loop(0, 3)
            def _(j):
                to = tile(j, model // 3)
                part[0, at, to] = matmul_nt(grads[at], w_all[to]).astype(BF16)
                part[1, at, to] = matmul(hid[at], wd[:, to]).astype(BF16)

        def piece(ref, i, c, count):
            return lambda j: ref.at[i, pl.ds(pl.multiple_of(j * seq + c * half, half), half)]

        gathers = [
            [
                Gather(
                    net, piece(part, i, c, TP), piece(side, i, c, DEPTH), piece(up, i, c, DEPTH),
                    piece(down, i, c, DEPTH), total.at[pl.ds(c * half, half)],
                )
                for c in range(PIECES)
            ]
            for i, total in enumerate((rows_sum, ffn_sum))
        ]
        @pl.loop(1, DEPTH + 1)
        def _(k):
            @pl.when(k < DEPTH)
            def _():
                for wave in waves:
                    wave.hand_on(k)

            @pl.when(k == 1)
            def _():
                for wave in waves:
                    wave.turn()
                for copy in own:
                    copy.wait()
                for dst, sem in arriving:
                    net.arrive(dst, sem)

            for wave in waves:
                wave.across(k - 1)

            @pl.when(k == DEPTH)
            def _():
                for gather in gathers[0]:
                    gather.begin(DEPTH - 2)

            unit(k - 1)

        for k in (DEPTH - 1, *range(DEPTH - 3, 0, -1)):
            for gather in gathers[0]:
                gather.begin(k)
        begin_last(gathers[0], False)

        @pl.loop(0, model // 256)
        def _(j):
            at = tile(j, 256)
            in_part[at] = matmul_tn(rows[:, at], grads[...]).astype(BF16)

        begin_last(gathers[0], True)
        for k in range(DEPTH - 1, 0, -1):
            for gather in gathers[1]:
                gather.begin(k)
        begin_last(gathers[1], False)

        @pl.loop(0, 3)
        def _(j):
            at = tile(j, model // 3)
            down_part[:, at] = matmul_tn(hid[...], cot_all[:, at]).astype(BF16)

        first, arrived = net.take(2 * share), net.take(2 * share)
        away, back = net.take(2 * reps), net.take(2 * reps)
        for k, u in net.partners():
            f, slot = net.t * share + u, share - 1 - k
            net.send(
                in_part.at[:, pl.ds(2 * hs * k, 2 * hs)], in_got.at[slot], first + 2 * k, arrived + 2 * slot, f
            )
            net.send(
                down_part.at[pl.ds(hs * k, hs)], down_got.at[slot], first + 2 * k + 1, arrived + 2 * slot + 1, f
            )

        def own_grads():
            for slot in range(share - 1):
                net.arrive(in_got.at[slot], arrived + 2 * slot)
                net.arrive(down_got.at[slot], arrived + 2 * slot + 1)

            @pl.loop(0, model // 256)
            def _(j):
                at = tile(j, 256)
                total = in_part[at, : 2 * hs].astype(F32)
                for slot in range(share - 1):
                    total = total + in_got[slot, at].astype(F32)
                in_out[net.r, at] = total.astype(BF16)

            total = down_part[:hs].astype(F32)
            for slot in range(share - 1):
                total = total + down_got[slot].astype(F32)
            down_out[net.r] = total.astype(BF16)
            for k in range(1, reps):
                r = lax.rem(net.r + k, reps)
                net.send(in_out.at[net.r], in_out.at[net.r], away + 2 * k, back + 2 * net.r, net.f, r=r)
                net.send(down_out.at[net.r], down_out.at[net.r], away + 2 * k + 1, back + 2 * net.r + 1, net.f, r=r)

        def steps(both, start, stop):
            @pl.loop(start, stop)
            def _(j):
                for gather in both:
                    gather.step(DEPTH - 1 - j)

        steps(gathers[0], 0, 2)
        begin_last(gathers[1], True)
        own_grads()
        steps(gathers[0], 2, DEPTH)
        steps(gathers[1], 0, DEPTH)

        result = middle[...] + ffn_sum[...]
        act_ref[...] = result.astype(BF16)
        valid_col = column(valid_ref[...].astype(F32))
        scale = lax.rsqrt(jnp.mean(middle[...] * middle[...], axis=-1, keepdims=True) + EPSILON)
        lifted = rows_sum[...] * gain_ref[1:2]
        mean = jnp.mean(middle[...] * lifted, axis=-1, keepdims=True)
        grad_ref[...] = (
            block(cot_all, net.t)[...].astype(F32) + scale * lifted - middle[...] * (scale * scale * scale) * mean
        )
        sums_ref[...] = jnp.zeros_like(sums_ref)
        sums_ref[0:1] = jnp.sum(rows_sum[...] * middle[...] * scale, axis=0, keepdims=True)
        sums_ref[1:2] = jnp.sum(result * result * valid_col, axis=0, keepdims=True)
        sums_ref[2:3] = jnp.sum(branch_ref[...] * branch_ref[...] * valid_col, axis=0, keepdims=True)
        sums_ref[3:4] = jnp.sum(ffn_sum[...] * ffn_sum[...] * valid_col, axis=0, keepdims=True)
        for k in range(1, reps):
            r = lax.rem(net.r + k, reps)
            net.arrive(in_out.at[r], back + 2 * r)
            net.arrive(down_out.at[r], back + 2 * r + 1)
        net.drain()
        for wave in waves:
            wave.drain()
        for gather in gathers[0] + gathers[1]:
            gather.drain()

    shape = jax.ShapeDtypeStruct
    line = pltpu.VMEM((2, DEPTH * seq, model), BF16)
    return call(
        body, "feed_forward", 3, (x, branch, gain, valid, cot, w_in, w_down), [VMEM] * 4 + [ANY] * 3,
        [
            (shape((seq, model), BF16), VMEM),
            (shape((seq, model), F32), VMEM),
            (shape((8, model), F32), VMEM),
            (shape((reps, model, 2 * hs), BF16), VMEM),
            (shape((reps, hs, model), BF16), VMEM),
        ],
        [
            pltpu.VMEM((seq, model), F32),
            pltpu.VMEM((rows_all, model), BF16),
            pltpu.VMEM((rows_all, model), BF16),
            pltpu.VMEM((model, 2 * hidden_all), BF16),
            pltpu.VMEM((hidden_all, model), BF16),
            pltpu.VMEM((rows_all, hidden_all), BF16),
            pltpu.VMEM((rows_all, 2 * hidden_all), BF16),
            pltpu.VMEM((2, rows_all, model), BF16),
            line, line, line,
            pltpu.VMEM((seq, model), F32),
            pltpu.VMEM((seq, model), F32),
            pltpu.VMEM((model, 2 * hidden_all), BF16),
            pltpu.VMEM((hidden_all, model), BF16),
            pltpu.VMEM((share - 1, model, 2 * hs), BF16),
            pltpu.VMEM((share - 1, hs, model), BF16),
            pltpu.SemaphoreType.DMA((4,)),
        ],
        40 * PIECES + 24 * 2 * PIECES + 20 * share + 10 * reps,
    )


HEADS = H // TP
ROWS = 16


def cuts(reps, held):
    return reps if held % (16 * reps) == 0 else 1


def lane_mask(shape, low, high):
    lane = lax.broadcasted_iota(jnp.int32, shape, 1)
    return (lane >= low) & (lane < high)


def head_pieces(t, block):
    base = block * H * HD + t * HEADS * HD
    return [(base, 2 * HD, block * 2 * HD), (base + 2 * HD, HD, 8 * HD + block * HD)]


def attention(reps, share, x, cot, w_in, w_out, forget, gain_a, gain_f, mask, start, bias):
    n = TP * share
    seq, model = x.shape
    held = w_in.shape[0]
    width = 4 * HEADS * HD
    rows_all = TP * seq
    pair = 2 * seq
    half = seq // PIECES
    last = HEADS - 1
    cut = cuts(reps, held)

    def body(
        x_ref, cot_ref, in_ref, out_ref, forget_ref, gain_a_ref, gain_f_ref, mask_ref, start_ref, bias_ref,
        branch_ref, cot_out, rows_out, proj_out, sig_out, att_out, prob_out, logit_ref, wc_out, wo_out, wf_ref, gains_ref,
        xs, cots, rows, proj, sig, att, prob, wc, wo, split, smalls, lines, part, side, up, down, gated, local, sems,
    ):
        net = Net(reps, share, sems)

        def seq_block(ref, t):
            return ref.at[tile(t, seq)]

        def held_rows(f):
            return wc.at[tile(f, held)]

        def spot(r):
            return r if cut > 1 else 0

        def piece_of(r):
            return tile(spot(r), held // cut)

        def held_piece(f, r):
            return wc.at[pl.ds(pl.multiple_of(f * held + spot(r) * (held // cut), held // cut), held // cut)]

        own = [
            pltpu.make_async_copy(x_ref, seq_block(xs, net.t), local.at[0]),
            pltpu.make_async_copy(cot_ref, seq_block(cots, net.t), local.at[1]),
            pltpu.make_async_copy(out_ref, wo.at[tile(net.u, held)], local.at[3]),
        ]
        for copy in own:
            copy.start()
        small = lines.at[:, pl.ds(0, 128)]
        small[...] = jnp.zeros((32, 128), F32)
        small[:H, :held] = forget_ref[...].astype(F32)
        small[H : H + 1, :held] = gain_a_ref[...].astype(F32)
        small[H + 1 : H + 2, :held] = gain_f_ref[...].astype(F32)
        small[H + 2 : H + 3, :seq] = mask_ref[...].astype(F32)
        small[H + 3 : H + 4, :seq] = jnp.full((1, seq), start_ref[0], jnp.int32).astype(F32)
        smalls[net.f] = small[...].astype(BF16)
        for t in range(TP):
            for block in range(4):
                for column, wide, to in head_pieces(t, block):
                    split[t, :, to : to + wide] = in_ref[:, column : column + wide]
        wo[share * held :] = jnp.zeros((wo.shape[0] - share * held, model), BF16)
        others = [lax.rem(net.f + k, n) for k in range(n)]
        chips = [lax.rem(net.t + k, TP) for k in range(TP)]
        partners = list(net.partners())
        replicas = [lax.rem(net.r + k, reps) for k in range(reps)]
        net.greet([(None, net.r, f) for f in others[1:]] + [(None, r, net.f) for r in replicas[1:cut]])

        small_send, small_recv = net.take(n), net.take(n)
        w_send, w_recv = net.take(TP), net.take(n * cut)
        w_pass = net.take(share * TP * (cut + 1))
        w_away = net.take(TP * cut)
        wo_send, wo_recv = net.take(share), net.take(share)
        for k in range(1, n):
            net.send(smalls.at[net.f], smalls.at[net.f], small_send + k, small_recv + net.f, others[k])
        for k in range(1, TP):
            net.send(
                split.at[chips[k], piece_of(net.r)], held_piece(net.f, net.r), w_send + k, w_recv + cut * net.f + spot(net.r),
                net.place(chips[k]),
            )
        own_cols = pltpu.make_async_copy(split.at[net.t], held_rows(net.f), local.at[4])
        own_cols.start()
        for k, u in partners:
            f = net.t * share + u
            net.send(split.at[net.t], held_rows(net.f), w_pass + k, w_recv + cut * net.f, f)
            net.send(out_ref, wo.at[tile(net.u, held)], wo_send + k, wo_recv + net.u, f)

        def pieces(ref):
            return [
                Wave(net, lambda t, c=c: ref.at[pl.ds(pl.multiple_of(t * seq + c * half, half), half)])
                for c in range(PIECES)
            ]

        waves, cot_waves = pieces(xs), pieces(cots)
        for copy in own:
            copy.wait()
        for wave in waves:
            wave.hand_on(0, own=True)
        for wave in cot_waves:
            wave.copies(0)[2][1].start()

        def weights():
            for q in range(cut):
                r = replicas[q]
                for k in range(1, TP):
                    source = net.place(chips[k])
                    got, sem = held_piece(source, r), w_recv + cut * source + spot(r)
                    net.arrive(got, sem)
                    for j, u in partners:
                        net.send(got, got, w_pass + share * (TP * (q + 1) + k) + j, sem, net.t * share + u)
                    for p in range(1, cut if q == 0 else 1):
                        net.send(got, got, w_away + TP * p + k, sem, net.f, r=replicas[p])
                if q == 0:
                    for wave in waves:
                        wave.hand_on(2)
            for k in range(1, n):
                net.arrive(smalls.at[others[k]], small_recv + others[k])
            for j in range(model // 128):
                line = jnp.zeros((32, 128), F32)
                for f in range(j * 128 // held, ((j + 1) * 128 - 1) // held + 1):
                    start = f * held - j * 128
                    piece = pltpu.roll(smalls[f].astype(F32), net.none + start % 128, 1)
                    line = jnp.where(lane_mask((32, 128), start, start + held), piece, line)
                lines[:, j * 128 : (j + 1) * 128] = line
            pick = lax.broadcasted_iota(jnp.int32, (ROWS, 32), 0) + HEADS * net.t
            pick = pick == lax.broadcasted_iota(jnp.int32, (ROWS, 32), 1)
            pick &= lax.broadcasted_iota(jnp.int32, (ROWS, 32), 0) < HEADS
            wf_ref[...] = matmul(pick.astype(BF16), lines[...].astype(BF16)).astype(BF16)
            gains_ref[...] = lines[H : H + 8]
            for k, u in partners:
                net.arrive(wo.at[tile(u, held)], wo_recv + u)
                net.arrive(held_rows(net.t * share + u), w_recv + cut * (net.t * share + u))
                for k in range(1, TP):
                    f = chips[k] * share + u
                    for r in replicas[:cut]:
                        net.arrive(held_piece(f, r), w_recv + cut * f + spot(r))
            own_cols.wait()

        own_head = lax.broadcasted_iota(jnp.int32, (ROWS, H), 0)
        picked = own_head + HEADS * net.t == lax.broadcasted_iota(jnp.int32, (ROWS, H), 1)
        bias_col = jnp.sum(
            jnp.where(picked & (own_head < HEADS), bias_ref[...].astype(F32), 0.0), axis=1, keepdims=True
        )
        few = (ROWS, ROWS)
        same = lax.broadcasted_iota(jnp.int32, few, 0) == lax.broadcasted_iota(jnp.int32, few, 1)
        bias_row = jnp.sum(jnp.where(same, bias_col, 0.0), axis=0, keepdims=True)
        square = (seq, seq)
        at_row = lax.broadcasted_iota(jnp.int32, square, 0)
        at_col = lax.broadcasted_iota(jnp.int32, square, 1)

        def unit(k):
            place = nearest(net.z, k)
            at = tile(place, pair)
            values_in = xs[at].astype(F32)
            inverse = lax.rsqrt(jnp.mean(values_in * values_in, axis=-1, keepdims=True) + EPSILON)
            rows[at] = (values_in * inverse * gains_ref[0:1]).astype(BF16)
            projected = matmul(rows[at], wc[...])
            proj[at] = projected.astype(BF16)
            sig[at, : 2 * HD] = jax.nn.sigmoid(projected[:, 6 * HD : 8 * HD])
            tail = pltpu.roll(jax.nn.sigmoid(projected[:, 10 * HD : 12 * HD]), net.none + HD, 1)
            sig[at, 2 * HD :] = jnp.where(lane_mask(tail.shape, 0, HD), tail, 0.0)

            @pl.loop(0, 2, unroll=True)
            def _(j):
                t = place * 2 + j
                here = tile(t, seq)
                marks = smalls[net.place(t)].astype(F32)
                valid = marks[H + 2 : H + 3]
                start = marks[H + 3 : H + 4].astype(jnp.int32)
                causal = at_col <= at_row
                inside = (at_row >= start) & (at_row < start + PIC) & (at_col >= start) & (at_col < start + PIC)
                allowed = (causal | inside) & (valid > 0.0)
                sign = jnp.where(causal, 1.0, -1.0)
                below = sign * 0.5 + 0.5
                logit_col = matmul_nt(rows[here], wf_ref[...]) + bias_row
                logit_row = matmul_nt(wf_ref[...], rows[here]) + bias_col
                logit_ref[t] = logit_row
                decay_col = jnp.dot(
                    below, log_sigmoid(logit_col), precision=lax.Precision.HIGHEST, preferred_element_type=F32
                )
                decay_row = lax.dot_general(
                    log_sigmoid(logit_row), below, (((1,), (1,)), ((), ())),
                    precision=lax.Precision.HIGHEST, preferred_element_type=F32,
                )
                outs = []
                for h in range(HEADS):
                    if h < last:
                        query = jnp.where(lane_mask((seq, 2 * HD), h * HD, h * HD + HD), proj[here, : 2 * HD], 0)
                        key, value = proj[here, 2 * HD : 4 * HD], proj[here, 4 * HD : 6 * HD]
                    else:
                        query = jnp.where(lane_mask((seq, 2 * HD), 0, HD), proj[here, 8 * HD : 10 * HD], 0)
                        key = pltpu.roll(proj[here, 8 * HD : 10 * HD].astype(F32), net.none + HD, 1).astype(BF16)
                        value = proj[here, 10 * HD :]
                    scores = matmul_nt(query, key) * HD ** (-0.5)
                    scores = scores + sign * (decay_col[:, h : h + 1] - decay_row[h : h + 1])
                    masked = jnp.where(allowed, scores, NEGATIVE)
                    weights_now = jnp.exp(masked - jnp.max(masked, axis=-1, keepdims=True))
                    probability = weights_now / jnp.sum(weights_now, axis=-1, keepdims=True)
                    prob[t * HEADS + h] = probability
                    outs.append(matmul(probability.astype(BF16), value))
                low = lane_mask((seq, 2 * HD), 0, HD)
                att[here, : 2 * HD] = jnp.where(low, outs[0], outs[1])
                att[here, 2 * HD :] = jnp.where(low, outs[2], 0.0)

            gated[...] = (att[at] * sig[at]).astype(BF16)

            @pl.loop(0, 3)
            def _(j):
                to = tile(j, model // 3)
                part[at, to] = matmul(gated[...], wo[:, to]).astype(BF16)

        gathers = [
            Gather(
                net,
                *[
                    lambda j, ref=ref, c=c: ref.at[pl.ds(pl.multiple_of(j * seq + c * half, half), half)]
                    for ref in (part, side, up, down)
                ],
                branch_ref.at[pl.ds(c * half, half)],
            )
            for c in range(PIECES)
        ]

        for wave in waves:
            wave.hand_on(1)
            wave.turn()
        weights()

        @pl.loop(1, DEPTH + 1)
        def _(k):
            @pl.when(k == 2)
            def _():
                for wave in waves:
                    wave.hand_on(DEPTH - 1)
                for wave in cot_waves:
                    for cond, copy in wave.copies(0)[:2]:
                        pl.when(cond)(copy.start)
                    wave.turn()

            @pl.when(k == 3)
            def _():
                for wave in cot_waves:
                    wave.hand_on(1)

            for wave in waves:
                wave.across(k - 1)

            @pl.when(k == DEPTH)
            def _():
                for gather in gathers:
                    gather.begin(DEPTH - 2)

            unit(k - 1)

        keep = [
            pltpu.make_async_copy(src, dst, local.at[5 + i])
            for i, (src, dst) in enumerate(
                [
                    (rows, rows_out), (proj, proj_out), (sig, sig_out), (att, att_out), (prob, prob_out),
                    (wc, wc_out), (wo, wo_out),
                ]
            )
        ]
        for k in (DEPTH - 1, *range(DEPTH - 3, 0, -1)):
            for gather in gathers:
                gather.begin(k)
        begin_last(gathers, False)

        for copy in keep:
            copy.start()

        @pl.loop(0, DEPTH)
        def _(j):
            for gather in gathers:
                gather.step(DEPTH - 1 - j)

            @pl.when(j == 0)
            def _():
                begin_last(gathers, True)

            @pl.when(j < DEPTH - 2)
            def _():
                for wave in cot_waves:
                    wave.hand_on(j + 2)

        for k in range(DEPTH):
            for wave in cot_waves:
                wave.across(k)
        save = pltpu.make_async_copy(cots, cot_out, local.at[1])
        save.start()
        net.drain()
        for wave in waves + cot_waves:
            wave.drain()
        for gather in gathers:
            gather.drain()
        for copy in keep:
            copy.wait()
        save.wait()

    shape = jax.ShapeDtypeStruct
    line = pltpu.VMEM((DEPTH * seq, model), BF16)
    kept = [
        ((rows_all, model), BF16),
        ((rows_all, model), BF16),
        ((rows_all, width), BF16),
        ((rows_all, 4 * HD), F32),
        ((rows_all, 4 * HD), F32),
        ((TP * HEADS, seq, seq), F32),
    ]
    return call(
        body, "attention", 1, (x, cot, w_in, w_out, forget, gain_a, gain_f, mask, start, bias),
        [ANY, ANY, VMEM, ANY, VMEM, VMEM, VMEM, VMEM, pl.BlockSpec(memory_space=pltpu.SMEM), VMEM],
        [(shape((seq, model), F32), VMEM)]
        + [(shape(*what), ANY) for what in kept]
        + [
            (shape((TP, ROWS, seq), F32), VMEM),
            (shape((model, width), BF16), ANY),
            (shape((4 * HD, model), BF16), ANY),
            (shape((ROWS, model), BF16), VMEM),
            (shape((8, model), F32), VMEM),
        ],
        [pltpu.VMEM((rows_all, model), BF16)]
        + [pltpu.VMEM(*what) for what in kept]
        + [
            pltpu.VMEM((model, width), BF16),
            pltpu.VMEM((4 * HD, model), BF16),
            pltpu.VMEM((TP, held, width), BF16),
            pltpu.VMEM((n, 32, 128), BF16),
            pltpu.VMEM((32, model), F32),
            pltpu.VMEM((rows_all, model), BF16),
            line, line, line,
            pltpu.VMEM((pair, 4 * HD), BF16),
            pltpu.SemaphoreType.DMA((12,)),
        ],
        2 * 20 * PIECES + 24 * PIECES + (2 + cut) * n + (1 + cut) * (TP + share * TP) + 2 * share,
    )


def attention_back(
    reps, share, x, middle_grad, sums, valid, rows_a, proj, sig, att, prob, logit, wc, wo, wf, gains,
    ffn_in, ffn_down,
):
    n = TP * share
    seq, model = x.shape
    width = 4 * HEADS * HD
    held = model // n
    rows_all = TP * seq
    pair = 2 * seq
    half = seq // PIECES
    last = HEADS - 1
    window = 256
    cut = cuts(reps, held)
    bit = held // cut
    sheets = 1 if cut > 1 else reps
    hs = ffn_down.shape[1]

    def body(
        x_ref, grad_ref, sums_ref, valid_ref, rows_in, proj_in, sig_in, att_in, prob_in, logit_ref, wc_in, wo_in, wf_ref,
        gains_ref, ffn_in_ref, ffn_down_ref,
        input_ref, in_ref, out_ref, gains_out, forget_ref, bias_ref, stats_ref, ffn_in_out, ffn_down_out,
        rows, proj, sig, att, prob, wcs, wos, bgs, pg, gated, part, side, up, down, rows_sum, ag, og, low_logit, bias_sum,
        forget_sum, lines, late, in_part, in_got, swapped_in, in_all, out_part, out_got, out_all, small_got, first_got,
        small_mid, ffn_in, ffn_down, ffn_in_sum, ffn_down_sum, local, sems,
    ):
        net = Net(reps, share, sems)
        others = [lax.rem(net.f + k, n) for k in range(n)]
        chips = [lax.rem(net.t + k, TP) for k in range(TP)]
        partners = list(net.partners())
        own = [
            pltpu.make_async_copy(src, dst, local.at[i])
            for i, (src, dst) in enumerate(
                [
                    (wo_in, wos), (sig_in, sig), (att_in, att), (proj_in, proj), (prob_in, prob), (rows_in, rows),
                    (wc_in, wcs),
                ]
            )
        ]
        ffn_parts = [
            pltpu.make_async_copy(ffn_in_ref, ffn_in, local.at[7]),
            pltpu.make_async_copy(ffn_down_ref, ffn_down, local.at[8]),
        ]
        ffn_totals = [
            pltpu.make_async_copy(ffn_in_sum, ffn_in_out, local.at[9]),
            pltpu.make_async_copy(ffn_down_sum, ffn_down_out, local.at[10]),
        ]
        for copy in own + ffn_parts:
            copy.start()
        bgs[tile(net.t, seq)] = grad_ref[...].astype(BF16)
        net.greet([(None, net.r, f) for f in others[1:]] + net.rep_peers())
        waves = [
            Wave(net, lambda t, c=c: bgs.at[pl.ds(pl.multiple_of(t * seq + c * half, half), half)], c == 1)
            for c in range(PIECES)
        ]
        for wave in waves:
            wave.hand_on(0, own=True)
        bias_sum[...] = jnp.zeros_like(bias_sum)
        forget_sum[...] = jnp.zeros_like(forget_sum)
        for copy in own:
            copy.wait()

        square = (seq, seq)
        causal = lax.broadcasted_iota(jnp.int32, square, 1) <= lax.broadcasted_iota(jnp.int32, square, 0)
        below = jnp.where(causal, 1.0, 0.0)
        low = lane_mask((seq, 2 * HD), 0, HD)
        head_row = lax.broadcasted_iota(jnp.int32, (ROWS, seq), 0)

        def unit(k):
            place = nearest(net.z, k)
            at = tile(place, pair)
            gated_grad = matmul_nt(bgs[at], wos[...])
            gate, attended = sig[at], att[at]
            ag[...] = (gated_grad * gate).astype(BF16)
            gated[at] = (attended * gate).astype(BF16)
            gate_grad = gated_grad * attended * (gate * (1.0 - gate))
            pg[at, 6 * HD : 8 * HD] = gate_grad[:, : 2 * HD].astype(BF16)
            og[...] = pltpu.roll(gate_grad[:, 2 * HD :], net.none + HD, 1)

            @pl.loop(0, 2, unroll=True)
            def _(j):
                t = place * 2 + j
                here = tile(t, seq)
                inner = tile(j, seq)
                swapped = pltpu.roll(proj[here, 8 * HD : 10 * HD].astype(F32), net.none + HD, 1).astype(BF16)
                decay_grad = jnp.zeros((ROWS, seq), F32)
                found = []
                for h in range(HEADS):
                    probability = prob[t * HEADS + h]
                    if h < last:
                        back_all = ag[inner, : 2 * HD]
                        back = jnp.where(lane_mask((seq, 2 * HD), h * HD, h * HD + HD), back_all, 0)
                        query, key, value = (proj[here, 2 * HD * i : 2 * HD * (i + 1)] for i in range(3))
                    else:
                        back = back_all = ag[inner, 2 * HD :]
                        query, key, value = swapped, swapped, proj[here, 10 * HD :]
                    prob_grad = matmul_nt(back, value)
                    score_grad = probability * (
                        prob_grad - jnp.sum(probability * prob_grad, axis=-1, keepdims=True)
                    )
                    dotted_grad = (score_grad * HD ** (-0.5)).astype(BF16)
                    found.append(
                        (
                            matmul(dotted_grad, key),
                            matmul_tn(dotted_grad, query),
                            matmul_tn(probability.astype(BF16), back_all),
                        )
                    )
                    signed = jnp.where(causal, score_grad, -score_grad)
                    line = jnp.sum(signed.T - signed, axis=0, keepdims=True)
                    decay_grad = jnp.where(head_row == h, line, decay_grad)
                for i in range(3):
                    pg[here, 2 * HD * i : 2 * HD * (i + 1)] = jnp.where(low, found[0][i], found[1][i]).astype(BF16)
                pg[here, 8 * HD : 10 * HD] = jnp.where(low, found[2][0], found[2][1]).astype(BF16)
                pg[here, 10 * HD :] = jnp.where(low, found[2][2], og[inner]).astype(BF16)
                later = jnp.dot(decay_grad, below, precision=lax.Precision.HIGHEST, preferred_element_type=F32)
                logit_grad = later * jax.nn.sigmoid(-logit_ref[t])
                bias_sum[...] += logit_grad
                low_logit[j] = logit_grad.astype(BF16)
                forget_sum[...] += matmul(logit_grad.astype(BF16), rows[here])

            @pl.loop(0, 3)
            def _(i):
                to = tile(i, model // 3)
                main = matmul_nt(pg[at], wcs[to])
                for j in range(2):
                    extra = matmul_tn(low_logit[j], wf_ref[:, to])
                    part[tile(place * 2 + j, seq), to] = (main[j * seq : (j + 1) * seq] + extra).astype(BF16)

        gathers = [
            Gather(
                net,
                *[
                    lambda j, ref=ref, c=c: ref.at[pl.ds(pl.multiple_of(j * seq + c * half, half), half)]
                    for ref in (part, side, up, down)
                ],
                rows_sum.at[pl.ds(c * half, half)], c == 1,
            )
            for c in range(PIECES)
        ]

        @pl.loop(1, DEPTH + 1)
        def _(k):
            @pl.when(k < DEPTH)
            def _():
                for wave in waves:
                    wave.hand_on(k)

            @pl.when(k == 1)
            def _():
                for wave in waves:
                    wave.turn()

            for wave in waves:
                wave.across(k - 1)

            @pl.when(k == DEPTH)
            def _():
                for gather in gathers:
                    gather.begin(DEPTH - 2)

            unit(k - 1)

        for k in (DEPTH - 1, *range(DEPTH - 3, 0, -1)):
            for gather in gathers:
                gather.begin(k)
        begin_last(gathers, False)

        @pl.loop(0, model // 256)
        def _(j):
            at = tile(j, 256)
            in_part[at] = matmul_tn(rows[:, at], pg[...]).astype(BF16)

        @pl.loop(0, 3)
        def _(j):
            at = tile(j, model // 3)
            out_part[:, at] = matmul_tn(gated[...], bgs[:, at]).astype(BF16)

        begin_last(gathers, True)

        def ffn_grads():
            for copy in ffn_parts:
                copy.wait()

            @pl.loop(0, model // 256)
            def _(j):
                at = tile(j, 256)
                for i in range(2):
                    half_sum = ffn_in[0, at, i * hs : (i + 1) * hs].astype(F32)
                    for r in range(1, reps):
                        half_sum = half_sum + ffn_in[r, at, i * hs : (i + 1) * hs].astype(F32)
                    ffn_in_sum[i, at] = half_sum
                down_sum = ffn_down[0, :, at].astype(F32)
                for r in range(1, reps):
                    down_sum = down_sum + ffn_down[r, :, at].astype(F32)
                ffn_down_sum[:, at] = down_sum

            for copy in ffn_totals:
                copy.start()

        def owned(t, u):
            return tile(t * share + u, held)

        def seen(f):
            start = jnp.minimum(lax.div(f * held, 128) * 128, model - window)
            return pl.ds(pl.multiple_of(start, 128), window)

        small_send, small_recv = net.take(n), net.take(n)
        lines[...] = jnp.zeros_like(lines)
        lines[0:1] = sums_ref[0:1]
        lines[1 : 1 + HEADS] = forget_sum[:HEADS]
        for i in range(3):
            lines[4 + i : 5 + i] = jnp.broadcast_to(jnp.sum(sums_ref[1 + i : 2 + i], axis=1, keepdims=True), (1, model))
        lines[7:8] = jnp.broadcast_to(jnp.sum(valid_ref[...].astype(F32), axis=1, keepdims=True), (1, model))
        lines[8 : 8 + HEADS] = jnp.broadcast_to(jnp.sum(bias_sum[:HEADS], axis=1, keepdims=True), (HEADS, model))
        small_got[net.f] = lines[:, seen(net.f)]
        for k in range(1, n):
            net.send(
                lines.at[:, seen(others[k])], small_got.at[net.f], small_send + k, small_recv + net.f, others[k]
            )

        in_send, in_recv = net.take(share * TP), net.take(share * TP)
        out_send, out_recv = net.take(share), net.take(share)
        over, landed = net.take(TP), net.take(TP)
        away, back_in = net.take(TP * reps), net.take(TP * reps)
        out_away, out_back = net.take(reps), net.take(reps)
        first_send, first_recv = net.take(n), net.take(n)
        mid_send, mid_recv = net.take(reps), net.take(reps)
        swap_send, swap_recv = net.take(TP * reps), net.take(TP * reps)
        for k, u in partners:
            slot, f = share - 1 - k, net.t * share + u
            for j in range(TP):
                t = chips[(j + 1) % TP]
                net.send(
                    in_part.at[owned(t, u)], in_got.at[slot, t], in_send + share * j + k, in_recv + share * t + slot, f
                )
            net.send(out_part.at[tile(u, held)], out_got.at[slot], out_send + k, out_recv + slot, f)

        replicas = [lax.rem(net.r + k, reps) for k in range(reps)]

        def owned_bit(t, r):
            start = (t * share + net.u) * held + (r * bit if cut > 1 else 0)
            return pl.ds(pl.multiple_of(start, bit), bit)

        def piece(r, t):
            return in_all.at[0, t, tile(r, bit)] if cut > 1 else in_all.at[r, t]

        def steps(start, stop):
            @pl.loop(start, stop)
            def _(j):
                for gather in gathers:
                    gather.step(DEPTH - 1 - j)

        steps(0, 1)
        for j in range(TP):
            t = chips[(j + 1) % TP]
            total = in_part[owned(t, net.u)].astype(F32)
            for slot in range(share - 1):
                net.arrive(in_got.at[slot, t], in_recv + share * t + slot)
                total = total + in_got[slot, t].astype(F32)
            in_part[owned(t, net.u)] = total.astype(BF16)
            if cut > 1:
                for k in range(1, reps):
                    net.send(
                        in_part.at[owned_bit(t, replicas[k])], swapped_in.at[net.r, t], swap_send + TP * k + j,
                        swap_recv + TP * net.r + t, net.f, r=replicas[k],
                    )
        total = out_part[tile(net.u, held)].astype(F32)
        for slot in range(share - 1):
            net.arrive(out_got.at[slot], out_recv + slot)
            total = total + out_got[slot].astype(F32)
        out_all[net.r] = total.astype(BF16)
        steps(1, 2)
        for j in range(TP):
            t = chips[(j + 1) % TP]
            here = owned_bit(t, net.r)
            if cut > 1:
                total = in_part[here].astype(F32)
                for k in range(1, reps):
                    net.arrive(swapped_in.at[replicas[k], t], swap_recv + TP * replicas[k] + t)
                    total = total + swapped_in[replicas[k], t].astype(F32)
                in_part[here] = total.astype(BF16)
            if j < TP - 1:
                net.send(in_part.at[here], piece(net.r, net.t), over + j, landed + net.t, net.place(t))
            else:
                piece(net.r, net.t)[...] = in_part[here]
        for k in range(1, reps):
            net.send(
                out_all.at[net.r], out_all.at[net.r], out_away + k, out_back + net.r, net.f, r=replicas[k]
            )
            net.send(
                piece(net.r, net.t), piece(net.r, net.t), away + k, back_in + TP * net.r + net.t, net.f, r=replicas[k]
            )
        ffn_grads()
        steps(2, DEPTH)

        layer_in = x_ref[...].astype(F32)
        scale = lax.rsqrt(jnp.mean(layer_in * layer_in, axis=-1, keepdims=True) + EPSILON)
        lifted = rows_sum[...] * gains_ref[0:1]
        mean = jnp.mean(layer_in * lifted, axis=-1, keepdims=True)
        input_ref[...] = grad_ref[...] + scale * lifted - layer_in * (scale * scale * scale) * mean
        late[...] = jnp.broadcast_to(
            jnp.sum(rows_sum[...] * layer_in * scale, axis=0, keepdims=True), (8, model)
        )
        first_got[net.f] = late[:, seen(net.f)]
        for k in range(1, n):
            net.send(
                late.at[:, seen(others[k])], first_got.at[net.f], first_send + k, first_recv + net.f, others[k]
            )
        for j in range(1, TP):
            t = chips[TP - j]
            net.arrive(piece(net.r, t), landed + t)
            for k in range(1, reps):
                net.send(
                    piece(net.r, t), piece(net.r, t), away + reps * j + k, back_in + TP * net.r + t, net.f, r=replicas[k]
                )
        for k in range(1, n):
            net.arrive(small_got.at[others[k]], small_recv + others[k])
        for t in range(TP):
            total = small_got[t * share]
            for u in range(1, share):
                total = total + small_got[t * share + u]
            small_mid[net.r, t, :ROWS] = total
        for k in range(1, n):
            net.arrive(first_got.at[others[k]], first_recv + others[k])
        for t in range(TP):
            total = first_got[t * share]
            for u in range(1, share):
                total = total + first_got[t * share + u]
            small_mid[net.r, t, ROWS:] = total
        for k in range(1, reps):
            net.send(
                small_mid.at[net.r], small_mid.at[net.r], mid_send + k, mid_recv + net.r, net.f, r=replicas[k]
            )
        for k in range(1, reps):
            r = replicas[k]
            net.arrive(out_all.at[r], out_back + r)
            for t in range(TP):
                net.arrive(piece(r, t), back_in + TP * r + t)
        for t in range(TP):
            for block in range(4):
                for column, wide, to in head_pieces(t, block):
                    total = in_all[0, t, :, to : to + wide].astype(F32)
                    for r in range(1, sheets):
                        total = total + in_all[r, t, :, to : to + wide].astype(F32)
                    in_ref[:, column : column + wide] = total
        for r in replicas[1:]:
            net.arrive(small_mid.at[r], mid_recv + r)
        total, small = out_all[0].astype(F32), small_mid[0]
        for r in range(1, reps):
            total = total + out_all[r].astype(F32)
            small = small + small_mid[r]
        out_ref[...] = total
        together = jnp.sum(small, axis=0)
        turn = lax.rem(2 * window - (net.f * held - jnp.minimum(lax.div(net.f * held, 128) * 128, model - window)), window)
        gain_rows = pltpu.roll(together, turn, 1)
        gains_out[0:1] = gain_rows[ROWS : ROWS + 1, :held]
        gains_out[1:2] = gain_rows[0:1, :held]
        mean_squares = together[4:7, :128] / (together[7:8, :128] * model)
        roots = jnp.sqrt(mean_squares + EPSILON)
        forget = jnp.zeros((128, 128), F32)
        biases = jnp.zeros((1, 128), F32)
        lane = lax.broadcasted_iota(jnp.int32, (1, 128), 1)
        for t in range(TP):
            turned = pltpu.roll(small[t], turn, 1)[:, :128]
            for h in range(HEADS):
                row = HEADS * t + h
                forget = jnp.where(
                    lax.broadcasted_iota(jnp.int32, (128, 128), 0) == row, turned[1 + h : 2 + h], forget
                )
                biases = jnp.where(lane == row, small[t, 8 + h : 9 + h, :128], biases)
        forget_ref[...] = forget[:H, :held]
        bias_ref[...] = biases[:, :H]
        stats_ref[...] = jnp.where(lane == 0, roots[0:1], jnp.where(lane == 1, roots[1:2], roots[2:3]))[:, :3]
        net.drain()
        for wave in waves:
            wave.drain()
        for gather in gathers:
            gather.drain()
        for copy in ffn_totals:
            copy.wait()

    shape = jax.ShapeDtypeStruct
    line = pltpu.VMEM((DEPTH * seq, model), BF16)
    return call(
        body, "attention_back", 5,
        (x, middle_grad, sums, valid, rows_a, proj, sig, att, prob, logit, wc, wo, wf, gains, ffn_in, ffn_down),
        [VMEM] * 4 + [ANY] * 5 + [VMEM, ANY, ANY, VMEM, VMEM, ANY, ANY],
        [
            (shape((seq, model), F32), VMEM),
            (shape((held, 4 * model), F32), VMEM),
            (shape((held, model), F32), VMEM),
            (shape((2, held), F32), VMEM),
            (shape((H, held), F32), VMEM),
            (shape((1, H), F32), VMEM),
            (shape((1, 3), F32), VMEM),
            (shape((2, model, hs), F32), ANY),
            (shape((hs, model), F32), ANY),
        ],
        [
            pltpu.VMEM((rows_all, model), BF16),
            pltpu.VMEM((rows_all, width), BF16),
            pltpu.VMEM((rows_all, 4 * HD), F32),
            pltpu.VMEM((rows_all, 4 * HD), F32),
            pltpu.VMEM((TP * HEADS, seq, seq), F32),
            pltpu.VMEM((model, width), BF16),
            pltpu.VMEM((4 * HD, model), BF16),
            pltpu.VMEM((rows_all, model), BF16),
            pltpu.VMEM((rows_all, width), BF16),
            pltpu.VMEM((rows_all, 4 * HD), BF16),
            pltpu.VMEM((rows_all, model), BF16),
            line, line, line,
            pltpu.VMEM((seq, model), F32),
            pltpu.VMEM((pair, 4 * HD), BF16),
            pltpu.VMEM((pair, 2 * HD), F32),
            pltpu.VMEM((2, ROWS, seq), BF16),
            pltpu.VMEM((ROWS, seq), F32),
            pltpu.VMEM((ROWS, model), F32),
            pltpu.VMEM((ROWS, model), F32),
            pltpu.VMEM((8, model), F32),
            pltpu.VMEM((model, width), BF16),
            pltpu.VMEM((share - 1, TP, held, width), BF16),
            pltpu.VMEM((reps, TP, bit, width) if cut > 1 else (1, 1, 16, 128), BF16),
            pltpu.VMEM((sheets, TP, held, width), BF16),
            pltpu.VMEM((4 * HD, model), BF16),
            pltpu.VMEM((share - 1, held, model), BF16),
            pltpu.VMEM((reps, held, model), BF16),
            pltpu.VMEM((n, ROWS, window), F32),
            pltpu.VMEM((n, 8, window), F32),
            pltpu.VMEM((reps, TP, ROWS + 8, window), F32),
            pltpu.VMEM((reps, model, 2 * hs), BF16),
            pltpu.VMEM((reps, hs, model), BF16),
            pltpu.VMEM((2, model, hs), F32),
            pltpu.VMEM((hs, model), F32),
            pltpu.SemaphoreType.DMA((11,)),
        ],
        20 * PIECES + 24 * PIECES + 2 * share * (TP + 1) + 2 * TP + 2 * reps * (2 * TP + 2) + 4 * n,
    )


def log_sigmoid(values_in):
    return jnp.minimum(values_in, 0.0) - jnp.log1p(jnp.exp(-jnp.abs(values_in)))


def per_device(
    reps,
    share,
    tokens,
    cotangent,
    pic_start,
    valid_mask,
    gain_attn,
    attn_in,
    forget_w,
    forget_bias,
    attn_out,
    gain_ffn,
    ffn_in,
    ffn_down,
):
    branch_attn, cot, rows_a, proj, sig, att, probability, logit, w_cols, w_rows, w_forget, gains = attention(
        reps, share, tokens[0], cotangent[0], attn_in, attn_out, forget_w.T, gain_attn[None], gain_ffn[None],
        valid_mask, pic_start, forget_bias[None],
    )
    activations, middle_grad, sums, ffn_in_sum, ffn_down_sum = feed_forward(
        reps, share, tokens[0], branch_attn, gains, valid_mask, cot, ffn_in, ffn_down
    )
    (
        input_grad, grad_in, grad_out, grad_gains, grad_forget, bias_total, stats, grad_ffn_in, grad_ffn_down,
    ) = attention_back(
        reps, share, tokens[0], middle_grad, sums, valid_mask, rows_a, proj, sig, att, probability, logit, w_cols, w_rows,
        w_forget, gains, ffn_in_sum, ffn_down_sum,
    )

    return (
        activations[None],
        input_grad[None],
        grad_gains[0],
        grad_in,
        grad_forget.T,
        bias_total[0],
        grad_out,
        grad_gains[1],
        grad_ffn_in,
        grad_ffn_down,
        stats[0],
    )


def solution(mesh):
    placed = (
        P(("rep", "fsdp"), None, None),
        P(("rep", "fsdp"), None, None),
        P(("rep", "fsdp")),
        P(("rep", "fsdp"), None),
        P("fsdp"),
        P("fsdp", None),
        P("fsdp", None),
        P(),
        P("fsdp", None),
        P("fsdp"),
        P(None, None, "fsdp"),
        P("fsdp", None),
    )
    return jax.shard_map(
        functools.partial(per_device, mesh.shape["rep"], mesh.shape["fsdp"] // TP),
        mesh=mesh,
        in_specs=placed,
        out_specs=(
            P(("rep", "fsdp"), None, None),
            P(("rep", "fsdp"), None, None),
            P("fsdp"),
            P("fsdp", None),
            P("fsdp", None),
            P(),
            P("fsdp", None),
            P("fsdp"),
            P(None, None, "fsdp"),
            P("fsdp", None),
            P(),
        ),
        check_vma=False,
    )
```

```python
import functools

import jax
import jax.numpy as jnp
from jax import lax
from jax.experimental import pallas as pl
from jax.experimental.pallas import tpu as pltpu
from jax.sharding import PartitionSpec as P

H = 24
HD = 64
PIC = 32
TP = 8
DEPTH = 4
EPSILON = 1e-06
NEGATIVE = -1e30
MESH = pl.DeviceIdType.MESH
BF16 = jnp.bfloat16
F32 = jnp.float32
VMEM = pl.BlockSpec(memory_space=pltpu.VMEM)
ANY = pl.BlockSpec(memory_space=pl.ANY)


class Net:
    def __init__(self, reps, share, sems):
        self.reps, self.share, self.sems = reps, share, sems
        self.r = lax.axis_index("rep")
        self.f = lax.axis_index("fsdp")
        self.t = lax.div(self.f, share)
        self.u = lax.rem(self.f, share)
        self.z = lax.div(self.t, 2)
        self.x = lax.rem(self.t, 2)
        self.none = self.f * 0
        self.taken = 0
        self.sent = []

    def take(self, count=1):
        base = self.taken
        self.taken += count
        return base

    def place(self, t):
        return t * self.share + self.u

    def grid(self, z, x):
        return (z * 2 + x) * self.share + self.u

    def pair(self):
        return self.z + 1 - 2 * lax.rem(self.z, 2)

    def partners(self):
        for k in range(1, self.share):
            yield k, lax.rem(self.u + k, self.share)

    def greet(self, peers):
        barrier = pltpu.get_barrier_semaphore()
        total = 0
        for cond, r, f in peers:
            if cond is None:
                pl.semaphore_signal(barrier, 1, device_id=(r, f), device_id_type=MESH)
                total = total + 1
            else:

                @pl.when(cond)
                def _():
                    pl.semaphore_signal(barrier, 1, device_id=(r, f), device_id_type=MESH)

                total = total + cond.astype(jnp.int32)
        pl.semaphore_wait(barrier, total)

    def plane_peers(self):
        return [
            (self.z < DEPTH - 1, self.r, self.grid(self.z + 1, self.x)),
            (self.z > 0, self.r, self.grid(self.z - 1, self.x)),
            (None, self.r, self.grid(self.z, 1 - self.x)),
        ]

    def share_peers(self):
        return [(None, self.r, self.t * self.share + u) for _, u in self.partners()]

    def rep_peers(self):
        return [(None, lax.rem(self.r + k, self.reps), self.f) for k in range(1, self.reps)]

    def all_plane_peers(self):
        return [(None, self.r, self.place(lax.rem(self.t + k, TP))) for k in range(1, TP)]

    def copy(self, src, dst, ssem, rsem, f, r=None):
        return pltpu.make_async_remote_copy(
            src_ref=src,
            dst_ref=dst,
            send_sem=self.sems.at[ssem],
            recv_sem=self.sems.at[rsem],
            device_id=(self.r if r is None else r, f),
            device_id_type=MESH,
        )

    def send(self, src, dst, ssem, rsem, f, r=None, cond=None):
        copy = self.copy(src, dst, ssem, rsem, f, r)
        if cond is None:
            copy.start()
        else:
            pl.when(cond)(copy.start)
        self.sent.append((cond, copy))

    def arrive(self, dst, rsem, cond=None):
        copy = pltpu.make_async_remote_copy(
            src_ref=dst,
            dst_ref=dst,
            send_sem=self.sems.at[rsem],
            recv_sem=self.sems.at[rsem],
            device_id=(self.r, self.f),
            device_id_type=MESH,
        )
        if cond is None:
            copy.wait_recv()
        else:
            pl.when(cond)(copy.wait_recv)

    def drain(self):
        for cond, copy in self.sent:
            if cond is None:
                copy.wait_send()
            else:
                pl.when(cond)(copy.wait_send)
        self.sent = []


def nearest(z, k):
    swapped = (1, 0, 2, 3)[k] if isinstance(k, int) else None
    far = lax.div(z, 2)
    edge = z + far * (3 - 2 * z)
    if swapped is None:
        inner = jnp.where(k == 0, 1, jnp.where(k == 1, 0, k))
        place = jnp.where(edge == 0, k, inner)
    else:
        place = k + edge * (swapped - k)
    return far * 3 + (1 - 2 * far) * place


class Wave:
    def __init__(self, net, block, bent=False):
        self.net, self.block, self.bent = net, block, bent
        self.recv = net.take(TP)
        self.up, self.down, self.side = net.take(DEPTH), net.take(DEPTH), net.take(DEPTH)

    def copies(self, k):
        net = self.net
        z, x = net.z, net.x
        zo = nearest(z, k)
        t = zo * 2 + x
        block, sem = self.block(t), self.recv + t
        return [
            (
                (zo <= z) & (z < DEPTH - 1),
                net.copy(block, block, self.up + k, sem, net.grid(jnp.minimum(z + 1, DEPTH - 1), x)),
            ),
            (
                (zo >= z) & (z > 0),
                net.copy(block, block, self.down + k, sem, net.grid(jnp.maximum(z - 1, 0), x)),
            ),
            (None, net.copy(block, block, self.side + k, sem, net.grid(z, 1 - x))),
        ]

    def turn(self):
        if self.bent:
            net = self.net
            t = net.z * 2 + 1 - net.x
            block, sem = self.block(t), self.recv + t
            net.arrive(block, sem)
            net.copy(block, block, self.side + 1, sem, net.grid(net.pair(), net.x)).start()

    def hand_on(self, k, own=False):
        net = self.net
        t = nearest(net.z, k) * 2 + net.x
        if not own:
            net.arrive(self.block(t), self.recv + t, None if isinstance(k, int) else k > 0)
        up, down, side = self.copies(k)
        for cond, copy in (up, down):
            pl.when(cond)(copy.start)
        if self.bent:
            pl.when(net.none + k != 1)(side[1].start)
        else:
            side[1].start()

    def across(self, k):
        t = nearest(self.net.z, k) * 2 + 1 - self.net.x
        self.net.arrive(self.block(t), self.recv + t, self.net.none + k > 0 if self.bent else None)

    def drain(self):
        @pl.loop(0, DEPTH)
        def _(k):
            for cond, copy in self.copies(k):
                if cond is None:
                    copy.wait_send()
                else:
                    pl.when(cond)(copy.wait_send)


class Gather:
    def __init__(self, net, part, side, up, down, total, bent=False):
        self.net, self.part, self.side, self.up, self.down, self.total = net, part, side, up, down, total
        self.bent = bent
        self.sems = [net.take(DEPTH) for _ in range(6)]

    def across(self, k):
        net = self.net
        zo = nearest(net.z, k)
        return net.copy(
            self.part(zo * 2 + 1 - net.x), self.side(zo), self.sems[0] + zo, self.sems[1] + zo,
            net.grid(net.z, 1 - net.x),
        )

    def along(self, k):
        net = self.net
        z = net.z
        zo = nearest(z, k)
        part = self.part(zo * 2 + net.x)
        return [
            (
                zo > z,
                net.copy(
                    part, self.up(zo), self.sems[2] + zo, self.sems[3] + zo,
                    net.grid(jnp.minimum(z + 1, DEPTH - 1), net.x),
                ),
            ),
            (
                zo < z,
                net.copy(
                    part, self.down(zo), self.sems[4] + zo, self.sems[5] + zo,
                    net.grid(jnp.maximum(z - 1, 0), net.x),
                ),
            ),
        ]

    def begin(self, k):
        net = self.net
        z, pair = net.z, net.pair()
        if self.bent and k == 1:
            net.copy(
                self.part(pair * 2 + 1 - net.x), self.side(z), self.sems[0] + pair, self.sems[1] + z,
                net.grid(pair, net.x),
            ).start()
            return
        if self.bent and k == 0:
            net.arrive(self.side(pair), self.sems[1] + pair)
            part = self.part(z * 2 + 1 - net.x)
            part[...] = (part[...].astype(F32) + self.side(pair)[...].astype(F32)).astype(BF16)
        self.across(k).start()

    def step(self, k):
        net = self.net
        z = net.z
        zo = nearest(z, k)
        part = self.part(zo * 2 + net.x)
        if self.bent:
            self.total[...] = part[...].astype(F32)

            @pl.when(k != 1)
            def _():
                net.arrive(self.side(zo), self.sems[1] + zo)
                self.total[...] += self.side(zo)[...].astype(F32)
        else:
            net.arrive(self.side(zo), self.sems[1] + zo)
            self.total[...] = part[...].astype(F32) + self.side(zo)[...].astype(F32)
        for cond, ref, sem in (
            ((zo >= z) & (z > 0), self.up(zo), self.sems[3]),
            ((zo <= z) & (z < DEPTH - 1), self.down(zo), self.sems[5]),
        ):

            @pl.when(cond)
            def _():
                net.arrive(ref, sem + zo)
                self.total[...] += ref[...].astype(F32)

        @pl.when(zo != z)
        def _():
            part[...] = self.total[...].astype(BF16)

        for cond, copy in self.along(k):
            pl.when(cond)(copy.start)

    def drain(self):
        @pl.loop(0, DEPTH)
        def _(k):
            self.across(k).wait_send()
            for cond, copy in self.along(k):
                pl.when(cond)(copy.wait_send)


def column(row):
    size = row.shape[1]
    square = (size, size)
    same = lax.broadcasted_iota(jnp.int32, square, 0) == lax.broadcasted_iota(jnp.int32, square, 1)
    return jnp.sum(jnp.where(same, row, 0.0), axis=1, keepdims=True)


def step_order(j):
    return DEPTH - 1 - j + jnp.where(j == 1, 1, 0) - jnp.where(j == 0, 1, 0)


def begin_last(gathers, bent):
    for gather in gathers:
        if gather.bent == bent:
            gather.begin(0)


def call(body, name, number, operands, in_specs, outs, scratch, sems, limit=60 << 20):
    return pl.pallas_call(
        body,
        name=name,
        out_shape=tuple(shape for shape, _ in outs),
        in_specs=in_specs,
        out_specs=tuple(spec for _, spec in outs),
        scratch_shapes=list(scratch) + [pltpu.SemaphoreType.DMA((sems,))],
        compiler_params=pltpu.CompilerParams(
            collective_id=number, has_side_effects=True, vmem_limit_bytes=limit
        ),
    )(*operands)


def chunk(rows, count, c):
    return pl.ds(c * (rows // count), rows // count)


def matmul_nt(a, b):
    return lax.dot_general(a, b, (((1,), (1,)), ((), ())), preferred_element_type=F32)


def matmul_tn(a, b):
    return lax.dot_general(a, b, (((0,), (0,)), ((), ())), preferred_element_type=F32)


def matmul(a, b):
    return jnp.dot(a, b, preferred_element_type=F32)


def tile(j, size):
    return pl.ds(pl.multiple_of(j * size, size), size)


PIECES = 2


def feed_forward(reps, share, x, branch, gain, valid, cot, w_in, w_down):
    seq, model = x.shape
    hs = w_in.shape[2]
    hidden_all = share * hs
    rows_all = TP * seq
    pair = 2 * seq
    half = seq // PIECES

    def body(
        x_ref, branch_ref, gain_ref, valid_ref, cot_ref, in_ref, down_ref,
        act_ref, grad_ref, sums_ref, in_out, down_out,
        middle, rows, cot_all, w_all, wd, hid, grads, part, side, up, down, rows_sum, ffn_sum,
        in_part, down_part, in_got, down_got, local, sems,
    ):
        net = Net(reps, share, sems)
        own = [
            pltpu.make_async_copy(in_ref.at[0], w_all.at[:, pl.ds(0, hs)], local.at[0]),
            pltpu.make_async_copy(in_ref.at[1], w_all.at[:, pl.ds(hs, hs)], local.at[1]),
            pltpu.make_async_copy(down_ref, wd.at[pl.ds(0, hs)], local.at[2]),
            pltpu.make_async_copy(cot_ref, cot_all, local.at[3]),
        ]
        for copy in own:
            copy.start()

        def block(ref, t):
            return ref.at[tile(t, seq)]

        middle[...] = x_ref[...].astype(F32) + branch_ref[...]
        scale = lax.rsqrt(jnp.mean(middle[...] * middle[...], axis=-1, keepdims=True) + EPSILON)
        block(rows, net.t)[...] = (middle[...] * scale * gain_ref[1:2]).astype(BF16)
        net.greet(net.plane_peers() + net.share_peers() + net.rep_peers())

        waves = [
            Wave(net, lambda t, c=c: rows.at[pl.ds(pl.multiple_of(t * seq + c * half, half), half)])
            for c in range(PIECES)
        ]
        weights = net.take(3 * share), net.take(3 * share)
        for wave in waves:
            wave.hand_on(0, own=True)
        arriving = []
        for k, u in net.partners():
            f, p = net.t * share + u, share - k
            for j, (src, dst) in enumerate(
                [
                    (in_ref.at[0], w_all.at[:, pl.ds(2 * hs * p, hs)]),
                    (in_ref.at[1], w_all.at[:, pl.ds(2 * hs * p + hs, hs)]),
                    (down_ref, wd.at[pl.ds(hs * p, hs)]),
                ]
            ):
                net.send(src, dst, weights[0] + 3 * k + j, weights[1] + 3 * p + j, f)
                arriving.append((dst, weights[1] + 3 * p + j))

        def unit(k):
            at = tile(nearest(net.z, k), pair)
            projected = matmul(rows[at], w_all[...])
            hidden_grad = matmul_nt(cot_all[at], wd[...])
            for p in range(share):
                gate = projected[:, 2 * hs * p : 2 * hs * p + hs]
                lift = projected[:, 2 * hs * p + hs : 2 * hs * (p + 1)]
                back = hidden_grad[:, hs * p : hs * (p + 1)]
                sig = jax.nn.sigmoid(gate)
                silu = gate * sig
                hid[at, hs * p : hs * (p + 1)] = (silu * lift).astype(BF16)
                grads[at, 2 * hs * p : 2 * hs * p + hs] = (
                    back * lift * sig * (1.0 + gate * (1.0 - sig))
                ).astype(BF16)
                grads[at, 2 * hs * p + hs : 2 * hs * (p + 1)] = (back * silu).astype(BF16)

            @pl.loop(0, 3)
            def _(j):
                to = tile(j, model // 3)
                part[0, at, to] = matmul_nt(grads[at], w_all[to]).astype(BF16)
                part[1, at, to] = matmul(hid[at], wd[:, to]).astype(BF16)

        def piece(ref, i, c, count):
            return lambda j: ref.at[i, pl.ds(pl.multiple_of(j * seq + c * half, half), half)]

        gathers = [
            [
                Gather(
                    net, piece(part, i, c, TP), piece(side, i, c, DEPTH), piece(up, i, c, DEPTH),
                    piece(down, i, c, DEPTH), total.at[pl.ds(c * half, half)],
                )
                for c in range(PIECES)
            ]
            for i, total in enumerate((rows_sum, ffn_sum))
        ]
        @pl.loop(1, DEPTH + 1)
        def _(k):
            @pl.when(k < DEPTH)
            def _():
                for wave in waves:
                    wave.hand_on(k)

            @pl.when(k == 1)
            def _():
                for wave in waves:
                    wave.turn()
                for copy in own:
                    copy.wait()
                for dst, sem in arriving:
                    net.arrive(dst, sem)

            for wave in waves:
                wave.across(k - 1)

            @pl.when(k == DEPTH)
            def _():
                for gather in gathers[0]:
                    gather.begin(DEPTH - 2)

            unit(k - 1)

        for k in (DEPTH - 1, *range(DEPTH - 3, 0, -1)):
            for gather in gathers[0]:
                gather.begin(k)
        begin_last(gathers[0], False)

        @pl.loop(0, model // 256)
        def _(j):
            at = tile(j, 256)
            in_part[at] = matmul_tn(rows[:, at], grads[...]).astype(BF16)

        begin_last(gathers[0], True)
        for k in range(DEPTH - 1, 0, -1):
            for gather in gathers[1]:
                gather.begin(k)
        begin_last(gathers[1], False)

        @pl.loop(0, 3)
        def _(j):
            at = tile(j, model // 3)
            down_part[:, at] = matmul_tn(hid[...], cot_all[:, at]).astype(BF16)

        first, arrived = net.take(2 * share), net.take(2 * share)
        away, back = net.take(2 * reps), net.take(2 * reps)
        for k, u in net.partners():
            f, slot = net.t * share + u, share - 1 - k
            net.send(
                in_part.at[:, pl.ds(2 * hs * k, 2 * hs)], in_got.at[slot], first + 2 * k, arrived + 2 * slot, f
            )
            net.send(
                down_part.at[pl.ds(hs * k, hs)], down_got.at[slot], first + 2 * k + 1, arrived + 2 * slot + 1, f
            )

        def own_grads():
            for slot in range(share - 1):
                net.arrive(in_got.at[slot], arrived + 2 * slot)
                net.arrive(down_got.at[slot], arrived + 2 * slot + 1)

            @pl.loop(0, model // 256)
            def _(j):
                at = tile(j, 256)
                total = in_part[at, : 2 * hs].astype(F32)
                for slot in range(share - 1):
                    total = total + in_got[slot, at].astype(F32)
                in_out[net.r, at] = total.astype(BF16)

            total = down_part[:hs].astype(F32)
            for slot in range(share - 1):
                total = total + down_got[slot].astype(F32)
            down_out[net.r] = total.astype(BF16)
            for k in range(1, reps):
                r = lax.rem(net.r + k, reps)
                net.send(in_out.at[net.r], in_out.at[net.r], away + 2 * k, back + 2 * net.r, net.f, r=r)
                net.send(down_out.at[net.r], down_out.at[net.r], away + 2 * k + 1, back + 2 * net.r + 1, net.f, r=r)

        def steps(both, start, stop):
            @pl.loop(start, stop)
            def _(j):
                for gather in both:
                    gather.step(DEPTH - 1 - j)

        steps(gathers[0], 0, 2)
        begin_last(gathers[1], True)
        own_grads()
        steps(gathers[0], 2, DEPTH)
        steps(gathers[1], 0, DEPTH)

        result = middle[...] + ffn_sum[...]
        act_ref[...] = result.astype(BF16)
        valid_col = column(valid_ref[...].astype(F32))
        scale = lax.rsqrt(jnp.mean(middle[...] * middle[...], axis=-1, keepdims=True) + EPSILON)
        lifted = rows_sum[...] * gain_ref[1:2]
        mean = jnp.mean(middle[...] * lifted, axis=-1, keepdims=True)
        grad_ref[...] = (
            block(cot_all, net.t)[...].astype(F32) + scale * lifted - middle[...] * (scale * scale * scale) * mean
        )
        sums_ref[...] = jnp.zeros_like(sums_ref)
        sums_ref[0:1] = jnp.sum(rows_sum[...] * middle[...] * scale, axis=0, keepdims=True)
        sums_ref[1:2] = jnp.sum(result * result * valid_col, axis=0, keepdims=True)
        sums_ref[2:3] = jnp.sum(branch_ref[...] * branch_ref[...] * valid_col, axis=0, keepdims=True)
        sums_ref[3:4] = jnp.sum(ffn_sum[...] * ffn_sum[...] * valid_col, axis=0, keepdims=True)
        for k in range(1, reps):
            r = lax.rem(net.r + k, reps)
            net.arrive(in_out.at[r], back + 2 * r)
            net.arrive(down_out.at[r], back + 2 * r + 1)
        net.drain()
        for wave in waves:
            wave.drain()
        for gather in gathers[0] + gathers[1]:
            gather.drain()

    shape = jax.ShapeDtypeStruct
    line = pltpu.VMEM((2, DEPTH * seq, model), BF16)
    return call(
        body, "feed_forward", 3, (x, branch, gain, valid, cot, w_in, w_down), [VMEM] * 4 + [ANY] * 3,
        [
            (shape((seq, model), BF16), VMEM),
            (shape((seq, model), F32), VMEM),
            (shape((8, model), F32), VMEM),
            (shape((reps, model, 2 * hs), BF16), VMEM),
            (shape((reps, hs, model), BF16), VMEM),
        ],
        [
            pltpu.VMEM((seq, model), F32),
            pltpu.VMEM((rows_all, model), BF16),
            pltpu.VMEM((rows_all, model), BF16),
            pltpu.VMEM((model, 2 * hidden_all), BF16),
            pltpu.VMEM((hidden_all, model), BF16),
            pltpu.VMEM((rows_all, hidden_all), BF16),
            pltpu.VMEM((rows_all, 2 * hidden_all), BF16),
            pltpu.VMEM((2, rows_all, model), BF16),
            line, line, line,
            pltpu.VMEM((seq, model), F32),
            pltpu.VMEM((seq, model), F32),
            pltpu.VMEM((model, 2 * hidden_all), BF16),
            pltpu.VMEM((hidden_all, model), BF16),
            pltpu.VMEM((share - 1, model, 2 * hs), BF16),
            pltpu.VMEM((share - 1, hs, model), BF16),
            pltpu.SemaphoreType.DMA((4,)),
        ],
        40 * PIECES + 24 * 2 * PIECES + 20 * share + 10 * reps,
    )


HEADS = H // TP
ROWS = 16


def cuts(reps, held):
    return reps if held % (16 * reps) == 0 else 1


def lane_mask(shape, low, high):
    lane = lax.broadcasted_iota(jnp.int32, shape, 1)
    return (lane >= low) & (lane < high)


def head_pieces(t, block):
    base = block * H * HD + t * HEADS * HD
    return [(base, 2 * HD, block * 2 * HD), (base + 2 * HD, HD, 8 * HD + block * HD)]


def attention(reps, share, x, cot, w_in, w_out, forget, gain_a, gain_f, mask, start, bias):
    n = TP * share
    seq, model = x.shape
    held = w_in.shape[0]
    width = 4 * HEADS * HD
    rows_all = TP * seq
    pair = 2 * seq
    half = seq // PIECES
    last = HEADS - 1
    cut = cuts(reps, held)

    def body(
        x_ref, cot_ref, in_ref, out_ref, forget_ref, gain_a_ref, gain_f_ref, mask_ref, start_ref, bias_ref,
        branch_ref, cot_out, rows_out, proj_out, sig_out, att_out, prob_out, logit_ref, wc_out, wo_out, wf_ref, gains_ref,
        xs, cots, rows, proj, sig, att, prob, wc, wo, split, smalls, lines, part, side, up, down, gated, local, sems,
    ):
        net = Net(reps, share, sems)

        def seq_block(ref, t):
            return ref.at[tile(t, seq)]

        def held_rows(f):
            return wc.at[tile(f, held)]

        def spot(r):
            return r if cut > 1 else 0

        def piece_of(r):
            return tile(spot(r), held // cut)

        def held_piece(f, r):
            return wc.at[pl.ds(pl.multiple_of(f * held + spot(r) * (held // cut), held // cut), held // cut)]

        own = [
            pltpu.make_async_copy(x_ref, seq_block(xs, net.t), local.at[0]),
            pltpu.make_async_copy(cot_ref, seq_block(cots, net.t), local.at[1]),
            pltpu.make_async_copy(out_ref, wo.at[tile(net.u, held)], local.at[3]),
        ]
        for copy in own:
            copy.start()
        small = lines.at[:, pl.ds(0, 128)]
        small[...] = jnp.zeros((32, 128), F32)
        small[:H, :held] = forget_ref[...].astype(F32)
        small[H : H + 1, :held] = gain_a_ref[...].astype(F32)
        small[H + 1 : H + 2, :held] = gain_f_ref[...].astype(F32)
        small[H + 2 : H + 3, :seq] = mask_ref[...].astype(F32)
        small[H + 3 : H + 4, :seq] = jnp.full((1, seq), start_ref[0], jnp.int32).astype(F32)
        smalls[net.f] = small[...].astype(BF16)
        for t in range(TP):
            for block in range(4):
                for column, wide, to in head_pieces(t, block):
                    split[t, :, to : to + wide] = in_ref[:, column : column + wide]
        wo[share * held :] = jnp.zeros((wo.shape[0] - share * held, model), BF16)
        others = [lax.rem(net.f + k, n) for k in range(n)]
        chips = [lax.rem(net.t + k, TP) for k in range(TP)]
        partners = list(net.partners())
        replicas = [lax.rem(net.r + k, reps) for k in range(reps)]
        net.greet([(None, net.r, f) for f in others[1:]] + [(None, r, net.f) for r in replicas[1:cut]])

        small_send, small_recv = net.take(n), net.take(n)
        w_send, w_recv = net.take(TP), net.take(n * cut)
        w_pass = net.take(share * TP * (cut + 1))
        w_away = net.take(TP * cut)
        wo_send, wo_recv = net.take(share), net.take(share)
        for k in range(1, n):
            net.send(smalls.at[net.f], smalls.at[net.f], small_send + k, small_recv + net.f, others[k])
        for k in range(1, TP):
            net.send(
                split.at[chips[k], piece_of(net.r)], held_piece(net.f, net.r), w_send + k, w_recv + cut * net.f + spot(net.r),
                net.place(chips[k]),
            )
        own_cols = pltpu.make_async_copy(split.at[net.t], held_rows(net.f), local.at[4])
        own_cols.start()
        for k, u in partners:
            f = net.t * share + u
            net.send(split.at[net.t], held_rows(net.f), w_pass + k, w_recv + cut * net.f, f)
            net.send(out_ref, wo.at[tile(net.u, held)], wo_send + k, wo_recv + net.u, f)

        def pieces(ref):
            return [
                Wave(net, lambda t, c=c: ref.at[pl.ds(pl.multiple_of(t * seq + c * half, half), half)])
                for c in range(PIECES)
            ]

        waves, cot_waves = pieces(xs), pieces(cots)
        for copy in own:
            copy.wait()
        for wave in waves:
            wave.hand_on(0, own=True)
        for wave in cot_waves:
            wave.copies(0)[2][1].start()

        def weights():
            for q in range(cut):
                r = replicas[q]
                for k in range(1, TP):
                    source = net.place(chips[k])
                    got, sem = held_piece(source, r), w_recv + cut * source + spot(r)
                    net.arrive(got, sem)
                    for j, u in partners:
                        net.send(got, got, w_pass + share * (TP * (q + 1) + k) + j, sem, net.t * share + u)
                    for p in range(1, cut if q == 0 else 1):
                        net.send(got, got, w_away + TP * p + k, sem, net.f, r=replicas[p])
                if q == 0:
                    for wave in waves:
                        wave.hand_on(2)
            for k in range(1, n):
                net.arrive(smalls.at[others[k]], small_recv + others[k])
            for j in range(model // 128):
                line = jnp.zeros((32, 128), F32)
                for f in range(j * 128 // held, ((j + 1) * 128 - 1) // held + 1):
                    start = f * held - j * 128
                    piece = pltpu.roll(smalls[f].astype(F32), net.none + start % 128, 1)
                    line = jnp.where(lane_mask((32, 128), start, start + held), piece, line)
                lines[:, j * 128 : (j + 1) * 128] = line
            pick = lax.broadcasted_iota(jnp.int32, (ROWS, 32), 0) + HEADS * net.t
            pick = pick == lax.broadcasted_iota(jnp.int32, (ROWS, 32), 1)
            pick &= lax.broadcasted_iota(jnp.int32, (ROWS, 32), 0) < HEADS
            wf_ref[...] = matmul(pick.astype(BF16), lines[...].astype(BF16)).astype(BF16)
            gains_ref[...] = lines[H : H + 8]
            for k, u in partners:
                net.arrive(wo.at[tile(u, held)], wo_recv + u)
                net.arrive(held_rows(net.t * share + u), w_recv + cut * (net.t * share + u))
                for k in range(1, TP):
                    f = chips[k] * share + u
                    for r in replicas[:cut]:
                        net.arrive(held_piece(f, r), w_recv + cut * f + spot(r))
            own_cols.wait()

        own_head = lax.broadcasted_iota(jnp.int32, (ROWS, H), 0)
        picked = own_head + HEADS * net.t == lax.broadcasted_iota(jnp.int32, (ROWS, H), 1)
        bias_col = jnp.sum(
            jnp.where(picked & (own_head < HEADS), bias_ref[...].astype(F32), 0.0), axis=1, keepdims=True
        )
        few = (ROWS, ROWS)
        same = lax.broadcasted_iota(jnp.int32, few, 0) == lax.broadcasted_iota(jnp.int32, few, 1)
        bias_row = jnp.sum(jnp.where(same, bias_col, 0.0), axis=0, keepdims=True)
        square = (seq, seq)
        at_row = lax.broadcasted_iota(jnp.int32, square, 0)
        at_col = lax.broadcasted_iota(jnp.int32, square, 1)

        def unit(k):
            place = nearest(net.z, k)
            at = tile(place, pair)
            values_in = xs[at].astype(F32)
            inverse = lax.rsqrt(jnp.mean(values_in * values_in, axis=-1, keepdims=True) + EPSILON)
            rows[at] = (values_in * inverse * gains_ref[0:1]).astype(BF16)
            projected = matmul(rows[at], wc[...])
            proj[at] = projected.astype(BF16)
            sig[at, : 2 * HD] = jax.nn.sigmoid(projected[:, 6 * HD : 8 * HD])
            tail = pltpu.roll(jax.nn.sigmoid(projected[:, 10 * HD : 12 * HD]), net.none + HD, 1)
            sig[at, 2 * HD :] = jnp.where(lane_mask(tail.shape, 0, HD), tail, 0.0)

            @pl.loop(0, 2, unroll=True)
            def _(j):
                t = place * 2 + j
                here = tile(t, seq)
                marks = smalls[net.place(t)].astype(F32)
                valid = marks[H + 2 : H + 3]
                start = marks[H + 3 : H + 4].astype(jnp.int32)
                causal = at_col <= at_row
                inside = (at_row >= start) & (at_row < start + PIC) & (at_col >= start) & (at_col < start + PIC)
                allowed = (causal | inside) & (valid > 0.0)
                sign = jnp.where(causal, 1.0, -1.0)
                below = sign * 0.5 + 0.5
                logit_col = matmul_nt(rows[here], wf_ref[...]) + bias_row
                logit_row = matmul_nt(wf_ref[...], rows[here]) + bias_col
                logit_ref[t] = logit_row
                decay_col = jnp.dot(
                    below, log_sigmoid(logit_col), precision=lax.Precision.HIGHEST, preferred_element_type=F32
                )
                decay_row = lax.dot_general(
                    log_sigmoid(logit_row), below, (((1,), (1,)), ((), ())),
                    precision=lax.Precision.HIGHEST, preferred_element_type=F32,
                )
                outs = []
                for h in range(HEADS):
                    if h < last:
                        query = jnp.where(lane_mask((seq, 2 * HD), h * HD, h * HD + HD), proj[here, : 2 * HD], 0)
                        key, value = proj[here, 2 * HD : 4 * HD], proj[here, 4 * HD : 6 * HD]
                    else:
                        query = jnp.where(lane_mask((seq, 2 * HD), 0, HD), proj[here, 8 * HD : 10 * HD], 0)
                        key = pltpu.roll(proj[here, 8 * HD : 10 * HD].astype(F32), net.none + HD, 1).astype(BF16)
                        value = proj[here, 10 * HD :]
                    scores = matmul_nt(query, key) * HD ** (-0.5)
                    scores = scores + sign * (decay_col[:, h : h + 1] - decay_row[h : h + 1])
                    masked = jnp.where(allowed, scores, NEGATIVE)
                    weights_now = jnp.exp(masked - jnp.max(masked, axis=-1, keepdims=True))
                    probability = weights_now / jnp.sum(weights_now, axis=-1, keepdims=True)
                    prob[t * HEADS + h] = probability
                    outs.append(matmul(probability.astype(BF16), value))
                low = lane_mask((seq, 2 * HD), 0, HD)
                att[here, : 2 * HD] = jnp.where(low, outs[0], outs[1])
                att[here, 2 * HD :] = jnp.where(low, outs[2], 0.0)

            gated[...] = (att[at] * sig[at]).astype(BF16)

            @pl.loop(0, 3)
            def _(j):
                to = tile(j, model // 3)
                part[at, to] = matmul(gated[...], wo[:, to]).astype(BF16)

        gathers = [
            Gather(
                net,
                *[
                    lambda j, ref=ref, c=c: ref.at[pl.ds(pl.multiple_of(j * seq + c * half, half), half)]
                    for ref in (part, side, up, down)
                ],
                branch_ref.at[pl.ds(c * half, half)],
            )
            for c in range(PIECES)
        ]

        for wave in waves:
            wave.hand_on(1)
            wave.turn()
        weights()

        @pl.loop(1, DEPTH + 1)
        def _(k):
            @pl.when(k == 2)
            def _():
                for wave in waves:
                    wave.hand_on(DEPTH - 1)
                for wave in cot_waves:
                    for cond, copy in wave.copies(0)[:2]:
                        pl.when(cond)(copy.start)
                    wave.turn()

            @pl.when(k == 3)
            def _():
                for wave in cot_waves:
                    wave.hand_on(1)

            for wave in waves:
                wave.across(k - 1)

            @pl.when(k == DEPTH - 1)
            def _():
                for gather in gathers:
                    gather.begin(1)

            @pl.when(k == DEPTH)
            def _():
                for gather in gathers:
                    gather.begin(DEPTH - 2)
                for wave in cot_waves:
                    wave.hand_on(2)

            unit(k - 1)

        keep = [
            pltpu.make_async_copy(src, dst, local.at[5 + i])
            for i, (src, dst) in enumerate(
                [
                    (rows, rows_out), (proj, proj_out), (sig, sig_out), (att, att_out), (prob, prob_out),
                    (wc, wc_out), (wo, wo_out),
                ]
            )
        ]
        for gather in gathers:
            gather.begin(DEPTH - 1)
        begin_last(gathers, False)

        for copy in keep:
            copy.start()

        @pl.loop(0, DEPTH)
        def _(j):
            for gather in gathers:
                gather.step(step_order(j))

            @pl.when(j == 0)
            def _():
                begin_last(gathers, True)

            @pl.when(j == 0)
            def _():
                for wave in cot_waves:
                    wave.hand_on(DEPTH - 1)

        for k in range(DEPTH):
            for wave in cot_waves:
                wave.across(k)
        save = pltpu.make_async_copy(cots, cot_out, local.at[1])
        save.start()
        net.drain()
        for wave in waves + cot_waves:
            wave.drain()
        for gather in gathers:
            gather.drain()
        for copy in keep:
            copy.wait()
        save.wait()

    shape = jax.ShapeDtypeStruct
    line = pltpu.VMEM((DEPTH * seq, model), BF16)
    kept = [
        ((rows_all, model), BF16),
        ((rows_all, model), BF16),
        ((rows_all, width), BF16),
        ((rows_all, 4 * HD), F32),
        ((rows_all, 4 * HD), F32),
        ((TP * HEADS, seq, seq), F32),
    ]
    return call(
        body, "attention", 1, (x, cot, w_in, w_out, forget, gain_a, gain_f, mask, start, bias),
        [ANY, ANY, VMEM, ANY, VMEM, VMEM, VMEM, VMEM, pl.BlockSpec(memory_space=pltpu.SMEM), VMEM],
        [(shape((seq, model), F32), VMEM)]
        + [(shape(*what), ANY) for what in kept]
        + [
            (shape((TP, ROWS, seq), F32), VMEM),
            (shape((model, width), BF16), ANY),
            (shape((4 * HD, model), BF16), ANY),
            (shape((ROWS, model), BF16), VMEM),
            (shape((8, model), F32), VMEM),
        ],
        [pltpu.VMEM((rows_all, model), BF16)]
        + [pltpu.VMEM(*what) for what in kept]
        + [
            pltpu.VMEM((model, width), BF16),
            pltpu.VMEM((4 * HD, model), BF16),
            pltpu.VMEM((TP, held, width), BF16),
            pltpu.VMEM((n, 32, 128), BF16),
            pltpu.VMEM((32, model), F32),
            pltpu.VMEM((rows_all, model), BF16),
            line, line, line,
            pltpu.VMEM((pair, 4 * HD), BF16),
            pltpu.SemaphoreType.DMA((12,)),
        ],
        2 * 20 * PIECES + 24 * PIECES + (2 + cut) * n + (1 + cut) * (TP + share * TP) + 2 * share,
    )


def attention_back(
    reps, share, x, middle_grad, sums, valid, rows_a, proj, sig, att, prob, logit, wc, wo, wf, gains,
    ffn_in, ffn_down,
):
    n = TP * share
    seq, model = x.shape
    width = 4 * HEADS * HD
    held = model // n
    rows_all = TP * seq
    pair = 2 * seq
    half = seq // PIECES
    last = HEADS - 1
    window = 256
    cut = cuts(reps, held)
    bit = held // cut
    sheets = 1 if cut > 1 else reps
    hs = ffn_down.shape[1]

    def body(
        x_ref, grad_ref, sums_ref, valid_ref, rows_in, proj_in, sig_in, att_in, prob_in, logit_ref, wc_in, wo_in, wf_ref,
        gains_ref, ffn_in_ref, ffn_down_ref,
        input_ref, in_ref, out_ref, gains_out, forget_ref, bias_ref, stats_ref, ffn_in_out, ffn_down_out,
        rows, proj, sig, att, prob, wcs, wos, bgs, pg, gated, part, side, up, down, rows_sum, ag, og, low_logit, bias_sum,
        forget_sum, lines, late, in_part, in_got, swapped_in, in_all, out_part, out_got, out_all, small_got, first_got,
        small_mid, ffn_in, ffn_down, ffn_in_sum, ffn_down_sum, local, sems,
    ):
        net = Net(reps, share, sems)
        others = [lax.rem(net.f + k, n) for k in range(n)]
        chips = [lax.rem(net.t + k, TP) for k in range(TP)]
        partners = list(net.partners())
        own = [
            pltpu.make_async_copy(src, dst, local.at[i])
            for i, (src, dst) in enumerate(
                [
                    (wo_in, wos), (sig_in, sig), (att_in, att), (proj_in, proj), (prob_in, prob), (rows_in, rows),
                    (wc_in, wcs),
                ]
            )
        ]
        ffn_parts = [
            pltpu.make_async_copy(ffn_in_ref, ffn_in, local.at[7]),
            pltpu.make_async_copy(ffn_down_ref, ffn_down, local.at[8]),
        ]
        ffn_totals = [
            pltpu.make_async_copy(ffn_in_sum, ffn_in_out, local.at[9]),
            pltpu.make_async_copy(ffn_down_sum, ffn_down_out, local.at[10]),
        ]
        for copy in own + ffn_parts:
            copy.start()
        bgs[tile(net.t, seq)] = grad_ref[...].astype(BF16)
        net.greet([(None, net.r, f) for f in others[1:]] + net.rep_peers())
        waves = [
            Wave(net, lambda t, c=c: bgs.at[pl.ds(pl.multiple_of(t * seq + c * half, half), half)], c == 1)
            for c in range(PIECES)
        ]
        for wave in waves:
            wave.hand_on(0, own=True)
        bias_sum[...] = jnp.zeros_like(bias_sum)
        forget_sum[...] = jnp.zeros_like(forget_sum)
        for copy in own:
            copy.wait()

        square = (seq, seq)
        causal = lax.broadcasted_iota(jnp.int32, square, 1) <= lax.broadcasted_iota(jnp.int32, square, 0)
        below = jnp.where(causal, 1.0, 0.0)
        low = lane_mask((seq, 2 * HD), 0, HD)
        head_row = lax.broadcasted_iota(jnp.int32, (ROWS, seq), 0)

        def unit(k):
            place = nearest(net.z, k)
            at = tile(place, pair)
            gated_grad = matmul_nt(bgs[at], wos[...])
            gate, attended = sig[at], att[at]
            ag[...] = (gated_grad * gate).astype(BF16)
            gated[at] = (attended * gate).astype(BF16)
            gate_grad = gated_grad * attended * (gate * (1.0 - gate))
            pg[at, 6 * HD : 8 * HD] = gate_grad[:, : 2 * HD].astype(BF16)
            og[...] = pltpu.roll(gate_grad[:, 2 * HD :], net.none + HD, 1)

            @pl.loop(0, 2, unroll=True)
            def _(j):
                t = place * 2 + j
                here = tile(t, seq)
                inner = tile(j, seq)
                swapped = pltpu.roll(proj[here, 8 * HD : 10 * HD].astype(F32), net.none + HD, 1).astype(BF16)
                decay_grad = jnp.zeros((ROWS, seq), F32)
                found = []
                for h in range(HEADS):
                    probability = prob[t * HEADS + h]
                    if h < last:
                        back_all = ag[inner, : 2 * HD]
                        back = jnp.where(lane_mask((seq, 2 * HD), h * HD, h * HD + HD), back_all, 0)
                        query, key, value = (proj[here, 2 * HD * i : 2 * HD * (i + 1)] for i in range(3))
                    else:
                        back = back_all = ag[inner, 2 * HD :]
                        query, key, value = swapped, swapped, proj[here, 10 * HD :]
                    prob_grad = matmul_nt(back, value)
                    score_grad = probability * (
                        prob_grad - jnp.sum(probability * prob_grad, axis=-1, keepdims=True)
                    )
                    dotted_grad = (score_grad * HD ** (-0.5)).astype(BF16)
                    found.append(
                        (
                            matmul(dotted_grad, key),
                            matmul_tn(dotted_grad, query),
                            matmul_tn(probability.astype(BF16), back_all),
                        )
                    )
                    signed = jnp.where(causal, score_grad, -score_grad)
                    line = jnp.sum(signed.T - signed, axis=0, keepdims=True)
                    decay_grad = jnp.where(head_row == h, line, decay_grad)
                for i in range(3):
                    pg[here, 2 * HD * i : 2 * HD * (i + 1)] = jnp.where(low, found[0][i], found[1][i]).astype(BF16)
                pg[here, 8 * HD : 10 * HD] = jnp.where(low, found[2][0], found[2][1]).astype(BF16)
                pg[here, 10 * HD :] = jnp.where(low, found[2][2], og[inner]).astype(BF16)
                later = jnp.dot(decay_grad, below, precision=lax.Precision.HIGHEST, preferred_element_type=F32)
                logit_grad = later * jax.nn.sigmoid(-logit_ref[t])
                bias_sum[...] += logit_grad
                low_logit[j] = logit_grad.astype(BF16)
                forget_sum[...] += matmul(logit_grad.astype(BF16), rows[here])

            @pl.loop(0, 3)
            def _(i):
                to = tile(i, model // 3)
                main = matmul_nt(pg[at], wcs[to])
                for j in range(2):
                    extra = matmul_tn(low_logit[j], wf_ref[:, to])
                    part[tile(place * 2 + j, seq), to] = (main[j * seq : (j + 1) * seq] + extra).astype(BF16)

        gathers = [
            Gather(
                net,
                *[
                    lambda j, ref=ref, c=c: ref.at[pl.ds(pl.multiple_of(j * seq + c * half, half), half)]
                    for ref in (part, side, up, down)
                ],
                rows_sum.at[pl.ds(c * half, half)], c == 1,
            )
            for c in range(PIECES)
        ]

        @pl.loop(1, DEPTH + 1)
        def _(k):
            @pl.when(k < DEPTH)
            def _():
                for wave in waves:
                    wave.hand_on(k)

            @pl.when(k == 1)
            def _():
                for wave in waves:
                    wave.turn()

            for wave in waves:
                wave.across(k - 1)

            @pl.when(k == DEPTH - 1)
            def _():
                for gather in gathers:
                    gather.begin(1)

            @pl.when(k == DEPTH)
            def _():
                for gather in gathers:
                    gather.begin(DEPTH - 2)

            unit(k - 1)

        for gather in gathers:
            gather.begin(DEPTH - 1)
        begin_last(gathers, False)

        @pl.loop(0, model // 256)
        def _(j):
            at = tile(j, 256)
            in_part[at] = matmul_tn(rows[:, at], pg[...]).astype(BF16)

        @pl.loop(0, 3)
        def _(j):
            at = tile(j, model // 3)
            out_part[:, at] = matmul_tn(gated[...], bgs[:, at]).astype(BF16)

        begin_last(gathers, True)

        def ffn_grads():
            for copy in ffn_parts:
                copy.wait()

            @pl.loop(0, model // 256)
            def _(j):
                at = tile(j, 256)
                for i in range(2):
                    half_sum = ffn_in[0, at, i * hs : (i + 1) * hs].astype(F32)
                    for r in range(1, reps):
                        half_sum = half_sum + ffn_in[r, at, i * hs : (i + 1) * hs].astype(F32)
                    ffn_in_sum[i, at] = half_sum
                down_sum = ffn_down[0, :, at].astype(F32)
                for r in range(1, reps):
                    down_sum = down_sum + ffn_down[r, :, at].astype(F32)
                ffn_down_sum[:, at] = down_sum

            for copy in ffn_totals:
                copy.start()

        def owned(t, u):
            return tile(t * share + u, held)

        def seen(f):
            start = jnp.minimum(lax.div(f * held, 128) * 128, model - window)
            return pl.ds(pl.multiple_of(start, 128), window)

        small_send, small_recv = net.take(n), net.take(n)
        lines[...] = jnp.zeros_like(lines)
        lines[0:1] = sums_ref[0:1]
        lines[1 : 1 + HEADS] = forget_sum[:HEADS]
        for i in range(3):
            lines[4 + i : 5 + i] = jnp.broadcast_to(jnp.sum(sums_ref[1 + i : 2 + i], axis=1, keepdims=True), (1, model))
        lines[7:8] = jnp.broadcast_to(jnp.sum(valid_ref[...].astype(F32), axis=1, keepdims=True), (1, model))
        lines[8 : 8 + HEADS] = jnp.broadcast_to(jnp.sum(bias_sum[:HEADS], axis=1, keepdims=True), (HEADS, model))
        small_got[net.f] = lines[:, seen(net.f)]
        for k in range(1, n):
            net.send(
                lines.at[:, seen(others[k])], small_got.at[net.f], small_send + k, small_recv + net.f, others[k]
            )

        in_send, in_recv = net.take(share * TP), net.take(share * TP)
        out_send, out_recv = net.take(share), net.take(share)
        over, landed = net.take(TP), net.take(TP)
        away, back_in = net.take(TP * reps), net.take(TP * reps)
        out_away, out_back = net.take(reps), net.take(reps)
        first_send, first_recv = net.take(n), net.take(n)
        mid_send, mid_recv = net.take(reps), net.take(reps)
        swap_send, swap_recv = net.take(TP * reps), net.take(TP * reps)
        for k, u in partners:
            slot, f = share - 1 - k, net.t * share + u
            for j in range(TP):
                t = chips[(j + 1) % TP]
                net.send(
                    in_part.at[owned(t, u)], in_got.at[slot, t], in_send + share * j + k, in_recv + share * t + slot, f
                )
            net.send(out_part.at[tile(u, held)], out_got.at[slot], out_send + k, out_recv + slot, f)

        replicas = [lax.rem(net.r + k, reps) for k in range(reps)]

        def owned_bit(t, r):
            start = (t * share + net.u) * held + (r * bit if cut > 1 else 0)
            return pl.ds(pl.multiple_of(start, bit), bit)

        def piece(r, t):
            return in_all.at[0, t, tile(r, bit)] if cut > 1 else in_all.at[r, t]

        def steps(start, stop):
            @pl.loop(start, stop)
            def _(j):
                for gather in gathers:
                    gather.step(step_order(j))

        steps(0, 1)
        for j in range(TP):
            t = chips[(j + 1) % TP]
            total = in_part[owned(t, net.u)].astype(F32)
            for slot in range(share - 1):
                net.arrive(in_got.at[slot, t], in_recv + share * t + slot)
                total = total + in_got[slot, t].astype(F32)
            in_part[owned(t, net.u)] = total.astype(BF16)
            if cut > 1:
                for k in range(1, reps):
                    net.send(
                        in_part.at[owned_bit(t, replicas[k])], swapped_in.at[net.r, t], swap_send + TP * k + j,
                        swap_recv + TP * net.r + t, net.f, r=replicas[k],
                    )
        total = out_part[tile(net.u, held)].astype(F32)
        for slot in range(share - 1):
            net.arrive(out_got.at[slot], out_recv + slot)
            total = total + out_got[slot].astype(F32)
        out_all[net.r] = total.astype(BF16)
        steps(1, 2)
        for j in range(TP):
            t = chips[(j + 1) % TP]
            here = owned_bit(t, net.r)
            if cut > 1:
                total = in_part[here].astype(F32)
                for k in range(1, reps):
                    net.arrive(swapped_in.at[replicas[k], t], swap_recv + TP * replicas[k] + t)
                    total = total + swapped_in[replicas[k], t].astype(F32)
                in_part[here] = total.astype(BF16)
            if j < TP - 1:
                net.send(in_part.at[here], piece(net.r, net.t), over + j, landed + net.t, net.place(t))
            else:
                piece(net.r, net.t)[...] = in_part[here]
        for k in range(1, reps):
            net.send(
                out_all.at[net.r], out_all.at[net.r], out_away + k, out_back + net.r, net.f, r=replicas[k]
            )
            net.send(
                piece(net.r, net.t), piece(net.r, net.t), away + k, back_in + TP * net.r + net.t, net.f, r=replicas[k]
            )
        ffn_grads()
        steps(2, DEPTH)

        layer_in = x_ref[...].astype(F32)
        scale = lax.rsqrt(jnp.mean(layer_in * layer_in, axis=-1, keepdims=True) + EPSILON)
        lifted = rows_sum[...] * gains_ref[0:1]
        mean = jnp.mean(layer_in * lifted, axis=-1, keepdims=True)
        input_ref[...] = grad_ref[...] + scale * lifted - layer_in * (scale * scale * scale) * mean
        late[...] = jnp.broadcast_to(
            jnp.sum(rows_sum[...] * layer_in * scale, axis=0, keepdims=True), (8, model)
        )
        first_got[net.f] = late[:, seen(net.f)]
        for k in range(1, n):
            net.send(
                late.at[:, seen(others[k])], first_got.at[net.f], first_send + k, first_recv + net.f, others[k]
            )
        for j in range(1, TP):
            t = chips[TP - j]
            net.arrive(piece(net.r, t), landed + t)
            for k in range(1, reps):
                net.send(
                    piece(net.r, t), piece(net.r, t), away + reps * j + k, back_in + TP * net.r + t, net.f, r=replicas[k]
                )
        for k in range(1, n):
            net.arrive(small_got.at[others[k]], small_recv + others[k])
        for t in range(TP):
            total = small_got[t * share]
            for u in range(1, share):
                total = total + small_got[t * share + u]
            small_mid[net.r, t, :ROWS] = total
        for k in range(1, n):
            net.arrive(first_got.at[others[k]], first_recv + others[k])
        for t in range(TP):
            total = first_got[t * share]
            for u in range(1, share):
                total = total + first_got[t * share + u]
            small_mid[net.r, t, ROWS:] = total
        for k in range(1, reps):
            net.send(
                small_mid.at[net.r], small_mid.at[net.r], mid_send + k, mid_recv + net.r, net.f, r=replicas[k]
            )
        for k in range(1, reps):
            r = replicas[k]
            net.arrive(out_all.at[r], out_back + r)
            for t in range(TP):
                net.arrive(piece(r, t), back_in + TP * r + t)
        for t in range(TP):
            for block in range(4):
                for column, wide, to in head_pieces(t, block):
                    total = in_all[0, t, :, to : to + wide].astype(F32)
                    for r in range(1, sheets):
                        total = total + in_all[r, t, :, to : to + wide].astype(F32)
                    in_ref[:, column : column + wide] = total
        for r in replicas[1:]:
            net.arrive(small_mid.at[r], mid_recv + r)
        total, small = out_all[0].astype(F32), small_mid[0]
        for r in range(1, reps):
            total = total + out_all[r].astype(F32)
            small = small + small_mid[r]
        out_ref[...] = total
        together = jnp.sum(small, axis=0)
        turn = lax.rem(2 * window - (net.f * held - jnp.minimum(lax.div(net.f * held, 128) * 128, model - window)), window)
        gain_rows = pltpu.roll(together, turn, 1)
        gains_out[0:1] = gain_rows[ROWS : ROWS + 1, :held]
        gains_out[1:2] = gain_rows[0:1, :held]
        mean_squares = together[4:7, :128] / (together[7:8, :128] * model)
        roots = jnp.sqrt(mean_squares + EPSILON)
        forget = jnp.zeros((128, 128), F32)
        biases = jnp.zeros((1, 128), F32)
        lane = lax.broadcasted_iota(jnp.int32, (1, 128), 1)
        for t in range(TP):
            turned = pltpu.roll(small[t], turn, 1)[:, :128]
            for h in range(HEADS):
                row = HEADS * t + h
                forget = jnp.where(
                    lax.broadcasted_iota(jnp.int32, (128, 128), 0) == row, turned[1 + h : 2 + h], forget
                )
                biases = jnp.where(lane == row, small[t, 8 + h : 9 + h, :128], biases)
        forget_ref[...] = forget[:H, :held]
        bias_ref[...] = biases[:, :H]
        stats_ref[...] = jnp.where(lane == 0, roots[0:1], jnp.where(lane == 1, roots[1:2], roots[2:3]))[:, :3]
        net.drain()
        for wave in waves:
            wave.drain()
        for gather in gathers:
            gather.drain()
        for copy in ffn_totals:
            copy.wait()

    shape = jax.ShapeDtypeStruct
    line = pltpu.VMEM((DEPTH * seq, model), BF16)
    return call(
        body, "attention_back", 5,
        (x, middle_grad, sums, valid, rows_a, proj, sig, att, prob, logit, wc, wo, wf, gains, ffn_in, ffn_down),
        [VMEM] * 4 + [ANY] * 5 + [VMEM, ANY, ANY, VMEM, VMEM, ANY, ANY],
        [
            (shape((seq, model), F32), VMEM),
            (shape((held, 4 * model), F32), VMEM),
            (shape((held, model), F32), VMEM),
            (shape((2, held), F32), VMEM),
            (shape((H, held), F32), VMEM),
            (shape((1, H), F32), VMEM),
            (shape((1, 3), F32), VMEM),
            (shape((2, model, hs), F32), ANY),
            (shape((hs, model), F32), ANY),
        ],
        [
            pltpu.VMEM((rows_all, model), BF16),
            pltpu.VMEM((rows_all, width), BF16),
            pltpu.VMEM((rows_all, 4 * HD), F32),
            pltpu.VMEM((rows_all, 4 * HD), F32),
            pltpu.VMEM((TP * HEADS, seq, seq), F32),
            pltpu.VMEM((model, width), BF16),
            pltpu.VMEM((4 * HD, model), BF16),
            pltpu.VMEM((rows_all, model), BF16),
            pltpu.VMEM((rows_all, width), BF16),
            pltpu.VMEM((rows_all, 4 * HD), BF16),
            pltpu.VMEM((rows_all, model), BF16),
            line, line, line,
            pltpu.VMEM((seq, model), F32),
            pltpu.VMEM((pair, 4 * HD), BF16),
            pltpu.VMEM((pair, 2 * HD), F32),
            pltpu.VMEM((2, ROWS, seq), BF16),
            pltpu.VMEM((ROWS, seq), F32),
            pltpu.VMEM((ROWS, model), F32),
            pltpu.VMEM((ROWS, model), F32),
            pltpu.VMEM((8, model), F32),
            pltpu.VMEM((model, width), BF16),
            pltpu.VMEM((share - 1, TP, held, width), BF16),
            pltpu.VMEM((reps, TP, bit, width) if cut > 1 else (1, 1, 16, 128), BF16),
            pltpu.VMEM((sheets, TP, held, width), BF16),
            pltpu.VMEM((4 * HD, model), BF16),
            pltpu.VMEM((share - 1, held, model), BF16),
            pltpu.VMEM((reps, held, model), BF16),
            pltpu.VMEM((n, ROWS, window), F32),
            pltpu.VMEM((n, 8, window), F32),
            pltpu.VMEM((reps, TP, ROWS + 8, window), F32),
            pltpu.VMEM((reps, model, 2 * hs), BF16),
            pltpu.VMEM((reps, hs, model), BF16),
            pltpu.VMEM((2, model, hs), F32),
            pltpu.VMEM((hs, model), F32),
            pltpu.SemaphoreType.DMA((11,)),
        ],
        20 * PIECES + 24 * PIECES + 2 * share * (TP + 1) + 2 * TP + 2 * reps * (2 * TP + 2) + 4 * n,
    )


def log_sigmoid(values_in):
    return jnp.minimum(values_in, 0.0) - jnp.log1p(jnp.exp(-jnp.abs(values_in)))


def per_device(
    reps,
    share,
    tokens,
    cotangent,
    pic_start,
    valid_mask,
    gain_attn,
    attn_in,
    forget_w,
    forget_bias,
    attn_out,
    gain_ffn,
    ffn_in,
    ffn_down,
):
    branch_attn, cot, rows_a, proj, sig, att, probability, logit, w_cols, w_rows, w_forget, gains = attention(
        reps, share, tokens[0], cotangent[0], attn_in, attn_out, forget_w.T, gain_attn[None], gain_ffn[None],
        valid_mask, pic_start, forget_bias[None],
    )
    activations, middle_grad, sums, ffn_in_sum, ffn_down_sum = feed_forward(
        reps, share, tokens[0], branch_attn, gains, valid_mask, cot, ffn_in, ffn_down
    )
    (
        input_grad, grad_in, grad_out, grad_gains, grad_forget, bias_total, stats, grad_ffn_in, grad_ffn_down,
    ) = attention_back(
        reps, share, tokens[0], middle_grad, sums, valid_mask, rows_a, proj, sig, att, probability, logit, w_cols, w_rows,
        w_forget, gains, ffn_in_sum, ffn_down_sum,
    )

    return (
        activations[None],
        input_grad[None],
        grad_gains[0],
        grad_in,
        grad_forget.T,
        bias_total[0],
        grad_out,
        grad_gains[1],
        grad_ffn_in,
        grad_ffn_down,
        stats[0],
    )


def solution(mesh):
    placed = (
        P(("rep", "fsdp"), None, None),
        P(("rep", "fsdp"), None, None),
        P(("rep", "fsdp")),
        P(("rep", "fsdp"), None),
        P("fsdp"),
        P("fsdp", None),
        P("fsdp", None),
        P(),
        P("fsdp", None),
        P("fsdp"),
        P(None, None, "fsdp"),
        P("fsdp", None),
    )
    return jax.shard_map(
        functools.partial(per_device, mesh.shape["rep"], mesh.shape["fsdp"] // TP),
        mesh=mesh,
        in_specs=placed,
        out_specs=(
            P(("rep", "fsdp"), None, None),
            P(("rep", "fsdp"), None, None),
            P("fsdp"),
            P("fsdp", None),
            P("fsdp", None),
            P(),
            P("fsdp", None),
            P("fsdp"),
            P(None, None, "fsdp"),
            P("fsdp", None),
            P(),
        ),
        check_vma=False,
    )
```

```python
import functools

import jax
import jax.numpy as jnp
from jax import lax
from jax.experimental import pallas as pl
from jax.experimental.pallas import tpu as pltpu
from jax.sharding import PartitionSpec as P

H = 24
HD = 64
PIC = 32
TP = 8
DEPTH = 4
EPSILON = 1e-06
NEGATIVE = -1e30
MESH = pl.DeviceIdType.MESH
BF16 = jnp.bfloat16
F32 = jnp.float32
VMEM = pl.BlockSpec(memory_space=pltpu.VMEM)
ANY = pl.BlockSpec(memory_space=pl.ANY)


class Net:
    def __init__(self, reps, share, sems):
        self.reps, self.share, self.sems = reps, share, sems
        self.r = lax.axis_index("rep")
        self.f = lax.axis_index("fsdp")
        self.t = lax.div(self.f, share)
        self.u = lax.rem(self.f, share)
        self.z = lax.div(self.t, 2)
        self.x = lax.rem(self.t, 2)
        self.none = self.f * 0
        self.taken = 0
        self.sent = []

    def take(self, count=1):
        base = self.taken
        self.taken += count
        return base

    def place(self, t):
        return t * self.share + self.u

    def grid(self, z, x):
        return (z * 2 + x) * self.share + self.u

    def pair(self):
        return self.z + 1 - 2 * lax.rem(self.z, 2)

    def partners(self):
        for k in range(1, self.share):
            yield k, lax.rem(self.u + k, self.share)

    def greet(self, peers):
        barrier = pltpu.get_barrier_semaphore()
        total = 0
        for cond, r, f in peers:
            if cond is None:
                pl.semaphore_signal(barrier, 1, device_id=(r, f), device_id_type=MESH)
                total = total + 1
            else:

                @pl.when(cond)
                def _():
                    pl.semaphore_signal(barrier, 1, device_id=(r, f), device_id_type=MESH)

                total = total + cond.astype(jnp.int32)
        pl.semaphore_wait(barrier, total)

    def plane_peers(self):
        return [
            (self.z < DEPTH - 1, self.r, self.grid(self.z + 1, self.x)),
            (self.z > 0, self.r, self.grid(self.z - 1, self.x)),
            (None, self.r, self.grid(self.z, 1 - self.x)),
        ]

    def share_peers(self):
        return [(None, self.r, self.t * self.share + u) for _, u in self.partners()]

    def rep_peers(self):
        return [(None, lax.rem(self.r + k, self.reps), self.f) for k in range(1, self.reps)]

    def all_plane_peers(self):
        return [(None, self.r, self.place(lax.rem(self.t + k, TP))) for k in range(1, TP)]

    def copy(self, src, dst, ssem, rsem, f, r=None):
        return pltpu.make_async_remote_copy(
            src_ref=src,
            dst_ref=dst,
            send_sem=self.sems.at[ssem],
            recv_sem=self.sems.at[rsem],
            device_id=(self.r if r is None else r, f),
            device_id_type=MESH,
        )

    def send(self, src, dst, ssem, rsem, f, r=None, cond=None):
        copy = self.copy(src, dst, ssem, rsem, f, r)
        if cond is None:
            copy.start()
        else:
            pl.when(cond)(copy.start)
        self.sent.append((cond, copy))

    def arrive(self, dst, rsem, cond=None):
        copy = pltpu.make_async_remote_copy(
            src_ref=dst,
            dst_ref=dst,
            send_sem=self.sems.at[rsem],
            recv_sem=self.sems.at[rsem],
            device_id=(self.r, self.f),
            device_id_type=MESH,
        )
        if cond is None:
            copy.wait_recv()
        else:
            pl.when(cond)(copy.wait_recv)

    def drain(self):
        for cond, copy in self.sent:
            if cond is None:
                copy.wait_send()
            else:
                pl.when(cond)(copy.wait_send)
        self.sent = []


def nearest(z, k):
    swapped = (1, 0, 2, 3)[k] if isinstance(k, int) else None
    far = lax.div(z, 2)
    edge = z + far * (3 - 2 * z)
    if swapped is None:
        inner = jnp.where(k == 0, 1, jnp.where(k == 1, 0, k))
        place = jnp.where(edge == 0, k, inner)
    else:
        place = k + edge * (swapped - k)
    return far * 3 + (1 - 2 * far) * place


class Wave:
    def __init__(self, net, block, bent=False):
        self.net, self.block, self.bent = net, block, bent
        self.recv = net.take(TP)
        self.up, self.down, self.side = net.take(DEPTH), net.take(DEPTH), net.take(DEPTH)

    def copies(self, k):
        net = self.net
        z, x = net.z, net.x
        zo = nearest(z, k)
        t = zo * 2 + x
        block, sem = self.block(t), self.recv + t
        return [
            (
                (zo <= z) & (z < DEPTH - 1),
                net.copy(block, block, self.up + k, sem, net.grid(jnp.minimum(z + 1, DEPTH - 1), x)),
            ),
            (
                (zo >= z) & (z > 0),
                net.copy(block, block, self.down + k, sem, net.grid(jnp.maximum(z - 1, 0), x)),
            ),
            (None, net.copy(block, block, self.side + k, sem, net.grid(z, 1 - x))),
        ]

    def turn(self):
        if self.bent:
            net = self.net
            t = net.z * 2 + 1 - net.x
            block, sem = self.block(t), self.recv + t
            net.arrive(block, sem)
            net.copy(block, block, self.side + 1, sem, net.grid(net.pair(), net.x)).start()

    def hand_on(self, k, own=False):
        net = self.net
        t = nearest(net.z, k) * 2 + net.x
        if not own:
            net.arrive(self.block(t), self.recv + t, None if isinstance(k, int) else k > 0)
        up, down, side = self.copies(k)
        for cond, copy in (up, down):
            pl.when(cond)(copy.start)
        if self.bent:
            pl.when(net.none + k != 1)(side[1].start)
        else:
            side[1].start()

    def across(self, k):
        t = nearest(self.net.z, k) * 2 + 1 - self.net.x
        self.net.arrive(self.block(t), self.recv + t, self.net.none + k > 0 if self.bent else None)

    def drain(self):
        @pl.loop(0, DEPTH)
        def _(k):
            for cond, copy in self.copies(k):
                if cond is None:
                    copy.wait_send()
                else:
                    pl.when(cond)(copy.wait_send)


class Gather:
    def __init__(self, net, part, side, up, down, total, bent=False):
        self.net, self.part, self.side, self.up, self.down, self.total = net, part, side, up, down, total
        self.bent = bent
        self.sems = [net.take(DEPTH) for _ in range(6)]

    def across(self, k):
        net = self.net
        zo = nearest(net.z, k)
        return net.copy(
            self.part(zo * 2 + 1 - net.x), self.side(zo), self.sems[0] + zo, self.sems[1] + zo,
            net.grid(net.z, 1 - net.x),
        )

    def along(self, k):
        net = self.net
        z = net.z
        zo = nearest(z, k)
        part = self.part(zo * 2 + net.x)
        return [
            (
                zo > z,
                net.copy(
                    part, self.up(zo), self.sems[2] + zo, self.sems[3] + zo,
                    net.grid(jnp.minimum(z + 1, DEPTH - 1), net.x),
                ),
            ),
            (
                zo < z,
                net.copy(
                    part, self.down(zo), self.sems[4] + zo, self.sems[5] + zo,
                    net.grid(jnp.maximum(z - 1, 0), net.x),
                ),
            ),
        ]

    def begin(self, k):
        net = self.net
        z, pair = net.z, net.pair()
        if self.bent and k == 1:
            net.copy(
                self.part(pair * 2 + 1 - net.x), self.side(z), self.sems[0] + pair, self.sems[1] + z,
                net.grid(pair, net.x),
            ).start()
            return
        if self.bent and k == 0:
            net.arrive(self.side(pair), self.sems[1] + pair)
            part = self.part(z * 2 + 1 - net.x)
            part[...] = (part[...].astype(F32) + self.side(pair)[...].astype(F32)).astype(BF16)
        self.across(k).start()

    def step(self, k):
        net = self.net
        z = net.z
        zo = nearest(z, k)
        part = self.part(zo * 2 + net.x)
        if self.bent:
            self.total[...] = part[...].astype(F32)

            @pl.when(k != 1)
            def _():
                net.arrive(self.side(zo), self.sems[1] + zo)
                self.total[...] += self.side(zo)[...].astype(F32)
        else:
            net.arrive(self.side(zo), self.sems[1] + zo)
            self.total[...] = part[...].astype(F32) + self.side(zo)[...].astype(F32)
        for cond, ref, sem in (
            ((zo >= z) & (z > 0), self.up(zo), self.sems[3]),
            ((zo <= z) & (z < DEPTH - 1), self.down(zo), self.sems[5]),
        ):

            @pl.when(cond)
            def _():
                net.arrive(ref, sem + zo)
                self.total[...] += ref[...].astype(F32)

        @pl.when(zo != z)
        def _():
            part[...] = self.total[...].astype(BF16)

        for cond, copy in self.along(k):
            pl.when(cond)(copy.start)

    def drain(self):
        @pl.loop(0, DEPTH)
        def _(k):
            self.across(k).wait_send()
            for cond, copy in self.along(k):
                pl.when(cond)(copy.wait_send)


def column(row):
    size = row.shape[1]
    square = (size, size)
    same = lax.broadcasted_iota(jnp.int32, square, 0) == lax.broadcasted_iota(jnp.int32, square, 1)
    return jnp.sum(jnp.where(same, row, 0.0), axis=1, keepdims=True)


def step_order(j):
    return DEPTH - 1 - j + jnp.where(j == 1, 1, 0) - jnp.where(j == 0, 1, 0)


def begin_last(gathers, bent):
    for gather in gathers:
        if gather.bent == bent:
            gather.begin(0)


def call(body, name, number, operands, in_specs, outs, scratch, sems, limit=60 << 20):
    return pl.pallas_call(
        body,
        name=name,
        out_shape=tuple(shape for shape, _ in outs),
        in_specs=in_specs,
        out_specs=tuple(spec for _, spec in outs),
        scratch_shapes=list(scratch) + [pltpu.SemaphoreType.DMA((sems,))],
        compiler_params=pltpu.CompilerParams(
            collective_id=number, has_side_effects=True, vmem_limit_bytes=limit
        ),
    )(*operands)


def chunk(rows, count, c):
    return pl.ds(c * (rows // count), rows // count)


def matmul_nt(a, b):
    return lax.dot_general(a, b, (((1,), (1,)), ((), ())), preferred_element_type=F32)


def matmul_tn(a, b):
    return lax.dot_general(a, b, (((0,), (0,)), ((), ())), preferred_element_type=F32)


def matmul(a, b):
    return jnp.dot(a, b, preferred_element_type=F32)


def tile(j, size):
    return pl.ds(pl.multiple_of(j * size, size), size)


PIECES = 2


def feed_forward(reps, share, x, branch, gain, valid, cot, w_in, w_down):
    seq, model = x.shape
    hs = w_in.shape[2]
    hidden_all = share * hs
    rows_all = TP * seq
    pair = 2 * seq
    half = seq // PIECES

    def body(
        x_ref, branch_ref, gain_ref, valid_ref, cot_ref, in_ref, down_ref,
        act_ref, grad_ref, sums_ref, in_out, down_out,
        middle, rows, cot_all, w_all, wd, hid, grads, part, side, up, down, rows_sum, ffn_sum,
        in_part, down_part, in_got, down_got, local, sems,
    ):
        net = Net(reps, share, sems)
        own = [
            pltpu.make_async_copy(in_ref.at[0], w_all.at[:, pl.ds(0, hs)], local.at[0]),
            pltpu.make_async_copy(in_ref.at[1], w_all.at[:, pl.ds(hs, hs)], local.at[1]),
            pltpu.make_async_copy(down_ref, wd.at[pl.ds(0, hs)], local.at[2]),
            pltpu.make_async_copy(cot_ref, cot_all, local.at[3]),
        ]
        for copy in own:
            copy.start()

        def block(ref, t):
            return ref.at[tile(t, seq)]

        middle[...] = x_ref[...].astype(F32) + branch_ref[...]
        scale = lax.rsqrt(jnp.mean(middle[...] * middle[...], axis=-1, keepdims=True) + EPSILON)
        block(rows, net.t)[...] = (middle[...] * scale * gain_ref[1:2]).astype(BF16)
        net.greet(net.plane_peers() + net.share_peers() + net.rep_peers())

        waves = [
            Wave(net, lambda t, c=c: rows.at[pl.ds(pl.multiple_of(t * seq + c * half, half), half)])
            for c in range(PIECES)
        ]
        weights = net.take(3 * share), net.take(3 * share)
        for wave in waves:
            wave.hand_on(0, own=True)
        arriving = []
        for k, u in net.partners():
            f, p = net.t * share + u, share - k
            for j, (src, dst) in enumerate(
                [
                    (in_ref.at[0], w_all.at[:, pl.ds(2 * hs * p, hs)]),
                    (in_ref.at[1], w_all.at[:, pl.ds(2 * hs * p + hs, hs)]),
                    (down_ref, wd.at[pl.ds(hs * p, hs)]),
                ]
            ):
                net.send(src, dst, weights[0] + 3 * k + j, weights[1] + 3 * p + j, f)
                arriving.append((dst, weights[1] + 3 * p + j))

        def unit(k):
            at = tile(nearest(net.z, k), pair)
            projected = matmul(rows[at], w_all[...])
            hidden_grad = matmul_nt(cot_all[at], wd[...])
            for p in range(share):
                gate = projected[:, 2 * hs * p : 2 * hs * p + hs]
                lift = projected[:, 2 * hs * p + hs : 2 * hs * (p + 1)]
                back = hidden_grad[:, hs * p : hs * (p + 1)]
                sig = jax.nn.sigmoid(gate)
                silu = gate * sig
                hid[at, hs * p : hs * (p + 1)] = (silu * lift).astype(BF16)
                grads[at, 2 * hs * p : 2 * hs * p + hs] = (
                    back * lift * sig * (1.0 + gate * (1.0 - sig))
                ).astype(BF16)
                grads[at, 2 * hs * p + hs : 2 * hs * (p + 1)] = (back * silu).astype(BF16)

            @pl.loop(0, 3)
            def _(j):
                to = tile(j, model // 3)
                part[0, at, to] = matmul_nt(grads[at], w_all[to]).astype(BF16)
                part[1, at, to] = matmul(hid[at], wd[:, to]).astype(BF16)

        def piece(ref, i, c, count):
            return lambda j: ref.at[i, pl.ds(pl.multiple_of(j * seq + c * half, half), half)]

        gathers = [
            [
                Gather(
                    net, piece(part, i, c, TP), piece(side, i, c, DEPTH), piece(up, i, c, DEPTH),
                    piece(down, i, c, DEPTH), total.at[pl.ds(c * half, half)],
                )
                for c in range(PIECES)
            ]
            for i, total in enumerate((rows_sum, ffn_sum))
        ]
        @pl.loop(1, DEPTH + 1)
        def _(k):
            @pl.when(k < DEPTH)
            def _():
                for wave in waves:
                    wave.hand_on(k)

            @pl.when(k == 1)
            def _():
                for wave in waves:
                    wave.turn()
                for copy in own:
                    copy.wait()
                for dst, sem in arriving:
                    net.arrive(dst, sem)

            for wave in waves:
                wave.across(k - 1)

            @pl.when(k == DEPTH)
            def _():
                for gather in gathers[0]:
                    gather.begin(DEPTH - 2)

            unit(k - 1)

        for k in (DEPTH - 1, *range(DEPTH - 3, 0, -1)):
            for gather in gathers[0]:
                gather.begin(k)
        begin_last(gathers[0], False)

        @pl.loop(0, model // 256)
        def _(j):
            at = tile(j, 256)
            in_part[at] = matmul_tn(rows[:, at], grads[...]).astype(BF16)

        begin_last(gathers[0], True)
        for k in range(DEPTH - 1, 0, -1):
            for gather in gathers[1]:
                gather.begin(k)
        begin_last(gathers[1], False)

        @pl.loop(0, 3)
        def _(j):
            at = tile(j, model // 3)
            down_part[:, at] = matmul_tn(hid[...], cot_all[:, at]).astype(BF16)

        first, arrived = net.take(2 * share), net.take(2 * share)
        away, back = net.take(2 * reps), net.take(2 * reps)
        for k, u in net.partners():
            f, slot = net.t * share + u, share - 1 - k
            net.send(
                in_part.at[:, pl.ds(2 * hs * k, 2 * hs)], in_got.at[slot], first + 2 * k, arrived + 2 * slot, f
            )
            net.send(
                down_part.at[pl.ds(hs * k, hs)], down_got.at[slot], first + 2 * k + 1, arrived + 2 * slot + 1, f
            )

        def own_grads():
            for slot in range(share - 1):
                net.arrive(in_got.at[slot], arrived + 2 * slot)
                net.arrive(down_got.at[slot], arrived + 2 * slot + 1)

            @pl.loop(0, model // 256)
            def _(j):
                at = tile(j, 256)
                total = in_part[at, : 2 * hs].astype(F32)
                for slot in range(share - 1):
                    total = total + in_got[slot, at].astype(F32)
                in_out[net.r, at] = total.astype(BF16)

            total = down_part[:hs].astype(F32)
            for slot in range(share - 1):
                total = total + down_got[slot].astype(F32)
            down_out[net.r] = total.astype(BF16)
            for k in range(1, reps):
                r = lax.rem(net.r + k, reps)
                net.send(in_out.at[net.r], in_out.at[net.r], away + 2 * k, back + 2 * net.r, net.f, r=r)
                net.send(down_out.at[net.r], down_out.at[net.r], away + 2 * k + 1, back + 2 * net.r + 1, net.f, r=r)

        def steps(both, start, stop):
            @pl.loop(start, stop)
            def _(j):
                for gather in both:
                    gather.step(DEPTH - 1 - j)

        steps(gathers[0], 0, 2)
        begin_last(gathers[1], True)
        own_grads()
        steps(gathers[0], 2, DEPTH)
        steps(gathers[1], 0, DEPTH)

        result = middle[...] + ffn_sum[...]
        act_ref[...] = result.astype(BF16)
        valid_col = column(valid_ref[...].astype(F32))
        scale = lax.rsqrt(jnp.mean(middle[...] * middle[...], axis=-1, keepdims=True) + EPSILON)
        lifted = rows_sum[...] * gain_ref[1:2]
        mean = jnp.mean(middle[...] * lifted, axis=-1, keepdims=True)
        grad_ref[...] = (
            block(cot_all, net.t)[...].astype(F32) + scale * lifted - middle[...] * (scale * scale * scale) * mean
        )
        sums_ref[...] = jnp.zeros_like(sums_ref)
        sums_ref[0:1] = jnp.sum(rows_sum[...] * middle[...] * scale, axis=0, keepdims=True)
        sums_ref[1:2] = jnp.sum(result * result * valid_col, axis=0, keepdims=True)
        sums_ref[2:3] = jnp.sum(branch_ref[...] * branch_ref[...] * valid_col, axis=0, keepdims=True)
        sums_ref[3:4] = jnp.sum(ffn_sum[...] * ffn_sum[...] * valid_col, axis=0, keepdims=True)
        for k in range(1, reps):
            r = lax.rem(net.r + k, reps)
            net.arrive(in_out.at[r], back + 2 * r)
            net.arrive(down_out.at[r], back + 2 * r + 1)
        net.drain()
        for wave in waves:
            wave.drain()
        for gather in gathers[0] + gathers[1]:
            gather.drain()

    shape = jax.ShapeDtypeStruct
    line = pltpu.VMEM((2, DEPTH * seq, model), BF16)
    return call(
        body, "feed_forward", 3, (x, branch, gain, valid, cot, w_in, w_down), [VMEM] * 4 + [ANY] * 3,
        [
            (shape((seq, model), BF16), VMEM),
            (shape((seq, model), F32), VMEM),
            (shape((8, model), F32), VMEM),
            (shape((reps, model, 2 * hs), BF16), VMEM),
            (shape((reps, hs, model), BF16), VMEM),
        ],
        [
            pltpu.VMEM((seq, model), F32),
            pltpu.VMEM((rows_all, model), BF16),
            pltpu.VMEM((rows_all, model), BF16),
            pltpu.VMEM((model, 2 * hidden_all), BF16),
            pltpu.VMEM((hidden_all, model), BF16),
            pltpu.VMEM((rows_all, hidden_all), BF16),
            pltpu.VMEM((rows_all, 2 * hidden_all), BF16),
            pltpu.VMEM((2, rows_all, model), BF16),
            line, line, line,
            pltpu.VMEM((seq, model), F32),
            pltpu.VMEM((seq, model), F32),
            pltpu.VMEM((model, 2 * hidden_all), BF16),
            pltpu.VMEM((hidden_all, model), BF16),
            pltpu.VMEM((share - 1, model, 2 * hs), BF16),
            pltpu.VMEM((share - 1, hs, model), BF16),
            pltpu.SemaphoreType.DMA((4,)),
        ],
        40 * PIECES + 24 * 2 * PIECES + 20 * share + 10 * reps,
    )


HEADS = H // TP
ROWS = 16


def cuts(reps, held):
    return reps if held % (16 * reps) == 0 else 1


def lane_mask(shape, low, high):
    lane = lax.broadcasted_iota(jnp.int32, shape, 1)
    return (lane >= low) & (lane < high)


def head_pieces(t, block):
    base = block * H * HD + t * HEADS * HD
    return [(base, 2 * HD, block * 2 * HD), (base + 2 * HD, HD, 8 * HD + block * HD)]


def attention(reps, share, x, cot, w_in, w_out, forget, gain_a, gain_f, mask, start, bias):
    n = TP * share
    seq, model = x.shape
    held = w_in.shape[0]
    width = 4 * HEADS * HD
    rows_all = TP * seq
    pair = 2 * seq
    half = seq // PIECES
    last = HEADS - 1
    cut = cuts(reps, held)

    def body(
        x_ref, cot_ref, in_ref, out_ref, forget_ref, gain_a_ref, gain_f_ref, mask_ref, start_ref, bias_ref,
        branch_ref, cot_out, rows_out, proj_out, sig_out, att_out, prob_out, logit_ref, wc_out, wo_out, wf_ref, gains_ref,
        xs, cots, rows, proj, sig, att, prob, wc, wo, split, smalls, lines, part, side, up, down, gated, local, sems,
    ):
        net = Net(reps, share, sems)

        def seq_block(ref, t):
            return ref.at[tile(t, seq)]

        def held_rows(f):
            return wc.at[tile(f, held)]

        def spot(r):
            return r if cut > 1 else 0

        def piece_of(r):
            return tile(spot(r), held // cut)

        def held_piece(f, r):
            return wc.at[pl.ds(pl.multiple_of(f * held + spot(r) * (held // cut), held // cut), held // cut)]

        own = [
            pltpu.make_async_copy(x_ref, seq_block(xs, net.t), local.at[0]),
            pltpu.make_async_copy(cot_ref, seq_block(cots, net.t), local.at[1]),
            pltpu.make_async_copy(out_ref, wo.at[tile(net.u, held)], local.at[3]),
        ]
        for copy in own:
            copy.start()
        small = lines.at[:, pl.ds(0, 128)]
        small[...] = jnp.zeros((32, 128), F32)
        small[:H, :held] = forget_ref[...].astype(F32)
        small[H : H + 1, :held] = gain_a_ref[...].astype(F32)
        small[H + 1 : H + 2, :held] = gain_f_ref[...].astype(F32)
        small[H + 2 : H + 3, :seq] = mask_ref[...].astype(F32)
        small[H + 3 : H + 4, :seq] = jnp.full((1, seq), start_ref[0], jnp.int32).astype(F32)
        smalls[net.f] = small[...].astype(BF16)
        for t in range(TP):
            for block in range(4):
                for column, wide, to in head_pieces(t, block):
                    split[t, :, to : to + wide] = in_ref[:, column : column + wide]
        wo[share * held :] = jnp.zeros((wo.shape[0] - share * held, model), BF16)
        others = [lax.rem(net.f + k, n) for k in range(n)]
        chips = [lax.rem(net.t + k, TP) for k in range(TP)]
        partners = list(net.partners())
        replicas = [lax.rem(net.r + k, reps) for k in range(reps)]
        net.greet([(None, net.r, f) for f in others[1:]] + [(None, r, net.f) for r in replicas[1:cut]])

        small_send, small_recv = net.take(n), net.take(n)
        w_send, w_recv = net.take(TP), net.take(n * cut)
        w_pass = net.take(share * TP * (cut + 1))
        w_away = net.take(TP * cut)
        wo_send, wo_recv = net.take(share), net.take(share)
        for k in range(1, n):
            net.send(smalls.at[net.f], smalls.at[net.f], small_send + k, small_recv + net.f, others[k])
        for k in range(1, TP):
            net.send(
                split.at[chips[k], piece_of(net.r)], held_piece(net.f, net.r), w_send + k, w_recv + cut * net.f + spot(net.r),
                net.place(chips[k]),
            )
        own_cols = pltpu.make_async_copy(split.at[net.t], held_rows(net.f), local.at[4])
        own_cols.start()
        for k, u in partners:
            f = net.t * share + u
            net.send(split.at[net.t], held_rows(net.f), w_pass + k, w_recv + cut * net.f, f)
            net.send(out_ref, wo.at[tile(net.u, held)], wo_send + k, wo_recv + net.u, f)

        def pieces(ref):
            return [
                Wave(net, lambda t, c=c: ref.at[pl.ds(pl.multiple_of(t * seq + c * half, half), half)])
                for c in range(PIECES)
            ]

        waves, cot_waves = pieces(xs), pieces(cots)
        for copy in own:
            copy.wait()
        for wave in waves:
            wave.hand_on(0, own=True)
        for wave in cot_waves:
            wave.copies(0)[2][1].start()

        def weights():
            for q in range(cut):
                r = replicas[q]
                for k in range(1, TP):
                    source = net.place(chips[k])
                    got, sem = held_piece(source, r), w_recv + cut * source + spot(r)
                    net.arrive(got, sem)
                    for j, u in partners:
                        net.send(got, got, w_pass + share * (TP * (q + 1) + k) + j, sem, net.t * share + u)
                    for p in range(1, cut if q == 0 else 1):
                        net.send(got, got, w_away + TP * p + k, sem, net.f, r=replicas[p])
                if q == 0:
                    for wave in waves:
                        wave.hand_on(2)
            for k in range(1, n):
                net.arrive(smalls.at[others[k]], small_recv + others[k])
            for j in range(model // 128):
                line = jnp.zeros((32, 128), F32)
                for f in range(j * 128 // held, ((j + 1) * 128 - 1) // held + 1):
                    start = f * held - j * 128
                    piece = pltpu.roll(smalls[f].astype(F32), net.none + start % 128, 1)
                    line = jnp.where(lane_mask((32, 128), start, start + held), piece, line)
                lines[:, j * 128 : (j + 1) * 128] = line
            pick = lax.broadcasted_iota(jnp.int32, (ROWS, 32), 0) + HEADS * net.t
            pick = pick == lax.broadcasted_iota(jnp.int32, (ROWS, 32), 1)
            pick &= lax.broadcasted_iota(jnp.int32, (ROWS, 32), 0) < HEADS
            wf_ref[...] = matmul(pick.astype(BF16), lines[...].astype(BF16)).astype(BF16)
            gains_ref[...] = lines[H : H + 8]
            for k, u in partners:
                net.arrive(wo.at[tile(u, held)], wo_recv + u)
                net.arrive(held_rows(net.t * share + u), w_recv + cut * (net.t * share + u))
                for k in range(1, TP):
                    f = chips[k] * share + u
                    for r in replicas[:cut]:
                        net.arrive(held_piece(f, r), w_recv + cut * f + spot(r))
            own_cols.wait()

        own_head = lax.broadcasted_iota(jnp.int32, (ROWS, H), 0)
        picked = own_head + HEADS * net.t == lax.broadcasted_iota(jnp.int32, (ROWS, H), 1)
        bias_col = jnp.sum(
            jnp.where(picked & (own_head < HEADS), bias_ref[...].astype(F32), 0.0), axis=1, keepdims=True
        )
        few = (ROWS, ROWS)
        same = lax.broadcasted_iota(jnp.int32, few, 0) == lax.broadcasted_iota(jnp.int32, few, 1)
        bias_row = jnp.sum(jnp.where(same, bias_col, 0.0), axis=0, keepdims=True)
        square = (seq, seq)
        at_row = lax.broadcasted_iota(jnp.int32, square, 0)
        at_col = lax.broadcasted_iota(jnp.int32, square, 1)

        def unit(k):
            place = nearest(net.z, k)
            at = tile(place, pair)
            values_in = xs[at].astype(F32)
            inverse = lax.rsqrt(jnp.mean(values_in * values_in, axis=-1, keepdims=True) + EPSILON)
            rows[at] = (values_in * inverse * gains_ref[0:1]).astype(BF16)
            projected = matmul(rows[at], wc[...])
            proj[at] = projected.astype(BF16)
            sig[at, : 2 * HD] = jax.nn.sigmoid(projected[:, 6 * HD : 8 * HD])
            tail = pltpu.roll(jax.nn.sigmoid(projected[:, 10 * HD : 12 * HD]), net.none + HD, 1)
            sig[at, 2 * HD :] = jnp.where(lane_mask(tail.shape, 0, HD), tail, 0.0)

            @pl.loop(0, 2, unroll=True)
            def _(j):
                t = place * 2 + j
                here = tile(t, seq)
                marks = smalls[net.place(t)].astype(F32)
                valid = marks[H + 2 : H + 3]
                start = marks[H + 3 : H + 4].astype(jnp.int32)
                causal = at_col <= at_row
                inside = (at_row >= start) & (at_row < start + PIC) & (at_col >= start) & (at_col < start + PIC)
                allowed = (causal | inside) & (valid > 0.0)
                sign = jnp.where(causal, 1.0, -1.0)
                below = sign * 0.5 + 0.5
                logit_col = matmul_nt(rows[here], wf_ref[...]) + bias_row
                logit_row = matmul_nt(wf_ref[...], rows[here]) + bias_col
                logit_ref[t] = logit_row
                decay_col = jnp.dot(
                    below, log_sigmoid(logit_col), precision=lax.Precision.HIGHEST, preferred_element_type=F32
                )
                decay_row = lax.dot_general(
                    log_sigmoid(logit_row), below, (((1,), (1,)), ((), ())),
                    precision=lax.Precision.HIGHEST, preferred_element_type=F32,
                )
                outs = []
                for h in range(HEADS):
                    if h < last:
                        query = jnp.where(lane_mask((seq, 2 * HD), h * HD, h * HD + HD), proj[here, : 2 * HD], 0)
                        key, value = proj[here, 2 * HD : 4 * HD], proj[here, 4 * HD : 6 * HD]
                    else:
                        query = jnp.where(lane_mask((seq, 2 * HD), 0, HD), proj[here, 8 * HD : 10 * HD], 0)
                        key = pltpu.roll(proj[here, 8 * HD : 10 * HD].astype(F32), net.none + HD, 1).astype(BF16)
                        value = proj[here, 10 * HD :]
                    scores = matmul_nt(query, key) * HD ** (-0.5)
                    scores = scores + sign * (decay_col[:, h : h + 1] - decay_row[h : h + 1])
                    masked = jnp.where(allowed, scores, NEGATIVE)
                    weights_now = jnp.exp(masked - jnp.max(masked, axis=-1, keepdims=True))
                    probability = weights_now / jnp.sum(weights_now, axis=-1, keepdims=True)
                    prob[t * HEADS + h] = probability
                    outs.append(matmul(probability.astype(BF16), value))
                low = lane_mask((seq, 2 * HD), 0, HD)
                att[here, : 2 * HD] = jnp.where(low, outs[0], outs[1])
                att[here, 2 * HD :] = jnp.where(low, outs[2], 0.0)

            gated[...] = (att[at] * sig[at]).astype(BF16)

            @pl.loop(0, 3)
            def _(j):
                to = tile(j, model // 3)
                part[at, to] = matmul(gated[...], wo[:, to]).astype(BF16)

        gathers = [
            Gather(
                net,
                *[
                    lambda j, ref=ref, c=c: ref.at[pl.ds(pl.multiple_of(j * seq + c * half, half), half)]
                    for ref in (part, side, up, down)
                ],
                branch_ref.at[pl.ds(c * half, half)],
            )
            for c in range(PIECES)
        ]

        for wave in waves:
            wave.hand_on(1)
            wave.turn()
        weights()

        @pl.loop(1, DEPTH + 1)
        def _(k):
            @pl.when(k == 2)
            def _():
                for wave in waves:
                    wave.hand_on(DEPTH - 1)
                for wave in cot_waves:
                    for cond, copy in wave.copies(0)[:2]:
                        pl.when(cond)(copy.start)
                    wave.turn()

            @pl.when(k == 3)
            def _():
                for wave in cot_waves:
                    wave.hand_on(1)

            for wave in waves:
                wave.across(k - 1)

            @pl.when(k == DEPTH - 1)
            def _():
                for gather in gathers:
                    gather.begin(1)

            @pl.when(k == DEPTH)
            def _():
                for gather in gathers:
                    gather.begin(DEPTH - 2)
                for wave in cot_waves:
                    wave.hand_on(2)

            unit(k - 1)

        keep = [
            pltpu.make_async_copy(src, dst, local.at[5 + i])
            for i, (src, dst) in enumerate(
                [
                    (rows, rows_out), (proj, proj_out), (sig, sig_out), (att, att_out), (prob, prob_out),
                    (wc, wc_out), (wo, wo_out),
                ]
            )
        ]
        for gather in gathers:
            gather.begin(DEPTH - 1)
        begin_last(gathers, False)

        for copy in keep:
            copy.start()

        @pl.loop(0, DEPTH)
        def _(j):
            for gather in gathers:
                gather.step(step_order(j))

            @pl.when(j == 0)
            def _():
                begin_last(gathers, True)

            @pl.when(j == 0)
            def _():
                for wave in cot_waves:
                    wave.hand_on(DEPTH - 1)

        for k in range(DEPTH):
            for wave in cot_waves:
                wave.across(k)
        save = pltpu.make_async_copy(cots, cot_out, local.at[1])
        save.start()
        net.drain()
        for wave in waves + cot_waves:
            wave.drain()
        for gather in gathers:
            gather.drain()
        for copy in keep:
            copy.wait()
        save.wait()

    shape = jax.ShapeDtypeStruct
    line = pltpu.VMEM((DEPTH * seq, model), BF16)
    kept = [
        ((rows_all, model), BF16),
        ((rows_all, model), BF16),
        ((rows_all, width), BF16),
        ((rows_all, 4 * HD), F32),
        ((rows_all, 4 * HD), F32),
        ((TP * HEADS, seq, seq), F32),
    ]
    return call(
        body, "attention", 1, (x, cot, w_in, w_out, forget, gain_a, gain_f, mask, start, bias),
        [ANY, ANY, VMEM, ANY, VMEM, VMEM, VMEM, VMEM, pl.BlockSpec(memory_space=pltpu.SMEM), VMEM],
        [(shape((seq, model), F32), VMEM)]
        + [(shape(*what), ANY) for what in kept]
        + [
            (shape((TP, ROWS, seq), F32), VMEM),
            (shape((model, width), BF16), ANY),
            (shape((4 * HD, model), BF16), ANY),
            (shape((ROWS, model), BF16), VMEM),
            (shape((8, model), F32), VMEM),
        ],
        [pltpu.VMEM((rows_all, model), BF16)]
        + [pltpu.VMEM(*what) for what in kept]
        + [
            pltpu.VMEM((model, width), BF16),
            pltpu.VMEM((4 * HD, model), BF16),
            pltpu.VMEM((TP, held, width), BF16),
            pltpu.VMEM((n, 32, 128), BF16),
            pltpu.VMEM((32, model), F32),
            pltpu.VMEM((rows_all, model), BF16),
            line, line, line,
            pltpu.VMEM((pair, 4 * HD), BF16),
            pltpu.SemaphoreType.DMA((12,)),
        ],
        2 * 20 * PIECES + 24 * PIECES + (2 + cut) * n + (1 + cut) * (TP + share * TP) + 2 * share,
    )


def attention_back(
    reps, share, x, middle_grad, sums, valid, rows_a, proj, sig, att, prob, logit, wc, wo, wf, gains,
    ffn_in, ffn_down,
):
    n = TP * share
    seq, model = x.shape
    width = 4 * HEADS * HD
    held = model // n
    rows_all = TP * seq
    pair = 2 * seq
    half = seq // PIECES
    last = HEADS - 1
    window = 256
    cut = cuts(reps, held)
    bit = held // cut
    sheets = 1 if cut > 1 else reps
    hs = ffn_down.shape[1]

    def body(
        x_ref, grad_ref, sums_ref, valid_ref, rows_in, proj_in, sig_in, att_in, prob_in, logit_ref, wc_in, wo_in, wf_ref,
        gains_ref, ffn_in_ref, ffn_down_ref,
        input_ref, in_ref, out_ref, gains_out, forget_ref, bias_ref, stats_ref, ffn_in_out, ffn_down_out,
        rows, proj, sig, att, prob, wcs, wos, bgs, pg, gated, part, side, up, down, rows_sum, ag, og, low_logit, bias_sum,
        forget_sum, lines, late, in_part, in_got, swapped_in, in_all, out_part, out_got, out_all, small_got, first_got,
        small_mid, ffn_in, ffn_down, ffn_in_sum, ffn_down_sum, local, sems,
    ):
        net = Net(reps, share, sems)
        others = [lax.rem(net.f + k, n) for k in range(n)]
        chips = [lax.rem(net.t + k, TP) for k in range(TP)]
        partners = list(net.partners())
        own = [
            pltpu.make_async_copy(src, dst, local.at[i])
            for i, (src, dst) in enumerate(
                [
                    (wo_in, wos), (sig_in, sig), (att_in, att), (proj_in, proj), (prob_in, prob), (rows_in, rows),
                    (wc_in, wcs),
                ]
            )
        ]
        ffn_parts = [
            pltpu.make_async_copy(ffn_in_ref, ffn_in, local.at[7]),
            pltpu.make_async_copy(ffn_down_ref, ffn_down, local.at[8]),
        ]
        ffn_totals = [
            pltpu.make_async_copy(ffn_in_sum, ffn_in_out, local.at[9]),
            pltpu.make_async_copy(ffn_down_sum, ffn_down_out, local.at[10]),
        ]
        for copy in own + ffn_parts:
            copy.start()
        bgs[tile(net.t, seq)] = grad_ref[...].astype(BF16)
        net.greet([(None, net.r, f) for f in others[1:]] + net.rep_peers())
        waves = [
            Wave(net, lambda t, c=c: bgs.at[pl.ds(pl.multiple_of(t * seq + c * half, half), half)], c == 1)
            for c in range(PIECES)
        ]
        for wave in waves:
            wave.hand_on(0, own=True)
        bias_sum[...] = jnp.zeros_like(bias_sum)
        forget_sum[...] = jnp.zeros_like(forget_sum)
        for copy in own:
            copy.wait()

        square = (seq, seq)
        causal = lax.broadcasted_iota(jnp.int32, square, 1) <= lax.broadcasted_iota(jnp.int32, square, 0)
        below = jnp.where(causal, 1.0, 0.0)
        low = lane_mask((seq, 2 * HD), 0, HD)
        head_row = lax.broadcasted_iota(jnp.int32, (ROWS, seq), 0)

        def unit(k):
            place = nearest(net.z, k)
            at = tile(place, pair)
            gated_grad = matmul_nt(bgs[at], wos[...])
            gate, attended = sig[at], att[at]
            ag[...] = (gated_grad * gate).astype(BF16)
            gated[at] = (attended * gate).astype(BF16)
            gate_grad = gated_grad * attended * (gate * (1.0 - gate))
            pg[at, 6 * HD : 8 * HD] = gate_grad[:, : 2 * HD].astype(BF16)
            og[...] = pltpu.roll(gate_grad[:, 2 * HD :], net.none + HD, 1)

            @pl.loop(0, 2, unroll=True)
            def _(j):
                t = place * 2 + j
                here = tile(t, seq)
                inner = tile(j, seq)
                swapped = pltpu.roll(proj[here, 8 * HD : 10 * HD].astype(F32), net.none + HD, 1).astype(BF16)
                decay_grad = jnp.zeros((ROWS, seq), F32)
                found = []
                for h in range(HEADS):
                    probability = prob[t * HEADS + h]
                    if h < last:
                        back_all = ag[inner, : 2 * HD]
                        back = jnp.where(lane_mask((seq, 2 * HD), h * HD, h * HD + HD), back_all, 0)
                        query, key, value = (proj[here, 2 * HD * i : 2 * HD * (i + 1)] for i in range(3))
                    else:
                        back = back_all = ag[inner, 2 * HD :]
                        query, key, value = swapped, swapped, proj[here, 10 * HD :]
                    prob_grad = matmul_nt(back, value)
                    score_grad = probability * (
                        prob_grad - jnp.sum(probability * prob_grad, axis=-1, keepdims=True)
                    )
                    dotted_grad = (score_grad * HD ** (-0.5)).astype(BF16)
                    found.append(
                        (
                            matmul(dotted_grad, key),
                            matmul_tn(dotted_grad, query),
                            matmul_tn(probability.astype(BF16), back_all),
                        )
                    )
                    signed = jnp.where(causal, score_grad, -score_grad)
                    line = jnp.sum(signed.T - signed, axis=0, keepdims=True)
                    decay_grad = jnp.where(head_row == h, line, decay_grad)
                for i in range(3):
                    pg[here, 2 * HD * i : 2 * HD * (i + 1)] = jnp.where(low, found[0][i], found[1][i]).astype(BF16)
                pg[here, 8 * HD : 10 * HD] = jnp.where(low, found[2][0], found[2][1]).astype(BF16)
                pg[here, 10 * HD :] = jnp.where(low, found[2][2], og[inner]).astype(BF16)
                later = jnp.dot(decay_grad, below, precision=lax.Precision.HIGHEST, preferred_element_type=F32)
                logit_grad = later * jax.nn.sigmoid(-logit_ref[t])
                bias_sum[...] += logit_grad
                low_logit[j] = logit_grad.astype(BF16)
                forget_sum[...] += matmul(logit_grad.astype(BF16), rows[here])

            @pl.loop(0, 3)
            def _(i):
                to = tile(i, model // 3)
                main = matmul_nt(pg[at], wcs[to])
                for j in range(2):
                    extra = matmul_tn(low_logit[j], wf_ref[:, to])
                    part[tile(place * 2 + j, seq), to] = (main[j * seq : (j + 1) * seq] + extra).astype(BF16)

        gathers = [
            Gather(
                net,
                *[
                    lambda j, ref=ref, c=c: ref.at[pl.ds(pl.multiple_of(j * seq + c * half, half), half)]
                    for ref in (part, side, up, down)
                ],
                rows_sum.at[pl.ds(c * half, half)], c == 1,
            )
            for c in range(PIECES)
        ]

        @pl.loop(1, DEPTH + 1)
        def _(k):
            @pl.when(k < DEPTH)
            def _():
                for wave in waves:
                    wave.hand_on(k)

            @pl.when(k == 1)
            def _():
                for wave in waves:
                    wave.turn()

            for wave in waves:
                wave.across(k - 1)

            @pl.when(k == DEPTH)
            def _():
                for gather in gathers:
                    gather.begin(DEPTH - 2)

            unit(k - 1)

        for k in (DEPTH - 1, *range(DEPTH - 3, 0, -1)):
            for gather in gathers:
                gather.begin(k)
        begin_last(gathers, False)

        @pl.loop(0, model // 256)
        def _(j):
            at = tile(j, 256)
            in_part[at] = matmul_tn(rows[:, at], pg[...]).astype(BF16)

        @pl.loop(0, 3)
        def _(j):
            at = tile(j, model // 3)
            out_part[:, at] = matmul_tn(gated[...], bgs[:, at]).astype(BF16)

        begin_last(gathers, True)

        def ffn_grads():
            for copy in ffn_parts:
                copy.wait()

            @pl.loop(0, model // 256)
            def _(j):
                at = tile(j, 256)
                for i in range(2):
                    half_sum = ffn_in[0, at, i * hs : (i + 1) * hs].astype(F32)
                    for r in range(1, reps):
                        half_sum = half_sum + ffn_in[r, at, i * hs : (i + 1) * hs].astype(F32)
                    ffn_in_sum[i, at] = half_sum
                down_sum = ffn_down[0, :, at].astype(F32)
                for r in range(1, reps):
                    down_sum = down_sum + ffn_down[r, :, at].astype(F32)
                ffn_down_sum[:, at] = down_sum

            for copy in ffn_totals:
                copy.start()

        def owned(t, u):
            return tile(t * share + u, held)

        def seen(f):
            start = jnp.minimum(lax.div(f * held, 128) * 128, model - window)
            return pl.ds(pl.multiple_of(start, 128), window)

        small_send, small_recv = net.take(n), net.take(n)
        lines[...] = jnp.zeros_like(lines)
        lines[0:1] = sums_ref[0:1]
        lines[1 : 1 + HEADS] = forget_sum[:HEADS]
        for i in range(3):
            lines[4 + i : 5 + i] = jnp.broadcast_to(jnp.sum(sums_ref[1 + i : 2 + i], axis=1, keepdims=True), (1, model))
        lines[7:8] = jnp.broadcast_to(jnp.sum(valid_ref[...].astype(F32), axis=1, keepdims=True), (1, model))
        lines[8 : 8 + HEADS] = jnp.broadcast_to(jnp.sum(bias_sum[:HEADS], axis=1, keepdims=True), (HEADS, model))
        small_got[net.f] = lines[:, seen(net.f)]
        for k in range(1, n):
            net.send(
                lines.at[:, seen(others[k])], small_got.at[net.f], small_send + k, small_recv + net.f, others[k]
            )

        in_send, in_recv = net.take(share * TP), net.take(share * TP)
        out_send, out_recv = net.take(share), net.take(share)
        over, landed = net.take(TP), net.take(TP)
        away, back_in = net.take(TP * reps), net.take(TP * reps)
        out_away, out_back = net.take(reps), net.take(reps)
        first_send, first_recv = net.take(n), net.take(n)
        mid_send, mid_recv = net.take(reps), net.take(reps)
        swap_send, swap_recv = net.take(TP * reps), net.take(TP * reps)
        for k, u in partners:
            slot, f = share - 1 - k, net.t * share + u
            for j in range(TP):
                t = chips[(j + 1) % TP]
                net.send(
                    in_part.at[owned(t, u)], in_got.at[slot, t], in_send + share * j + k, in_recv + share * t + slot, f
                )
            net.send(out_part.at[tile(u, held)], out_got.at[slot], out_send + k, out_recv + slot, f)

        replicas = [lax.rem(net.r + k, reps) for k in range(reps)]

        def owned_bit(t, r):
            start = (t * share + net.u) * held + (r * bit if cut > 1 else 0)
            return pl.ds(pl.multiple_of(start, bit), bit)

        def piece(r, t):
            return in_all.at[0, t, tile(r, bit)] if cut > 1 else in_all.at[r, t]

        def steps(start, stop):
            @pl.loop(start, stop)
            def _(j):
                for gather in gathers:
                    gather.step(DEPTH - 1 - j)

        steps(0, 1)
        for j in range(TP):
            t = chips[(j + 1) % TP]
            total = in_part[owned(t, net.u)].astype(F32)
            for slot in range(share - 1):
                net.arrive(in_got.at[slot, t], in_recv + share * t + slot)
                total = total + in_got[slot, t].astype(F32)
            in_part[owned(t, net.u)] = total.astype(BF16)
            if cut > 1:
                for k in range(1, reps):
                    net.send(
                        in_part.at[owned_bit(t, replicas[k])], swapped_in.at[net.r, t], swap_send + TP * k + j,
                        swap_recv + TP * net.r + t, net.f, r=replicas[k],
                    )
        total = out_part[tile(net.u, held)].astype(F32)
        for slot in range(share - 1):
            net.arrive(out_got.at[slot], out_recv + slot)
            total = total + out_got[slot].astype(F32)
        out_all[net.r] = total.astype(BF16)
        steps(1, 2)
        for j in range(TP):
            t = chips[(j + 1) % TP]
            here = owned_bit(t, net.r)
            if cut > 1:
                total = in_part[here].astype(F32)
                for k in range(1, reps):
                    net.arrive(swapped_in.at[replicas[k], t], swap_recv + TP * replicas[k] + t)
                    total = total + swapped_in[replicas[k], t].astype(F32)
                in_part[here] = total.astype(BF16)
            if j < TP - 1:
                net.send(in_part.at[here], piece(net.r, net.t), over + j, landed + net.t, net.place(t))
            else:
                piece(net.r, net.t)[...] = in_part[here]
        for k in range(1, reps):
            net.send(
                out_all.at[net.r], out_all.at[net.r], out_away + k, out_back + net.r, net.f, r=replicas[k]
            )
            net.send(
                piece(net.r, net.t), piece(net.r, net.t), away + k, back_in + TP * net.r + net.t, net.f, r=replicas[k]
            )
        ffn_grads()
        steps(2, DEPTH)

        layer_in = x_ref[...].astype(F32)
        scale = lax.rsqrt(jnp.mean(layer_in * layer_in, axis=-1, keepdims=True) + EPSILON)
        lifted = rows_sum[...] * gains_ref[0:1]
        mean = jnp.mean(layer_in * lifted, axis=-1, keepdims=True)
        input_ref[...] = grad_ref[...] + scale * lifted - layer_in * (scale * scale * scale) * mean
        late[...] = jnp.broadcast_to(
            jnp.sum(rows_sum[...] * layer_in * scale, axis=0, keepdims=True), (8, model)
        )
        first_got[net.f] = late[:, seen(net.f)]
        for k in range(1, n):
            net.send(
                late.at[:, seen(others[k])], first_got.at[net.f], first_send + k, first_recv + net.f, others[k]
            )
        for j in range(1, TP):
            t = chips[TP - j]
            net.arrive(piece(net.r, t), landed + t)
            for k in range(1, reps):
                net.send(
                    piece(net.r, t), piece(net.r, t), away + reps * j + k, back_in + TP * net.r + t, net.f, r=replicas[k]
                )
        for k in range(1, n):
            net.arrive(small_got.at[others[k]], small_recv + others[k])
        for t in range(TP):
            total = small_got[t * share]
            for u in range(1, share):
                total = total + small_got[t * share + u]
            small_mid[net.r, t, :ROWS] = total
        for k in range(1, n):
            net.arrive(first_got.at[others[k]], first_recv + others[k])
        for t in range(TP):
            total = first_got[t * share]
            for u in range(1, share):
                total = total + first_got[t * share + u]
            small_mid[net.r, t, ROWS:] = total
        for k in range(1, reps):
            net.send(
                small_mid.at[net.r], small_mid.at[net.r], mid_send + k, mid_recv + net.r, net.f, r=replicas[k]
            )
        for k in range(1, reps):
            r = replicas[k]
            net.arrive(out_all.at[r], out_back + r)
            for t in range(TP):
                net.arrive(piece(r, t), back_in + TP * r + t)
        for t in range(TP):
            for block in range(4):
                for column, wide, to in head_pieces(t, block):
                    total = in_all[0, t, :, to : to + wide].astype(F32)
                    for r in range(1, sheets):
                        total = total + in_all[r, t, :, to : to + wide].astype(F32)
                    in_ref[:, column : column + wide] = total
        for r in replicas[1:]:
            net.arrive(small_mid.at[r], mid_recv + r)
        total, small = out_all[0].astype(F32), small_mid[0]
        for r in range(1, reps):
            total = total + out_all[r].astype(F32)
            small = small + small_mid[r]
        out_ref[...] = total
        together = jnp.sum(small, axis=0)
        turn = lax.rem(2 * window - (net.f * held - jnp.minimum(lax.div(net.f * held, 128) * 128, model - window)), window)
        gain_rows = pltpu.roll(together, turn, 1)
        gains_out[0:1] = gain_rows[ROWS : ROWS + 1, :held]
        gains_out[1:2] = gain_rows[0:1, :held]
        mean_squares = together[4:7, :128] / (together[7:8, :128] * model)
        roots = jnp.sqrt(mean_squares + EPSILON)
        forget = jnp.zeros((128, 128), F32)
        biases = jnp.zeros((1, 128), F32)
        lane = lax.broadcasted_iota(jnp.int32, (1, 128), 1)
        for t in range(TP):
            turned = pltpu.roll(small[t], turn, 1)[:, :128]
            for h in range(HEADS):
                row = HEADS * t + h
                forget = jnp.where(
                    lax.broadcasted_iota(jnp.int32, (128, 128), 0) == row, turned[1 + h : 2 + h], forget
                )
                biases = jnp.where(lane == row, small[t, 8 + h : 9 + h, :128], biases)
        forget_ref[...] = forget[:H, :held]
        bias_ref[...] = biases[:, :H]
        stats_ref[...] = jnp.where(lane == 0, roots[0:1], jnp.where(lane == 1, roots[1:2], roots[2:3]))[:, :3]
        net.drain()
        for wave in waves:
            wave.drain()
        for gather in gathers:
            gather.drain()
        for copy in ffn_totals:
            copy.wait()

    shape = jax.ShapeDtypeStruct
    line = pltpu.VMEM((DEPTH * seq, model), BF16)
    return call(
        body, "attention_back", 5,
        (x, middle_grad, sums, valid, rows_a, proj, sig, att, prob, logit, wc, wo, wf, gains, ffn_in, ffn_down),
        [VMEM] * 4 + [ANY] * 5 + [VMEM, ANY, ANY, VMEM, VMEM, ANY, ANY],
        [
            (shape((seq, model), F32), VMEM),
            (shape((held, 4 * model), F32), VMEM),
            (shape((held, model), F32), VMEM),
            (shape((2, held), F32), VMEM),
            (shape((H, held), F32), VMEM),
            (shape((1, H), F32), VMEM),
            (shape((1, 3), F32), VMEM),
            (shape((2, model, hs), F32), ANY),
            (shape((hs, model), F32), ANY),
        ],
        [
            pltpu.VMEM((rows_all, model), BF16),
            pltpu.VMEM((rows_all, width), BF16),
            pltpu.VMEM((rows_all, 4 * HD), F32),
            pltpu.VMEM((rows_all, 4 * HD), F32),
            pltpu.VMEM((TP * HEADS, seq, seq), F32),
            pltpu.VMEM((model, width), BF16),
            pltpu.VMEM((4 * HD, model), BF16),
            pltpu.VMEM((rows_all, model), BF16),
            pltpu.VMEM((rows_all, width), BF16),
            pltpu.VMEM((rows_all, 4 * HD), BF16),
            pltpu.VMEM((rows_all, model), BF16),
            line, line, line,
            pltpu.VMEM((seq, model), F32),
            pltpu.VMEM((pair, 4 * HD), BF16),
            pltpu.VMEM((pair, 2 * HD), F32),
            pltpu.VMEM((2, ROWS, seq), BF16),
            pltpu.VMEM((ROWS, seq), F32),
            pltpu.VMEM((ROWS, model), F32),
            pltpu.VMEM((ROWS, model), F32),
            pltpu.VMEM((8, model), F32),
            pltpu.VMEM((model, width), BF16),
            pltpu.VMEM((share - 1, TP, held, width), BF16),
            pltpu.VMEM((reps, TP, bit, width) if cut > 1 else (1, 1, 16, 128), BF16),
            pltpu.VMEM((sheets, TP, held, width), BF16),
            pltpu.VMEM((4 * HD, model), BF16),
            pltpu.VMEM((share - 1, held, model), BF16),
            pltpu.VMEM((reps, held, model), BF16),
            pltpu.VMEM((n, ROWS, window), F32),
            pltpu.VMEM((n, 8, window), F32),
            pltpu.VMEM((reps, TP, ROWS + 8, window), F32),
            pltpu.VMEM((reps, model, 2 * hs), BF16),
            pltpu.VMEM((reps, hs, model), BF16),
            pltpu.VMEM((2, model, hs), F32),
            pltpu.VMEM((hs, model), F32),
            pltpu.SemaphoreType.DMA((11,)),
        ],
        20 * PIECES + 24 * PIECES + 2 * share * (TP + 1) + 2 * TP + 2 * reps * (2 * TP + 2) + 4 * n,
    )


def log_sigmoid(values_in):
    return jnp.minimum(values_in, 0.0) - jnp.log1p(jnp.exp(-jnp.abs(values_in)))


def per_device(
    reps,
    share,
    tokens,
    cotangent,
    pic_start,
    valid_mask,
    gain_attn,
    attn_in,
    forget_w,
    forget_bias,
    attn_out,
    gain_ffn,
    ffn_in,
    ffn_down,
):
    branch_attn, cot, rows_a, proj, sig, att, probability, logit, w_cols, w_rows, w_forget, gains = attention(
        reps, share, tokens[0], cotangent[0], attn_in, attn_out, forget_w.T, gain_attn[None], gain_ffn[None],
        valid_mask, pic_start, forget_bias[None],
    )
    activations, middle_grad, sums, ffn_in_sum, ffn_down_sum = feed_forward(
        reps, share, tokens[0], branch_attn, gains, valid_mask, cot, ffn_in, ffn_down
    )
    (
        input_grad, grad_in, grad_out, grad_gains, grad_forget, bias_total, stats, grad_ffn_in, grad_ffn_down,
    ) = attention_back(
        reps, share, tokens[0], middle_grad, sums, valid_mask, rows_a, proj, sig, att, probability, logit, w_cols, w_rows,
        w_forget, gains, ffn_in_sum, ffn_down_sum,
    )

    return (
        activations[None],
        input_grad[None],
        grad_gains[0],
        grad_in,
        grad_forget.T,
        bias_total[0],
        grad_out,
        grad_gains[1],
        grad_ffn_in,
        grad_ffn_down,
        stats[0],
    )


def solution(mesh):
    placed = (
        P(("rep", "fsdp"), None, None),
        P(("rep", "fsdp"), None, None),
        P(("rep", "fsdp")),
        P(("rep", "fsdp"), None),
        P("fsdp"),
        P("fsdp", None),
        P("fsdp", None),
        P(),
        P("fsdp", None),
        P("fsdp"),
        P(None, None, "fsdp"),
        P("fsdp", None),
    )
    return jax.shard_map(
        functools.partial(per_device, mesh.shape["rep"], mesh.shape["fsdp"] // TP),
        mesh=mesh,
        in_specs=placed,
        out_specs=(
            P(("rep", "fsdp"), None, None),
            P(("rep", "fsdp"), None, None),
            P("fsdp"),
            P("fsdp", None),
            P("fsdp", None),
            P(),
            P("fsdp", None),
            P("fsdp"),
            P(None, None, "fsdp"),
            P("fsdp", None),
            P(),
        ),
        check_vma=False,
    )
```
